32 devices in a mesh: dp: 16 (over z, y, core), mp: 2 (over x).
Axes of the slice: x: 2, y: 2, z: 4, core: 2. Of those that a mesh axis runs over, the one named last changes fastest.
Arguments:
- hidden_in: bfloat16 [8192, 2048], P('dp', 'mp'), may hold values from -6 to 6
- doc_starts: int32 [16, 2], replicated, may hold values from 1 to 511, as said below
- attn_gain: bfloat16 [2048], P('dp'), may hold values from 0.25 to 1.75
- w_query: bfloat16 [2048, 2048], P('dp', 'mp'), may hold values from -0.125 to 0.125
- w_key: bfloat16 [2048, 512], P('dp', 'mp'), may hold values from -0.125 to 0.125
- w_value: bfloat16 [2048, 512], P('dp', 'mp'), may hold values from -0.125 to 0.125
- query_gain: bfloat16 [64], replicated, may hold values from 0.25 to 1.75
- key_gain: bfloat16 [64], replicated, may hold values from 0.25 to 1.75
- w_out: bfloat16 [2048, 2048], P('mp', 'dp'), may hold values from -0.5 to 0.5
- mlp_gain: bfloat16 [2048], P('dp'), may hold values from 0.25 to 1.75
- w_gate: bfloat16 [2048, 8192], P('dp', 'mp'), may hold values from -0.125 to 0.125
- w_up: bfloat16 [2048, 8192], P('dp', 'mp'), may hold values from -0.125 to 0.125
- w_down: bfloat16 [8192, 2048], P('mp', 'dp'), may hold values from -0.125 to 0.125
- cotangent: bfloat16 [8192, 2048], P('dp', 'mp'), may hold values from -12 to 12
Outputs:
- block_out: bfloat16 [8192, 2048], P('dp', 'mp')
- d_input: float32 [8192, 2048], P('dp', 'mp')
- d_attn_gain: float32 [2048], P('dp')
- d_query: float32 [2048, 2048], P('dp', 'mp')
- d_key: float32 [2048, 512], P('dp', 'mp')
- d_value: float32 [2048, 512], P('dp', 'mp')
- d_query_gain: float32 [64], replicated
- d_key_gain: float32 [64], replicated
- d_out_proj: float32 [2048, 2048], P('mp', 'dp')
- d_mlp_gain: float32 [2048], P('dp')
- d_gate: float32 [2048, 8192], P('dp', 'mp')
- d_up: float32 [2048, 8192], P('dp', 'mp')
- d_down: float32 [8192, 2048], P('mp', 'dp')
The draws below stay inside these ranges and needn't reach their ends.
Inputs may be any that keep to these rules, and one draw needn't show every extreme that they name: `doc_starts`: in each row the first number is at most the second; documents may be empty.
All inputs are finite; a program needn't handle non-finite values.
Results may differ from the reference program's by a relative error of at most 0.017.
Values may be sent and summed in bfloat16 or wider, within the bound.
A program may use at most 256 MiB of HBM per device.

```python
import math
import jax
import jax.numpy as jnp
from jax import lax

D = 2048
H = 32
KV = 8
HD = 64
FF = 8192
SEQ_LEN = 512
SEQS = 16
TOKENS = 8192


def draw_doc_starts(key, part):
    first = jax.random.randint(jax.random.fold_in(key, 1), (SEQS,), 1, SEQ_LEN)
    second = jax.random.randint(jax.random.fold_in(key, 2), (SEQS,), 1, SEQ_LEN)
    return jnp.stack([jnp.minimum(first, second), jnp.maximum(first, second)], axis=1).astype(jnp.int32)


def draw_cotangent(key, part):
    ramp = 3.0 ** (jnp.arange(TOKENS, dtype=jnp.float32) / TOKENS)
    base = jnp.clip(jax.random.normal(key, (TOKENS, D), jnp.float32), -4.0, 4.0)
    return (base * ramp[:, None]).astype(jnp.bfloat16)


def spiked(values, key, source, target, parts, factor):
    def block_of(axis_at):
        return (jnp.arange(values.shape[axis_at]) // (values.shape[axis_at] // parts)).reshape((-1,) + (1,) * (values.ndim - 1 - axis_at))

    one_side = jax.random.permutation(key, parts)[block_of(target)]
    other_side = (block_of(target) + parts // 2) % parts
    return jnp.where((block_of(source) == one_side) | (block_of(source) == other_side), factor * values, values)


def block_levels(stream_key, dims, split, smallest, top_value):
    def one(dim, parts):
        steps = jax.random.uniform(jax.random.fold_in(jax.random.fold_in(stream_key, 6), dim), (parts,), jnp.float32, smallest / len(split), top_value / len(split))
        return jnp.repeat(jnp.exp(steps), dims[dim] // parts).reshape((-1,) + (1,) * (len(dims) - dim - 1))

    loudness = one(*split[0])
    for cut in split[1:]:
        loudness = loudness * one(*cut)
    return loudness


def scatter_about(key, shape, scale, reach, pieces=(), kind=jnp.bfloat16):
    drawn = jax.random.normal(key, shape, jnp.float32) * scale
    if len(pieces) > 0:
        drawn = block_levels(key, shape, pieces, -0.22, 0.18) * drawn
    return jnp.clip(drawn, min=-reach, max=reach).astype(kind)


def noise_with(key, shape, scale, limit, pieces, heavy, kind=jnp.bfloat16):
    values = scale * jax.random.normal(key, shape, jnp.float32)
    if pieces:
        values = values * block_levels(key, shape, pieces, -0.22, 0.18)
    return jnp.clip(spiked(values, jax.random.fold_in(key, 3), *heavy), -limit, limit).astype(kind)


def setup_inputs(seed: int = 0) -> dict:
    streams_of = jax.random.split(jax.random.key(seed), 15)
    hidden_in = noise_with(streams_of[0], (TOKENS, D), 1.0, 6.0, ((0, 16), (1, 2)), (0, 1, 16, 2.0))
    doc_starts = draw_doc_starts(jax.random.fold_in(streams_of[14], 71), 0)
    attn_gain = jnp.clip(1.0 + 0.15 * jax.random.normal(streams_of[2], (D,), jnp.float32), 0.25, 1.75).astype(jnp.bfloat16)
    w_query = scatter_about(streams_of[3], (D, H * HD), D ** -0.5, 0.125, ((0, 16), (1, 2)))
    w_key = scatter_about(streams_of[4], (D, KV * HD), D ** -0.5, 0.125, ((0, 16), (1, 2)))
    w_value = scatter_about(streams_of[5], (D, KV * HD), D ** -0.5, 0.125, ((0, 16), (1, 2)))
    query_gain = jnp.clip(1.0 + 0.15 * jax.random.normal(streams_of[6], (HD,), jnp.float32), 0.25, 1.75).astype(jnp.bfloat16)
    key_gain = jnp.clip(1.0 + 0.15 * jax.random.normal(streams_of[7], (HD,), jnp.float32), 0.25, 1.75).astype(jnp.bfloat16)
    w_out = scatter_about(streams_of[8], (H * HD, D), (H * HD // 16) ** -0.5, 0.5, ((0, 2), (1, 16)))
    mlp_gain = jnp.clip(1.0 + 0.15 * jax.random.normal(streams_of[9], (D,), jnp.float32), 0.25, 1.75).astype(jnp.bfloat16)
    w_gate = scatter_about(streams_of[10], (D, FF), D ** -0.5, 0.125, ((0, 16), (1, 2)))
    w_up = scatter_about(streams_of[11], (D, FF), D ** -0.5, 0.125, ((0, 16), (1, 2)))
    w_down = scatter_about(streams_of[12], (FF, D), (FF // 4) ** -0.5, 0.125, ((0, 2), (1, 16)))
    cotangent = draw_cotangent(jax.random.fold_in(streams_of[14], 71), 0)
    return dict(hidden_in=hidden_in, doc_starts=doc_starts, attn_gain=attn_gain, w_query=w_query, w_key=w_key, w_value=w_value, query_gain=query_gain, key_gain=key_gain, w_out=w_out, mlp_gain=mlp_gain, w_gate=w_gate, w_up=w_up, w_down=w_down, cotangent=cotangent)


@jax.custom_vjp
def low(v):
    return lax.optimization_barrier(v.astype(jnp.bfloat16)).astype(jnp.float32)

@jax.custom_vjp
def low_back(v):
    return v

def low_keep(v):
    return (low(v), None)

def low_pass(kept, grad):
    return (grad,)

def back_keep(v):
    return (v, None)

def back_low(kept, grad):
    return (low(grad),)
low.defvjp(low_keep, low_pass)
low_back.defvjp(back_keep, back_low)

def rms_rows(v, gain):
    return v * lax.rsqrt(lax.optimization_barrier(jnp.mean(v * v, axis=-1, keepdims=True)) + 1e-05) * gain

def tables(cut_row):
    position = jnp.arange(SEQ_LEN, dtype=jnp.int32)
    doc = (position >= cut_row[0]).astype(jnp.int32) + (position >= cut_row[1]).astype(jnp.int32)
    starts = jnp.where(doc == 0, 0, jnp.where(doc == 1, cut_row[0], cut_row[1])).astype(jnp.int32)
    places = (position - starts).astype(jnp.float32)
    freqs = jnp.exp(-math.log(1000000.0) * 2.0 * jnp.arange(HD // 2, dtype=jnp.float32) / HD)
    angles = places[:, None] * freqs[None, :]
    angles = jnp.concatenate([angles, angles], axis=-1)
    allowed = (doc[:, None] == doc[None, :]) & (position[None, :] <= position[:, None])
    return (jnp.cos(angles)[:, None, :], jnp.sin(angles)[:, None, :], allowed)

def rotate(v, cosine, sine_table):
    halfway = v.shape[-1] // 2
    turned = jnp.concatenate([-v[..., halfway:], v[..., :halfway]], axis=-1)
    return v * cosine + turned * sine_table

def head_piece(pre, gain, cosine, sine_table):
    shaped = pre.reshape(pre.shape[0], pre.shape[1] // gain.shape[0], gain.shape[0])
    return rotate(rms_rows(shaped, gain), cosine, sine_table)

def attend_seq(inputs):
    queries, keys, values, allowed = inputs
    highest = lax.Precision.HIGHEST
    scores = jnp.einsum('qkgd,tkd->kgqt', queries, keys, precision=highest) * HD ** (-0.5)
    scores = low_back(scores)
    scores = jnp.where(allowed[None, None], scores, -1e+30)
    probs = low(jax.nn.softmax(scores, axis=-1))
    outputs = jnp.einsum('kgqt,tkd->qkgd', probs, values, precision=highest)
    return outputs.reshape(queries.shape[0], -1)

def reference(hidden_in, doc_starts, attn_gain, w_query, w_key, w_value, query_gain, key_gain, w_out, mlp_gain, w_gate, w_up, w_down, cotangent):
    cosine, sine_table, allowed = jax.vmap(tables)(doc_starts)
    cosine = cosine.reshape(TOKENS, 1, HD)
    sine_table = sine_table.reshape(TOKENS, 1, HD)
    group = H // KV
    highest = lax.Precision.HIGHEST

    def forward(resid, gain_one, wq_full, wk_full, wv_full, qgain, kgain, wo_full, gain_two, wg_full, wu_full, wd_full):
        normed_one = low(rms_rows(resid, gain_one))
        query_pre = low_back(jnp.dot(normed_one, wq_full, precision=highest))
        key_pre = low_back(jnp.dot(normed_one, wk_full, precision=highest))
        values = low(low_back(jnp.dot(normed_one, wv_full, precision=highest)))
        query_rot = low(head_piece(query_pre, qgain, cosine, sine_table))
        key_rot = low(head_piece(key_pre, kgain, cosine, sine_table))
        attended = lax.map(jax.checkpoint(attend_seq), (query_rot.reshape(SEQS, SEQ_LEN, KV, group, HD), key_rot.reshape(SEQS, SEQ_LEN, KV, HD), values.reshape(SEQS, SEQ_LEN, KV, HD), allowed))
        mixed = low(low_back(attended.reshape(TOKENS, H * HD)))
        middle = resid + low_back(jnp.dot(mixed, wo_full, precision=highest))
        normed_two = low(rms_rows(middle, gain_two))
        gate_pre = low_back(jnp.dot(normed_two, wg_full, precision=highest))
        up_pre = low_back(jnp.dot(normed_two, wu_full, precision=highest))
        inner = low(jax.nn.silu(gate_pre) * up_pre)
        return middle + low_back(jnp.dot(inner, wd_full, precision=highest))
    result, pullback = jax.vjp(forward, hidden_in.astype(jnp.float32), attn_gain.astype(jnp.float32), w_query.astype(jnp.float32), w_key.astype(jnp.float32), w_value.astype(jnp.float32), query_gain.astype(jnp.float32), key_gain.astype(jnp.float32), w_out.astype(jnp.float32), mlp_gain.astype(jnp.float32), w_gate.astype(jnp.float32), w_up.astype(jnp.float32), w_down.astype(jnp.float32))
    grads = pullback(cotangent.astype(jnp.float32))
    return (result.astype(jnp.bfloat16), grads[0], grads[1], grads[2], grads[3], grads[4], grads[5], grads[6], grads[7], grads[8], grads[9], grads[10], grads[11])
```

```python
from functools import partial
import math

import jax
import jax.numpy as jnp
from jax import lax
from jax.sharding import Mesh, PartitionSpec as P

BF = jnp.bfloat16
F32 = jnp.float32
EPS = 1e-05
TP = ("i", "m")
ALL = ("t", "i", "m")


def dot_f32(left, right, dims):
    return lax.dot_general(left, right, (dims, ((), ())), preferred_element_type=F32)


def nn(left, right):
    return dot_f32(left, right, ((1,), (0,)))


def nt(left, right):
    return dot_f32(left, right, ((1,), (1,)))


def tn(left, right):
    return dot_f32(left, right, ((0,), (0,)))


def rms_rows(v, gain):
    return v * lax.rsqrt(jnp.mean(v * v, axis=-1, keepdims=True) + EPS) * gain


def tables(cut_row, length, head_dim):
    position = jnp.arange(length, dtype=jnp.int32)
    doc = (position >= cut_row[0]).astype(jnp.int32) + (position >= cut_row[1]).astype(jnp.int32)
    starts = jnp.where(doc == 0, 0, jnp.where(doc == 1, cut_row[0], cut_row[1]))
    places = (position - starts).astype(F32)
    freqs = jnp.exp(-math.log(1000000.0) * 2.0 * jnp.arange(head_dim // 2, dtype=F32) / head_dim)
    angles = places[:, None] * freqs[None, :]
    angles = jnp.concatenate([angles, angles], axis=-1)
    allowed = (doc[:, None] == doc[None, :]) & (position[None, :] <= position[:, None])
    return jnp.cos(angles), jnp.sin(angles), allowed


def rotate(v, cosine, sine_table):
    halfway = v.shape[-1] // 2
    turned = jnp.concatenate([-v[..., halfway:], v[..., :halfway]], axis=-1)
    return v * cosine + turned * sine_table


def head_piece(pre, gain, cosine, sine_table):
    shaped = pre.reshape(pre.shape[0], -1, gain.shape[0])
    return rotate(rms_rows(shaped, gain), cosine, sine_table)


def attend(inputs, scale):
    queries, keys, values, allowed = inputs
    scores = jnp.einsum("qgd,td->gqt", queries, keys, preferred_element_type=F32) * scale
    scores = jnp.where(allowed[None], scores, -1e30)
    highest = jnp.max(scores, axis=-1, keepdims=True)
    weights_exp = jnp.exp(scores - highest)
    totals = jnp.sum(weights_exp, axis=-1, keepdims=True)
    probs = weights_exp / totals
    log_norm = highest[..., 0] + jnp.log(totals[..., 0])
    outputs = jnp.einsum("gqt,td->qgd", probs.astype(BF), values, preferred_element_type=F32)
    return outputs.astype(BF), log_norm


def attend_grad(inputs, scale):
    queries, keys, values, d_outputs, log_norm, allowed = inputs
    scores = jnp.einsum("qgd,td->gqt", queries, keys, preferred_element_type=F32) * scale
    scores = jnp.where(allowed[None], scores, -1e30)
    probs = jnp.exp(scores - log_norm[..., None])
    d_probs = jnp.einsum("qgd,td->gqt", d_outputs, values, preferred_element_type=F32)
    inner_sum = jnp.sum(probs * d_probs, axis=-1, keepdims=True)
    d_scores = (probs * (d_probs - inner_sum)).astype(BF)
    d_queries = jnp.einsum("gqt,td->qgd", d_scores, keys, preferred_element_type=F32) * scale
    d_keys = jnp.einsum("gqt,qgd->td", d_scores, queries, preferred_element_type=F32) * scale
    d_values = jnp.einsum("gqt,qgd->td", probs.astype(BF), d_outputs, preferred_element_type=F32)
    return d_queries, d_keys, d_values


def gather_pieces(piece, ranks):
    rows, cols = piece.shape
    parts = lax.all_gather(piece, TP, axis=0)
    parts = parts.reshape(ranks[0], ranks[1], rows, cols)
    return jnp.moveaxis(parts, 1, 2).reshape(ranks[0] * rows, ranks[1] * cols)


def scatter_pieces(partial_sum, ranks):
    rows, cols = partial_sum.shape
    parts = partial_sum.astype(BF).reshape(ranks[0], rows // ranks[0], ranks[1], cols // ranks[1])
    parts = jnp.moveaxis(parts, 2, 1).reshape(-1, rows // ranks[0], cols // ranks[1])
    mine = lax.psum_scatter(parts, TP, scatter_dimension=0, tiled=False)
    return mine.astype(F32)


def spread(local, inner):
    rows, cols = local.shape
    parts = jnp.moveaxis(local.reshape(rows, inner, cols // inner), 1, 0)
    parts = lax.all_to_all(parts, "i", 0, 0, tiled=False)
    return parts.reshape(inner * rows, cols // inner)


def collect(block, inner):
    rows, cols = block.shape
    parts = lax.all_to_all(block.reshape(inner, rows // inner, cols), "i", 0, 0, tiled=False)
    return jnp.moveaxis(parts, 0, 1).reshape(rows // inner, inner * cols)


def full_rows(local, inner):
    return lax.all_gather(spread(local, inner), "t", axis=0, tiled=True)


def grad_rows(part, inner):
    mine = lax.psum_scatter(part.astype(BF), "t", scatter_dimension=0, tiled=True)
    return collect(mine, inner).astype(F32)


def body(
    hidden_in, doc_starts, attn_gain, w_query, w_key, w_value, query_gain, key_gain,
    w_out, mlp_gain, w_gate, w_up, w_down, cotangent, *, groups, inner, halves,
):
    length, width_part = hidden_in.shape
    ranks = (inner, halves)
    width = width_part * halves
    head_dim = query_gain.shape[0]
    scale = head_dim ** (-0.5)
    t_index, m_index = lax.axis_index("t"), lax.axis_index("m")
    cuts = lax.dynamic_slice_in_dim(doc_starts, t_index * inner, inner, 0)
    cosine, sine_table, allowed = jax.vmap(partial(tables, length=length, head_dim=head_dim))(cuts)
    cosine = cosine.reshape(inner * length, 1, head_dim)
    sine_table = sine_table.reshape(inner * length, 1, head_dim)
    q_gain, k_gain = query_gain.astype(F32), key_gain.astype(F32)
    gains = lax.all_gather(jnp.stack([attn_gain, mlp_gain], 1), ("t", "i"), axis=0, tiled=True)
    gain_one, gain_two = gains[:, 0].astype(F32), gains[:, 1].astype(F32)

    full_in = gather_pieces(hidden_in, ranks)
    sizes = [w.shape[1] // inner for w in (w_query, w_key, w_value)] + [w_out.shape[0] // inner]
    edges = [sum(sizes[:n]) for n in range(5)]

    def by_rank(w):
        return w.reshape(w.shape[0], inner, w.shape[1] // inner)

    attn_local = jnp.concatenate([by_rank(w_query), by_rank(w_key), by_rank(w_value), by_rank(w_out.T)], 2)
    attn_cols = full_rows(attn_local.reshape(attn_local.shape[0], -1), inner)
    query_cols, key_cols, value_cols, out_t = [attn_cols[:, edges[n]:edges[n + 1]] for n in range(4)]
    resid = full_in.astype(F32)
    r_one = lax.rsqrt(jnp.mean(resid * resid, axis=-1, keepdims=True) + EPS)
    normed_one = (resid * r_one * gain_one).astype(BF)
    gate_cols = full_rows(w_gate, inner)
    up_cols = full_rows(w_up, inner)
    down_t = full_rows(w_down.T, inner)
    grad_full = gather_pieces(cotangent, ranks)

    query_pre = nn(normed_one, query_cols)
    key_pre = nn(normed_one, key_cols)
    value_low = nn(normed_one, value_cols).astype(BF)
    query_rot = head_piece(query_pre, q_gain, cosine, sine_table).astype(BF)
    key_rot = head_piece(key_pre, k_gain, cosine, sine_table).astype(BF)
    group = query_rot.shape[1]
    query_stack = query_rot.reshape(inner, length, group, head_dim)
    key_stack = key_rot.reshape(inner, length, head_dim)
    value_stack = value_low.reshape(inner, length, head_dim)
    attended, log_norm = lax.map(partial(attend, scale=scale), (query_stack, key_stack, value_stack, allowed))
    mixed = attended.reshape(inner * length, group * head_dim)
    middle = hidden_in.astype(F32) + scatter_pieces(nt(mixed, out_t), ranks)
    my_gain_one = lax.dynamic_slice_in_dim(gain_one, m_index * width_part, width_part, 0)
    my_gain_two = lax.dynamic_slice_in_dim(gain_two, m_index * width_part, width_part, 0)
    r_two = lax.rsqrt(lax.psum(jnp.sum(middle * middle, axis=-1, keepdims=True), "m") / width + EPS)
    normed_two = gather_pieces((middle * r_two * my_gain_two).astype(BF), ranks)

    gate_pre, up_pre = nn(normed_two, gate_cols), nn(normed_two, up_cols)
    d_inner = nn(grad_full, down_t)
    sigmoid_gate = jax.nn.sigmoid(gate_pre)
    inner_act = (gate_pre * sigmoid_gate * up_pre).astype(BF)
    d_gate_pre = (d_inner * up_pre * sigmoid_gate * (1.0 + gate_pre * (1.0 - sigmoid_gate))).astype(BF)
    d_up_pre = (d_inner * gate_pre * sigmoid_gate).astype(BF)
    d_normed_two = scatter_pieces(nt(d_gate_pre, gate_cols) + nt(d_up_pre, up_cols), ranks)
    mlp_out = scatter_pieces(nt(inner_act, down_t), ranks)
    block_out = (middle + mlp_out).astype(BF)

    scaled = d_normed_two * my_gain_two
    dot_two = lax.psum(jnp.sum(scaled * middle, axis=-1, keepdims=True), "m") / width
    d_gain_two = jnp.sum(d_normed_two * middle * r_two, axis=0)
    d_middle = cotangent.astype(F32) + r_two * scaled - middle * (r_two * r_two * r_two) * dot_two
    d_middle_low = gather_pieces(d_middle.astype(BF), ranks)
    d_gate = grad_rows(tn(normed_two, d_gate_pre), inner)
    d_up = grad_rows(tn(normed_two, d_up_pre), inner)
    d_down = grad_rows(tn(grad_full, inner_act), inner).T

    d_mixed = nn(d_middle_low, out_t).astype(BF)
    d_out_part = tn(d_middle_low, mixed)
    d_mixed_stack = d_mixed.reshape(inner, length, group, head_dim)
    d_query_stack, d_key_stack, d_value_stack = lax.map(
        partial(attend_grad, scale=scale),
        (query_stack, key_stack, value_stack, d_mixed_stack, log_norm, allowed),
    )
    rotary_piece = partial(head_piece, cosine=cosine, sine_table=sine_table)
    _, query_pull = jax.vjp(rotary_piece, query_pre, q_gain)
    d_query_pre, d_qgain_part = query_pull(d_query_stack.reshape(inner * length, group, head_dim))
    _, key_pull = jax.vjp(rotary_piece, key_pre, k_gain)
    d_key_pre, d_kgain_part = key_pull(d_key_stack.reshape(inner * length, 1, head_dim))
    d_heads = jnp.concatenate(
        [d_query_pre, d_key_pre, d_value_stack.reshape(inner * length, head_dim)], 1
    ).astype(BF)
    heads_cols = attn_cols[:, : edges[3]]
    d_normed_one = scatter_pieces(nt(d_heads, heads_cols), ranks)
    d_attn = jnp.concatenate([tn(normed_one, d_heads), d_out_part], 1)
    d_attn = grad_rows(d_attn, inner).reshape(-1, inner, edges[4])
    d_query, d_key, d_value, d_out_t = [
        d_attn[:, :, edges[n]:edges[n + 1]].reshape(d_attn.shape[0], -1) for n in range(4)
    ]
    mine = hidden_in.astype(F32)
    i_index = lax.axis_index("i")
    r_own = lax.dynamic_slice_in_dim(r_one, i_index * length, length, 0)
    scaled = d_normed_one * my_gain_one
    dot_one = lax.psum(jnp.sum(scaled * mine, axis=-1, keepdims=True), "m") / width
    d_gain_one = jnp.sum(d_normed_one * mine * r_own, axis=0)
    d_input = d_middle + r_own * scaled - mine * (r_own * r_own * r_own) * dot_one

    both = jnp.stack([d_gain_one, d_gain_two], 0)
    wide = lax.dynamic_update_slice(jnp.zeros((2, width), F32), both, (0, m_index * width_part))
    small = jnp.concatenate([wide.reshape(-1), d_qgain_part, d_kgain_part])
    small = lax.psum(small, ALL)
    wide = small[: 2 * width].reshape(2, width)
    shard = attn_gain.shape[0]
    own = lax.dynamic_slice(wide, (0, (t_index * inner + i_index) * shard), (2, shard))
    return (
        block_out, d_input, own[0], d_query, d_key, d_value,
        small[2 * width : 2 * width + head_dim], small[2 * width + head_dim :],
        d_out_t.T, own[1], d_gate, d_up, d_down,
    )


def solution(mesh):
    dp, halves = mesh.shape["dp"], mesh.shape["mp"]
    inner = 4
    groups = dp // inner
    fine = Mesh(mesh.devices.reshape(groups, inner, halves), ("t", "i", "m"))
    rows = P(("t", "i"))
    block = P(("t", "i"), "m")
    turned = P("m", ("t", "i"))
    return jax.shard_map(
        partial(body, groups=groups, inner=inner, halves=halves),
        mesh=fine,
        in_specs=(block, P(), rows, block, block, block, P(), P(), turned, rows, block, block, turned, block),
        out_specs=(block, block, rows, block, block, block, P(), P(), turned, rows, block, block, turned),
        check_vma=False,
    )
```

```python
from functools import partial
import math

import jax
import jax.numpy as jnp
from jax import lax
from jax.experimental import pallas as pl
from jax.experimental.pallas import tpu as pltpu
from jax.sharding import Mesh, PartitionSpec as P

BF = jnp.bfloat16
F32 = jnp.float32
EPS = 1e-05
TP = ("i", "m")
ALL = ("t", "i", "m")


def dot_f32(left, right, dims):
    return lax.dot_general(left, right, (dims, ((), ())), preferred_element_type=F32)


def nn(left, right):
    return dot_f32(left, right, ((1,), (0,)))


def nt(left, right):
    return dot_f32(left, right, ((1,), (1,)))


def tn(left, right):
    return dot_f32(left, right, ((0,), (0,)))


def rms_rows(v, gain):
    return v * lax.rsqrt(jnp.mean(v * v, axis=-1, keepdims=True) + EPS) * gain


def tables(cut_row, length, head_dim):
    position = jnp.arange(length, dtype=jnp.int32)
    doc = (position >= cut_row[0]).astype(jnp.int32) + (position >= cut_row[1]).astype(jnp.int32)
    starts = jnp.where(doc == 0, 0, jnp.where(doc == 1, cut_row[0], cut_row[1]))
    places = (position - starts).astype(F32)
    freqs = jnp.exp(-math.log(1000000.0) * 2.0 * jnp.arange(head_dim // 2, dtype=F32) / head_dim)
    angles = places[:, None] * freqs[None, :]
    angles = jnp.concatenate([angles, angles], axis=-1)
    allowed = (doc[:, None] == doc[None, :]) & (position[None, :] <= position[:, None])
    return jnp.cos(angles), jnp.sin(angles), allowed


def rotate(v, cosine, sine_table):
    halfway = v.shape[-1] // 2
    turned = jnp.concatenate([-v[..., halfway:], v[..., :halfway]], axis=-1)
    return v * cosine + turned * sine_table


def head_piece(pre, gain, cosine, sine_table):
    shaped = pre.reshape(pre.shape[0], -1, gain.shape[0])
    return rotate(rms_rows(shaped, gain), cosine, sine_table)


def attend(inputs, scale):
    queries, keys, values, allowed = inputs
    scores = jnp.einsum("qgd,td->gqt", queries, keys, preferred_element_type=F32) * scale
    scores = jnp.where(allowed[None], scores, -1e30)
    highest = jnp.max(scores, axis=-1, keepdims=True)
    weights_exp = jnp.exp(scores - highest)
    totals = jnp.sum(weights_exp, axis=-1, keepdims=True)
    probs = weights_exp / totals
    log_norm = highest[..., 0] + jnp.log(totals[..., 0])
    outputs = jnp.einsum("gqt,td->qgd", probs.astype(BF), values, preferred_element_type=F32)
    return outputs.astype(BF), log_norm


def attend_grad(inputs, scale):
    queries, keys, values, d_outputs, log_norm, allowed = inputs
    scores = jnp.einsum("qgd,td->gqt", queries, keys, preferred_element_type=F32) * scale
    scores = jnp.where(allowed[None], scores, -1e30)
    probs = jnp.exp(scores - log_norm[..., None])
    d_probs = jnp.einsum("qgd,td->gqt", d_outputs, values, preferred_element_type=F32)
    inner_sum = jnp.sum(probs * d_probs, axis=-1, keepdims=True)
    d_scores = (probs * (d_probs - inner_sum)).astype(BF)
    d_queries = jnp.einsum("gqt,td->qgd", d_scores, keys, preferred_element_type=F32) * scale
    d_keys = jnp.einsum("gqt,qgd->td", d_scores, queries, preferred_element_type=F32) * scale
    d_values = jnp.einsum("gqt,qgd->td", probs.astype(BF), d_outputs, preferred_element_type=F32)
    return d_queries, d_keys, d_values


def gather_pieces(piece, ranks):
    rows, cols = piece.shape
    parts = lax.all_gather(piece, TP, axis=0)
    parts = parts.reshape(ranks[0], ranks[1], rows, cols)
    return jnp.moveaxis(parts, 1, 2).reshape(ranks[0] * rows, ranks[1] * cols)


def scatter_pieces(partial_sum, ranks):
    rows, cols = partial_sum.shape
    parts = partial_sum.astype(BF).reshape(ranks[0], rows // ranks[0], ranks[1], cols // ranks[1])
    parts = jnp.moveaxis(parts, 2, 1).reshape(-1, rows // ranks[0], cols // ranks[1])
    mine = lax.psum_scatter(parts, TP, scatter_dimension=0, tiled=False)
    return mine.astype(F32)


def spread(local, inner):
    rows, cols = local.shape
    parts = jnp.moveaxis(local.reshape(rows, inner, cols // inner), 1, 0)
    parts = lax.all_to_all(parts, "i", 0, 0, tiled=False)
    return parts.reshape(inner * rows, cols // inner)


def collect(block, inner):
    rows, cols = block.shape
    parts = lax.all_to_all(block.reshape(inner, rows // inner, cols), "i", 0, 0, tiled=False)
    return jnp.moveaxis(parts, 0, 1).reshape(rows // inner, inner * cols)


def full_rows(local, inner):
    return lax.all_gather(spread(local, inner), "t", axis=0, tiled=True)


def grad_rows(part, inner):
    mine = lax.psum_scatter(part.astype(BF), "t", scatter_dimension=0, tiled=True)
    return collect(mine, inner).astype(F32)


def plain_body(
    hidden_in, doc_starts, attn_gain, w_query, w_key, w_value, query_gain, key_gain,
    w_out, mlp_gain, w_gate, w_up, w_down, cotangent, *, groups, inner, halves,
):
    length, width_part = hidden_in.shape
    ranks = (inner, halves)
    width = width_part * halves
    head_dim = query_gain.shape[0]
    scale = head_dim ** (-0.5)
    t_index, m_index = lax.axis_index("t"), lax.axis_index("m")
    cuts = lax.dynamic_slice_in_dim(doc_starts, t_index * inner, inner, 0)
    cosine, sine_table, allowed = jax.vmap(partial(tables, length=length, head_dim=head_dim))(cuts)
    cosine = cosine.reshape(inner * length, 1, head_dim)
    sine_table = sine_table.reshape(inner * length, 1, head_dim)
    q_gain, k_gain = query_gain.astype(F32), key_gain.astype(F32)
    gains = lax.all_gather(jnp.stack([attn_gain, mlp_gain], 1), ("t", "i"), axis=0, tiled=True)
    gain_one, gain_two = gains[:, 0].astype(F32), gains[:, 1].astype(F32)

    full_in = gather_pieces(hidden_in, ranks)
    sizes = [w.shape[1] // inner for w in (w_query, w_key, w_value)] + [w_out.shape[0] // inner]
    edges = [sum(sizes[:n]) for n in range(5)]

    def by_rank(w):
        return w.reshape(w.shape[0], inner, w.shape[1] // inner)

    attn_local = jnp.concatenate([by_rank(w_query), by_rank(w_key), by_rank(w_value), by_rank(w_out.T)], 2)
    attn_cols = full_rows(attn_local.reshape(attn_local.shape[0], -1), inner)
    query_cols, key_cols, value_cols, out_t = [attn_cols[:, edges[n]:edges[n + 1]] for n in range(4)]
    resid = full_in.astype(F32)
    r_one = lax.rsqrt(jnp.mean(resid * resid, axis=-1, keepdims=True) + EPS)
    normed_one = (resid * r_one * gain_one).astype(BF)
    gate_cols = full_rows(w_gate, inner)
    up_cols = full_rows(w_up, inner)
    down_t = full_rows(w_down.T, inner)
    grad_full = gather_pieces(cotangent, ranks)

    query_pre = nn(normed_one, query_cols)
    key_pre = nn(normed_one, key_cols)
    value_low = nn(normed_one, value_cols).astype(BF)
    query_rot = head_piece(query_pre, q_gain, cosine, sine_table).astype(BF)
    key_rot = head_piece(key_pre, k_gain, cosine, sine_table).astype(BF)
    group = query_rot.shape[1]
    query_stack = query_rot.reshape(inner, length, group, head_dim)
    key_stack = key_rot.reshape(inner, length, head_dim)
    value_stack = value_low.reshape(inner, length, head_dim)
    attended, log_norm = lax.map(partial(attend, scale=scale), (query_stack, key_stack, value_stack, allowed))
    mixed = attended.reshape(inner * length, group * head_dim)
    middle = hidden_in.astype(F32) + scatter_pieces(nt(mixed, out_t), ranks)
    my_gain_one = lax.dynamic_slice_in_dim(gain_one, m_index * width_part, width_part, 0)
    my_gain_two = lax.dynamic_slice_in_dim(gain_two, m_index * width_part, width_part, 0)
    r_two = lax.rsqrt(lax.psum(jnp.sum(middle * middle, axis=-1, keepdims=True), "m") / width + EPS)
    normed_two = gather_pieces((middle * r_two * my_gain_two).astype(BF), ranks)

    gate_pre, up_pre = nn(normed_two, gate_cols), nn(normed_two, up_cols)
    d_inner = nn(grad_full, down_t)
    sigmoid_gate = jax.nn.sigmoid(gate_pre)
    inner_act = (gate_pre * sigmoid_gate * up_pre).astype(BF)
    d_gate_pre = (d_inner * up_pre * sigmoid_gate * (1.0 + gate_pre * (1.0 - sigmoid_gate))).astype(BF)
    d_up_pre = (d_inner * gate_pre * sigmoid_gate).astype(BF)
    d_normed_two = scatter_pieces(nt(d_gate_pre, gate_cols) + nt(d_up_pre, up_cols), ranks)
    mlp_out = scatter_pieces(nt(inner_act, down_t), ranks)
    block_out = (middle + mlp_out).astype(BF)

    scaled = d_normed_two * my_gain_two
    dot_two = lax.psum(jnp.sum(scaled * middle, axis=-1, keepdims=True), "m") / width
    d_gain_two = jnp.sum(d_normed_two * middle * r_two, axis=0)
    d_middle = cotangent.astype(F32) + r_two * scaled - middle * (r_two * r_two * r_two) * dot_two
    d_middle_low = gather_pieces(d_middle.astype(BF), ranks)
    d_gate = grad_rows(tn(normed_two, d_gate_pre), inner)
    d_up = grad_rows(tn(normed_two, d_up_pre), inner)
    d_down = grad_rows(tn(grad_full, inner_act), inner).T

    d_mixed = nn(d_middle_low, out_t).astype(BF)
    d_out_part = tn(d_middle_low, mixed)
    d_mixed_stack = d_mixed.reshape(inner, length, group, head_dim)
    d_query_stack, d_key_stack, d_value_stack = lax.map(
        partial(attend_grad, scale=scale),
        (query_stack, key_stack, value_stack, d_mixed_stack, log_norm, allowed),
    )
    rotary_piece = partial(head_piece, cosine=cosine, sine_table=sine_table)
    _, query_pull = jax.vjp(rotary_piece, query_pre, q_gain)
    d_query_pre, d_qgain_part = query_pull(d_query_stack.reshape(inner * length, group, head_dim))
    _, key_pull = jax.vjp(rotary_piece, key_pre, k_gain)
    d_key_pre, d_kgain_part = key_pull(d_key_stack.reshape(inner * length, 1, head_dim))
    d_heads = jnp.concatenate(
        [d_query_pre, d_key_pre, d_value_stack.reshape(inner * length, head_dim)], 1
    ).astype(BF)
    heads_cols = attn_cols[:, : edges[3]]
    d_normed_one = scatter_pieces(nt(d_heads, heads_cols), ranks)
    d_attn = jnp.concatenate([tn(normed_one, d_heads), d_out_part], 1)
    d_attn = grad_rows(d_attn, inner).reshape(-1, inner, edges[4])
    d_query, d_key, d_value, d_out_t = [
        d_attn[:, :, edges[n]:edges[n + 1]].reshape(d_attn.shape[0], -1) for n in range(4)
    ]
    mine = hidden_in.astype(F32)
    i_index = lax.axis_index("i")
    r_own = lax.dynamic_slice_in_dim(r_one, i_index * length, length, 0)
    scaled = d_normed_one * my_gain_one
    dot_one = lax.psum(jnp.sum(scaled * mine, axis=-1, keepdims=True), "m") / width
    d_gain_one = jnp.sum(d_normed_one * mine * r_own, axis=0)
    d_input = d_middle + r_own * scaled - mine * (r_own * r_own * r_own) * dot_one

    both = jnp.stack([d_gain_one, d_gain_two], 0)
    wide = lax.dynamic_update_slice(jnp.zeros((2, width), F32), both, (0, m_index * width_part))
    small = jnp.concatenate([wide.reshape(-1), d_qgain_part, d_kgain_part])
    small = lax.psum(small, ALL)
    wide = small[: 2 * width].reshape(2, width)
    shard = attn_gain.shape[0]
    own = lax.dynamic_slice(wide, (0, (t_index * inner + i_index) * shard), (2, shard))
    return (
        block_out, d_input, own[0], d_query, d_key, d_value,
        small[2 * width : 2 * width + head_dim], small[2 * width + head_dim :],
        d_out_t.T, own[1], d_gate, d_up, d_down,
    )


MESH = pl.DeviceIdType.MESH
ANY = pl.BlockSpec(memory_space=pl.ANY)
VMEM = pl.BlockSpec(memory_space=pltpu.VMEM)
SMEM = pl.BlockSpec(memory_space=pltpu.SMEM)
DMA = pltpu.SemaphoreType.DMA
LIMIT = 60 * 1024 * 1024


def flip(index, mask):
    if mask == 1:
        return index + 1 - 2 * lax.rem(index, 2)
    if mask == 2:
        return lax.rem(index + 2, 4)
    return 3 - index


def meet(peers):
    barrier = pltpu.get_barrier_semaphore()
    for peer in peers:
        pl.semaphore_signal(barrier, inc=1, device_id=peer, device_id_type=MESH)
    pl.semaphore_wait(barrier, len(peers))


def remote(src, dst, sems, k, peer):
    return pltpu.make_async_remote_copy(
        src_ref=src, dst_ref=dst, send_sem=sems[0].at[k], recv_sem=sems[1].at[k],
        device_id=peer, device_id_type=MESH,
    )


def at(start, size):
    return pl.ds(pl.multiple_of(start, size), size)


def tp_peers(i, m):
    return {"i": flip(i, 1)}, {"m": 1 - m}, {"i": flip(i, 2)}


class TpGather:
    def __init__(self, piece, full, sems, base, i, m):
        rows, cols = piece.shape
        half = rows // 2
        core, across, along = tp_peers(i, m)

        def slot(a, b, part=None):
            if part is None:
                return full.at[at(a * rows, rows), at(b * cols, cols)]
            return full.at[at(a * rows + part * half, half), at(b * cols, cols)]

        def go(src, dst, k, peer):
            return remote(src, dst, sems, base + k, peer)

        mine, far = slot(i, m), flip(i, 2)
        self.local = pltpu.make_async_copy(piece, mine, sems[2].at[base // 8])
        self.copies = [
            go(piece, mine, 0, core),
            go(piece, mine, 1, across),
            go(piece, mine, 2, along),
            go(slot(i, 1 - m, 0), slot(i, 1 - m, 0), 3, along),
            go(slot(i, 1 - m), slot(i, 1 - m), 4, core),
            go(slot(far, m, 1), slot(far, m, 1), 5, across),
            go(slot(far, m), slot(far, m), 6, core),
            go(slot(far, 1 - m), slot(far, 1 - m), 7, core),
        ]

    def start(self):
        for k in (1, 2, 0):
            self.copies[k].start()
        self.local.start()

    def relay(self):
        self.copies[1].wait_recv()
        self.copies[3].start()
        self.copies[4].start()
        self.copies[2].wait_recv()
        self.copies[5].start()
        self.copies[6].start()

    def relay_far(self):
        self.copies[3].wait_recv()
        self.copies[5].wait_recv()
        self.copies[7].start()

    def finish(self):
        for k in (0, 4, 6, 7):
            self.copies[k].wait_recv()
        for copy in self.copies:
            copy.wait_send()
        self.local.wait()


def add_rows(target, first, second, step=64):
    rows = target.shape[0]

    @pl.loop(0, rows, step=step)
    def _(r):
        span = pl.ds(pl.multiple_of(r, step), step)
        total = first[span, :].astype(F32) + second[span, :].astype(F32)
        target[span, :] = total.astype(target.dtype)


def tp_reduce_scratch(rows, cols, halves):
    return [
        pltpu.VMEM((2, rows, cols * halves), BF),
        pltpu.VMEM((2, rows, cols * halves), BF),
        pltpu.VMEM((2, rows // 2, cols), BF),
        pltpu.VMEM((rows // 2, cols * halves), BF),
        pltpu.VMEM((2, rows // 2, cols), BF),
        DMA((7,)), DMA((7,)), DMA((2,)),
    ]


class TpReduce:
    def __init__(self, parts, out, scratch, i, m):
        own, mate, by_x, by_y, last, send, recv, load = scratch
        rows, cols = out.shape
        half = rows // 2
        core, across, along = tp_peers(i, m)
        sems = (send, recv)
        self.args = (own, mate, by_x, by_y, last, out, m, rows, cols, half)

        def seq(a):
            return parts.at[at(a * rows, rows), :]

        self.loads = [
            pltpu.make_async_copy(seq(flip(i, 2)), own.at[1], load.at[1]),
            pltpu.make_async_copy(seq(i), own.at[0], load.at[0]),
        ]
        theirs = at((1 - m) * cols, cols)
        ours = at(m * cols, cols)
        low, high = pl.ds(0, half), pl.ds(half, half)
        self.copies = [
            remote(seq(flip(i, 3)), mate.at[1], sems, 0, core),
            remote(seq(flip(i, 1)), mate.at[0], sems, 1, core),
            remote(own.at[1, low, theirs], by_x.at[1], sems, 2, across),
            remote(own.at[0, low, theirs], by_x.at[0], sems, 3, across),
            remote(own.at[1, high, :], by_y, sems, 4, along),
            remote(own.at[1, low, ours], last.at[0], sems, 5, along),
            remote(own.at[0, high, theirs], last.at[1], sems, 6, across),
        ]
        self.ours = ours

    def start(self):
        for k in (0, 1):
            self.copies[k].start()
            self.loads[k].start()

    def run(self):
        own, mate, by_x, by_y, last, out, m, rows, cols, half = self.args
        copies, ours = self.copies, self.ours
        low, high = pl.ds(0, half), pl.ds(half, half)
        for side, k in ((1, 0), (0, 1)):
            self.loads[k].wait()
            copies[k].wait_recv()
            add_rows(own.at[side], own.at[side], mate.at[side])
            if side == 1:
                copies[2].start()
                copies[4].start()
            else:
                copies[3].start()
        copies[2].wait_recv()
        add_rows(own.at[1, low, ours], own.at[1, low, ours], by_x.at[1])
        copies[5].start()
        copies[4].wait_recv()
        add_rows(own.at[0, high, :], own.at[0, high, :], by_y)
        copies[6].start()
        copies[3].wait_recv()
        add_rows(own.at[0, low, ours], own.at[0, low, ours], by_x.at[0])
        copies[5].wait_recv()
        add_rows(out.at[low, :], own.at[0, low, ours], last.at[0])
        copies[6].wait_recv()
        add_rows(out.at[high, :], own.at[0, high, ours], last.at[1])
        for copy in copies:
            copy.wait_send()


def line_gather(full, block_rows, groups, sems, t):
    def go(block, k, step):
        view = full.at[at(block * block_rows, block_rows), :]
        side = 0 if step > 0 else 1
        return remote(view, view, sems, side * groups + k, {"t": t + step})

    up, down = t < groups - 1, t > 0
    for k in range(groups - 1):
        @pl.when(up & (t - k >= 0))
        def _():
            go(t - k, k, 1).start()

        @pl.when(down & (t + k <= groups - 1))
        def _():
            go(t + k, k, -1).start()

        @pl.when(t - k - 1 >= 0)
        def _():
            go(t - k - 1, k, 1).wait_recv()

        @pl.when(t + k + 1 <= groups - 1)
        def _():
            go(t + k + 1, k, -1).wait_recv()

    for k in range(groups - 1):
        @pl.when(up & (t - k >= 0))
        def _():
            go(t - k, k, 1).wait_send()

        @pl.when(down & (t + k <= groups - 1))
        def _():
            go(t + k, k, -1).wait_send()


def spread_kernel(groups, pack, gate, up, down, attn, gate_out, up_out, down_out,
                  send, recv, local, z_send, z_recv):
    t, i, m = lax.axis_index("t"), lax.axis_index("i"), lax.axis_index("m")
    rows = pack.shape[1]
    width = gate_out.shape[1]
    others = [{"i": flip(i, j)} for j in (1, 2, 3)]
    meet(others + [{"t": flip(t, j)} for j in (1, 2, 3)])
    mine = attn.at[at((t * 4 + i) * rows, rows), :]
    first, rest = [], []
    for j in (2, 3, 1):
        first.append(remote(pack.at[flip(i, j)], mine, (send, recv), j - 1, others[j - 1]))
    own = [pltpu.make_async_copy(pack.at[i], mine, local.at[0])]
    place = at(i * rows, rows)
    for n, (src, dst) in enumerate(((gate, gate_out), (up, up_out), (down, down_out))):
        for j in (2, 3, 1):
            view = src.at[:, at(flip(i, j) * width, width)]
            rest.append(remote(view, dst.at[place, :], (send, recv), 3 * n + 2 + j, others[j - 1]))
        own.append(pltpu.make_async_copy(src.at[:, at(i * width, width)], dst.at[place, :], local.at[n + 1]))
    for copy in first + own + rest:
        copy.start()
    own[0].wait()
    for copy in first:
        copy.wait_recv()
    line_gather(attn, 4 * rows, groups, (z_send, z_recv), t)
    for copy in own[1:]:
        copy.wait()
    for copy in rest:
        copy.wait_recv()
    for copy in first + rest:
        copy.wait_send()


def tp_group(i, m):
    return list(tp_peers(i, m))


def gather_kernel(hidden, cot, full_in, grad_full, send, recv, local):
    i, m = lax.axis_index("i"), lax.axis_index("m")
    meet(tp_group(i, m))
    one = TpGather(hidden, full_in, (send, recv, local), 0, i, m)
    two = TpGather(cot, grad_full, (send, recv, local), 8, i, m)
    one.start()
    two.start()
    one.relay()
    one.relay_far()
    two.relay()
    two.relay_far()
    one.finish()
    two.finish()


def row_loop(rows, step=64):
    def wrap(f):
        @pl.loop(0, rows, step=step)
        def _(r):
            f(pl.ds(pl.multiple_of(r, step), step))

    return wrap


def middle_kernel(parts, hidden, gain, middle, stat, full, *scratch):
    reduce_scratch, (piece, other, send, recv, local, s_send, s_recv) = scratch[:8], scratch[8:]
    i, m = lax.axis_index("i"), lax.axis_index("m")
    meet(tp_group(i, m))
    width = hidden.shape[1] * 2
    reduce = TpReduce(parts, middle, reduce_scratch, i, m)
    reduce.start()
    reduce.run()

    @row_loop(hidden.shape[0])
    def _(span):
        v = middle[span, :] + hidden[span, :].astype(F32)
        middle[span, :] = v
        stat[span, :] = jnp.broadcast_to(jnp.sum(v * v, axis=-1, keepdims=True), stat[span, :].shape)

    swap = remote(stat, other, (s_send, s_recv), 0, {"m": 1 - m})
    swap.start()
    swap.wait()

    @row_loop(hidden.shape[0])
    def _(span):
        r = lax.rsqrt((stat[span, :] + other[span, :]) / width + EPS)
        stat[span, :] = r
        piece[span, :] = (middle[span, :] * r[:, :1] * gain[...]).astype(BF)

    gather = TpGather(piece, full, (send, recv, local), 0, i, m)
    gather.start()
    gather.relay()
    gather.relay_far()
    gather.finish()


def back_kernel(parts, middle, stat, cot, gain, d_middle, d_gain, full, *scratch):
    reduce_scratch, (piece, sums, other, send, recv, local, s_send, s_recv) = scratch[:8], scratch[8:]
    i, m = lax.axis_index("i"), lax.axis_index("m")
    meet(tp_group(i, m))
    width = middle.shape[1] * 2
    reduce = TpReduce(parts, d_middle, reduce_scratch, i, m)
    reduce.start()
    d_gain[...] = jnp.zeros_like(d_gain)
    reduce.run()

    @row_loop(middle.shape[0])
    def _(span):
        dn, v, r = d_middle[span, :], middle[span, :], stat[span, :]
        scaled = dn * gain[...]
        sums[span, :] = jnp.broadcast_to(jnp.sum(scaled * v, axis=-1, keepdims=True), r.shape)
        d_gain[0:1, :] += jnp.sum(dn * v * r[:, :1], axis=0, keepdims=True)

    swap = remote(sums, other, (s_send, s_recv), 0, {"m": 1 - m})
    swap.start()
    swap.wait()

    @row_loop(middle.shape[0])
    def _(span):
        r = stat[span, :]
        factor = (r * r * r * ((sums[span, :] + other[span, :]) / width))[:, :1]
        d = cot[span, :].astype(F32) + r[:, :1] * (d_middle[span, :] * gain[...]) - middle[span, :] * factor
        d_middle[span, :] = d
        piece[span, :] = d.astype(BF)

    gather = TpGather(piece, full, (send, recv, local), 0, i, m)
    gather.start()
    gather.relay()
    gather.relay_far()
    gather.finish()


def final_kernel(groups, parts, out_parts, grads, hidden, stat, gain, d_middle, middle, gains_in,
                 d_input, block_out, attn, gains, *scratch):
    reduce_one, reduce_two = scratch[:8], scratch[8:16]
    (res, up_in, down_in, total, sums, other, g_in, send, recv, z_send, z_recv, g_send, g_recv,
     s_send, s_recv, local) = scratch[16:]
    t, i, m = lax.axis_index("t"), lax.axis_index("i"), lax.axis_index("m")
    others = [{"i": flip(i, j)} for j in (1, 2, 3)]
    meet(others + [{"m": 1 - m}] + [{"t": flip(t, j)} for j in (1, 2, 3)])
    width = hidden.shape[1] * 2
    block = width // groups
    one = TpReduce(parts, d_input, reduce_one, i, m)
    two = TpReduce(out_parts, res, reduce_two, i, m)
    one.start()
    two.start()

    def lanes(b):
        return grads.at[:, at(b * block, block)]

    def up(k, src):
        return remote(src, up_in.at[k], (z_send, z_recv), k, {"t": t + 1})

    def down(k, src):
        return remote(src, down_in.at[k], (z_send, z_recv), groups + k, {"t": t - 1})

    @pl.when(t == 0)
    def _():
        for k in range(groups - 1):
            up(k, lanes(groups - 1 - k)).start()

    @pl.when(t == groups - 1)
    def _():
        for k in range(groups - 1):
            down(k, lanes(k)).start()

    one.run()
    for k in range(groups - 1):
        b = groups - 1 - k

        @pl.when((t > 0) & (b > t))
        def _():
            up(k, up_in.at[k]).wait_recv()
            add_rows(up_in.at[k], up_in.at[k], lanes(b))
            up(k, up_in.at[k]).start()

        @pl.when((t < groups - 1) & (k < t))
        def _():
            down(k, down_in.at[k]).wait_recv()
            add_rows(down_in.at[k], down_in.at[k], lanes(k))
            down(k, down_in.at[k]).start()

    rows = hidden.shape[0]
    gains[...] = gains_in[...]

    @row_loop(rows)
    def _(span):
        dn, v, r = d_input[span, :], hidden[span, :].astype(F32), stat[span, :]
        sums[span, :] = jnp.broadcast_to(jnp.sum(dn * gain[...] * v, axis=-1, keepdims=True), r.shape)
        gains[0:1, at(m * (width // 2), width // 2)] += jnp.sum(dn * v * r[:, :1], axis=0, keepdims=True)

    swap = remote(sums, other, (s_send, s_recv), 0, {"m": 1 - m})
    swap.start()
    swap.wait()

    @row_loop(rows)
    def _(span):
        r = stat[span, :]
        factor = (r * r * r * ((sums[span, :] + other[span, :]) / width))[:, :1]
        d = d_middle[span, :] + r[:, :1] * (d_input[span, :] * gain[...])
        d_input[span, :] = d - hidden[span, :].astype(F32) * factor

    ways = [{"i": flip(i, 1)}, {"m": 1 - m}, {"i": flip(i, 2)}, {"t": flip(t, 1)}, {"t": flip(t, 2)}]
    for k, peer in enumerate(ways):
        trade = remote(gains, g_in.at[k], (g_send, g_recv), k, peer)
        trade.start()
        trade.wait()
        gains[...] += g_in[k]

    for b in range(groups):
        @pl.when(t == b)
        def _():
            own = lanes(b)
            if b > 0:
                up(groups - 1 - b, up_in.at[0]).wait_recv()
                add_rows(total, own, up_in.at[groups - 1 - b])
                own = total
            if b < groups - 1:
                down(b, down_in.at[0]).wait_recv()
                add_rows(total, own, down_in.at[b])

    sub = block // 4
    moves = []
    for j in (2, 3, 1):
        view = total.at[:, at(flip(i, j) * sub, sub)]
        moves.append(remote(view, attn.at[i], (send, recv), j, others[j - 1]))
    keep = pltpu.make_async_copy(total.at[:, at(i * sub, sub)], attn.at[i], local.at[0])
    for move in moves:
        move.start()
    keep.start()
    two.run()

    @row_loop(rows)
    def _(span):
        block_out[span, :] = (middle[span, :] + res[span, :]).astype(BF)

    for k in range(groups - 1):
        @pl.when(t < groups - 1 - k)
        def _():
            up(k, up_in.at[k]).wait_send()

        @pl.when(t > k)
        def _():
            down(k, down_in.at[k]).wait_send()

    keep.wait()
    for move in moves:
        move.wait()


def collect_kernel(gate, up, down, gate_out, up_out, down_out, send, recv, local):
    i = lax.axis_index("i")
    others = [{"i": flip(i, j)} for j in (1, 2, 3)]
    meet(others)
    rows, width = gate_out.shape[0], gate.shape[1]
    place = at(i * width, width)
    moves, own = [], []
    for n, (src, dst) in enumerate(((gate, gate_out), (up, up_out), (down, down_out))):
        for j in (2, 3, 1):
            view = src.at[at(flip(i, j) * rows, rows), :]
            moves.append(remote(view, dst.at[:, place], (send, recv), 3 * n + j - 1, others[j - 1]))
        own.append(pltpu.make_async_copy(src.at[at(i * rows, rows), :], dst.at[:, place], local.at[n]))
    for copy in moves + own:
        copy.start()
    for copy in moves + own:
        copy.wait()


def shape(dims, dtype):
    return jax.ShapeDtypeStruct(dims, dtype)


def comm_call(kernel, ins, outs, scratch, number):
    return pl.pallas_call(
        kernel,
        out_shape=[s for s, _ in outs],
        in_specs=ins,
        out_specs=[b for _, b in outs],
        scratch_shapes=scratch,
        compiler_params=pltpu.CompilerParams(
            collective_id=number, has_side_effects=True, vmem_limit_bytes=LIMIT
        ),
    )


def allow(cut, q0, qn, kn):
    q = q0 + lax.broadcasted_iota(jnp.int32, (qn, kn), 0)
    k = lax.broadcasted_iota(jnp.int32, (qn, kn), 1)
    doc_q = (q >= cut[0]).astype(jnp.int32) + (q >= cut[1]).astype(jnp.int32)
    doc_k = (k >= cut[0]).astype(jnp.int32) + (k >= cut[1]).astype(jnp.int32)
    return (doc_q == doc_k) & (k <= q)


def turn(v):
    half = v.shape[1] // 2
    return jnp.concatenate([-v[:, half:], v[:, :half]], axis=1)


def turn_back(v):
    half = v.shape[1] // 2
    return jnp.concatenate([v[:, half:], -v[:, :half]], axis=1)


def fore_kernel(heads, hd, cuts, x, weights, gain, qk_gain, cos, sin,
                normed, pre, qkv, stats, mixed, parts):
    s = pl.program_id(0)
    cut = (cuts[s, 0], cuts[s, 1])
    rows = x.shape[0]
    nq, kv = heads * hd, (heads + 2) * hd

    @row_loop(rows)
    def _(span):
        v = x[span, :].astype(F32)
        r = lax.rsqrt(jnp.mean(v * v, axis=-1, keepdims=True) + EPS)
        stats[span, :] = jnp.broadcast_to(r, (r.shape[0], stats.shape[1]))
        normed[span, :] = (v * r * gain[...]).astype(BF)

    heads_pre = nn(normed[...], weights[:, :kv])
    pre[...] = heads_pre
    for h in range(heads + 1):
        lanes = slice(h * hd, (h + 1) * hd)
        v = heads_pre[:, lanes]
        g = qk_gain[0:1, :] if h < heads else qk_gain[1:2, :]
        n = rms_rows(v, g)
        qkv[:, lanes] = (n * cos[...] + turn(n) * sin[...]).astype(BF)
    qkv[:, nq + hd:kv] = heads_pre[:, nq + hd:kv].astype(BF)
    step = rows // 2
    for b in range(2):
        span, kn = slice(b * step, (b + 1) * step), (b + 1) * step
        mask = allow(cut, b * step, step, kn)
        keys, values = qkv[0:kn, nq:nq + hd], qkv[0:kn, nq + hd:kv]
        for h in range(heads):
            q = qkv[span, h * hd:(h + 1) * hd]
            scores = jnp.where(mask, nt(q, keys) * (hd ** -0.5), -1e30)
            top = jnp.max(scores, axis=-1, keepdims=True)
            e = jnp.exp(scores - top)
            total = jnp.sum(e, axis=-1, keepdims=True)
            probs = (e * (1.0 / total)).astype(BF)
            stats[span, h:h + 1] = top + jnp.log(total)
            mixed[span, h * hd:(h + 1) * hd] = nn(probs, values).astype(BF)
    wide = parts.shape[1]

    @pl.loop(0, wide, step=512)
    def _(c):
        cols = pl.ds(pl.multiple_of(c, 512), 512)
        parts[:, cols] = nt(mixed[...], weights[cols, kv:kv + nq]).astype(BF)


def aft_kernel(heads, hd, cuts, dm, normed, pre, qkv, stats, mixed, weights, qk_gain, cos, sin,
               parts, grads, gains, d_mix, d_pre, d_kv, acc):
    s = pl.program_id(0)
    cut = (cuts[s, 0], cuts[s, 1])
    rows = dm.shape[0]
    nq, kv = heads * hd, (heads + 2) * hd
    scale = hd ** -0.5

    @pl.when(s == 0)
    def _():
        acc[...] = jnp.zeros_like(acc)
        gains[...] = jnp.zeros_like(gains)

    d_mix[...] = nn(dm[...], weights[:, kv:kv + nq]).astype(BF)
    d_kv[...] = jnp.zeros_like(d_kv)
    step = rows // 2

    def undo(h, grad):
        lanes = slice(h * hd, (h + 1) * hd)
        row = 0 if h < heads else 1
        g = qk_gain[row:row + 1, :]
        u = cos[...] * grad + turn_back(sin[...] * grad)
        v = pre[:, lanes]
        r = lax.rsqrt(jnp.mean(v * v, axis=-1, keepdims=True) + EPS)
        gains[0:1, row * hd:(row + 1) * hd] += jnp.sum(u * v * r, axis=0, keepdims=True)
        scaled = u * g
        back = r * scaled - v * (r * r * r) * jnp.mean(scaled * v, axis=-1, keepdims=True)
        d_pre[:, lanes] = back.astype(BF)

    for h in range(heads):
        lanes = slice(h * hd, (h + 1) * hd)
        pieces = []
        for b in range(2):
            span, kn = slice(b * step, (b + 1) * step), (b + 1) * step
            mask = allow(cut, b * step, step, kn)
            keys, values = qkv[0:kn, nq:nq + hd], qkv[0:kn, nq + hd:kv]
            q, go = qkv[span, lanes], d_mix[span, lanes]
            scores = jnp.where(mask, nt(q, keys) * scale, -1e30)
            probs = jnp.exp(scores - stats[span, h:h + 1])
            d_probs = nt(go, values)
            inner = jnp.sum(probs * d_probs, axis=-1, keepdims=True)
            d_scores = (probs * (d_probs - inner)).astype(BF)
            pieces.append(nn(d_scores, keys) * scale)
            d_kv[0:kn, 0:hd] += tn(d_scores, q) * scale
            d_kv[0:kn, hd:2 * hd] += tn(probs.astype(BF), go)
        undo(h, jnp.concatenate(pieces, axis=0))
    undo(heads, d_kv[:, 0:hd])
    d_pre[:, nq + hd:kv] = d_kv[:, hd:2 * hd].astype(BF)
    wide = parts.shape[1]

    @pl.loop(0, wide, step=512)
    def _(c):
        cols = pl.ds(pl.multiple_of(c, 512), 512)
        parts[:, cols] = nt(d_pre[...], weights[cols, 0:kv]).astype(BF)
        acc[0:kv, cols] += tn(d_pre[...], normed[:, cols])
        acc[kv:kv + nq, cols] += tn(mixed[...], dm[:, cols])

    @pl.when(s == pl.num_programs(0) - 1)
    def _():
        grads[...] = acc[...].astype(BF)


def fast_body(
    hidden_in, doc_starts, attn_gain, w_query, w_key, w_value, query_gain, key_gain,
    w_out, mlp_gain, w_gate, w_up, w_down, cotangent, *, groups, inner, halves,
):
    length, part = hidden_in.shape
    shard = w_query.shape[0]
    width, tokens = part * halves, length * inner
    hd = query_gain.shape[0]
    heads = w_query.shape[1] // inner // hd
    nq, kv = heads * hd, (heads + 2) * hd
    hidden_units = w_gate.shape[1] // inner
    t_index, i_index, m_index = lax.axis_index("t"), lax.axis_index("i"), lax.axis_index("m")
    cuts = lax.dynamic_slice_in_dim(doc_starts, t_index * inner, inner, 0)
    cosine, sine_table, _ = jax.vmap(partial(tables, length=length, head_dim=hd))(cuts)
    cosine, sine_table = cosine.reshape(tokens, hd), sine_table.reshape(tokens, hd)
    qk_gain = jnp.zeros((8, hd), F32).at[0].set(query_gain.astype(F32)).at[1].set(key_gain.astype(F32))

    def by_rank(w):
        return jnp.moveaxis(w.reshape(shard, inner, w.shape[1] // inner), 1, 0)

    gains = jnp.zeros((shard, 128), BF).at[:, 0].set(attn_gain).at[:, 1].set(mlp_gain)
    pack = jnp.concatenate(
        [by_rank(w_query), by_rank(w_key), by_rank(w_value), by_rank(w_out.T),
         jnp.broadcast_to(gains[None], (inner, shard, 128))], 2)
    cols = pack.shape[2]
    tp_rows = inner * shard
    attn_w, gate_w, up_w, down_w = comm_call(
        partial(spread_kernel, groups), [ANY] * 4,
        [(shape((groups * tp_rows, cols), BF), ANY)] + [(shape((tp_rows, hidden_units), BF), ANY)] * 3,
        [DMA((12,)), DMA((12,)), DMA((4,)), DMA((2 * groups,)), DMA((2 * groups,))], 0,
    )(pack, w_gate, w_up, w_down.T)
    gate_cols, up_cols, down_t = [lax.all_gather(w, "t", axis=0, tiled=True) for w in (gate_w, up_w, down_w)]
    full_in, grad_full = comm_call(
        gather_kernel, [ANY] * 2, [(shape((tokens, width), BF), ANY)] * 2,
        [DMA((16,)), DMA((16,)), DMA((2,))], 1,
    )(hidden_in, cotangent)
    both_gains = attn_w[:, nq + kv:nq + kv + 2].astype(F32).T
    gain_one = both_gains[0:1]
    own_gains = lax.dynamic_slice(both_gains, (0, m_index * part), (2, part))

    def seq(lanes):
        return pl.BlockSpec((length, lanes), lambda s: (s, 0))

    def whole(*dims):
        return pl.BlockSpec(dims, lambda s: (0,) * len(dims))

    params = pltpu.CompilerParams(vmem_limit_bytes=LIMIT, dimension_semantics=("arbitrary",))
    normed_one, pre, qkv, stats, mixed, parts = pl.pallas_call(
        partial(fore_kernel, heads, hd),
        grid=(inner,),
        in_specs=[SMEM, seq(width), whole(width, cols), whole(1, width), whole(8, hd), seq(hd), seq(hd)],
        out_shape=[shape((tokens, width), BF), shape((tokens, kv), F32), shape((tokens, kv), BF),
                   shape((tokens, 128), F32), shape((tokens, nq), BF), shape((tokens, width), BF)],
        out_specs=[seq(width), seq(kv), seq(kv), seq(128), seq(nq), seq(width)],
        compiler_params=params,
    )(cuts, full_in, attn_w, gain_one, qk_gain, cosine, sine_table)

    half_scratch = tp_reduce_scratch(length, part, halves)
    gather_sems = [DMA((8,)), DMA((8,)), DMA((1,)), DMA((1,)), DMA((1,))]
    middle, r_two, normed_two = comm_call(
        middle_kernel, [ANY, VMEM, VMEM],
        [(shape((length, part), F32), VMEM), (shape((length, 128), F32), VMEM), (shape((tokens, width), BF), ANY)],
        half_scratch + [pltpu.VMEM((length, part), BF), pltpu.VMEM((length, 128), F32)] + gather_sems, 2,
    )(parts, hidden_in, own_gains[1:2])

    gate_pre, up_pre = nn(normed_two, gate_cols), nn(normed_two, up_cols)
    d_inner = nn(grad_full, down_t)
    sigmoid_gate = jax.nn.sigmoid(gate_pre)
    inner_act = (gate_pre * sigmoid_gate * up_pre).astype(BF)
    d_gate_pre = (d_inner * up_pre * sigmoid_gate * (1.0 + gate_pre * (1.0 - sigmoid_gate))).astype(BF)
    d_up_pre = (d_inner * gate_pre * sigmoid_gate).astype(BF)
    d_two_parts = (nt(d_gate_pre, gate_cols) + nt(d_up_pre, up_cols)).astype(BF)
    d_down, d_gate, d_up = [
        lax.psum_scatter(tn(a, b).astype(BF), "t", scatter_dimension=0, tiled=True)
        for a, b in ((grad_full, inner_act), (normed_two, d_gate_pre), (normed_two, d_up_pre))
    ]
    out_parts = nt(inner_act, down_t).astype(BF)

    d_middle, d_gain_two, d_low = comm_call(
        back_kernel, [ANY] + [VMEM] * 4,
        [(shape((length, part), F32), VMEM), (shape((8, part), F32), VMEM), (shape((tokens, width), BF), ANY)],
        half_scratch + [pltpu.VMEM((length, part), BF)] + [pltpu.VMEM((length, 128), F32)] * 2 + gather_sems, 3,
    )(d_two_parts, middle, r_two, cotangent, own_gains[1:2])

    d_one_parts, d_attn, qk_grad = pl.pallas_call(
        partial(aft_kernel, heads, hd),
        grid=(inner,),
        in_specs=[SMEM, seq(width), seq(width), seq(kv), seq(kv), seq(128), seq(nq), whole(width, cols),
                  whole(8, hd), seq(hd), seq(hd)],
        out_shape=[shape((tokens, width), BF), shape((nq + kv, width), BF), shape((8, 2 * hd), F32)],
        out_specs=[seq(width), whole(nq + kv, width), whole(8, 2 * hd)],
        scratch_shapes=[pltpu.VMEM((length, nq), BF), pltpu.VMEM((length, kv), BF),
                        pltpu.VMEM((length, 2 * hd), F32), pltpu.VMEM((nq + kv, width), F32)],
        compiler_params=params,
    )(cuts, d_low, normed_one, pre, qkv, stats, mixed, attn_w, qk_gain, cosine, sine_table)

    gains_in = jnp.zeros((8, width), F32)
    gains_in = lax.dynamic_update_slice(gains_in, d_gain_two[0:1], (1, m_index * part))
    gains_in = gains_in.at[2].set(jnp.tile(qk_grad[0], width // (2 * hd)))
    r_one = lax.dynamic_slice_in_dim(stats, i_index * length, length, 0)
    r_one = jnp.broadcast_to(r_one[:, heads:heads + 1], (length, 128))
    block = width // groups
    d_input, block_out, attn_back, gains_out = comm_call(
        partial(final_kernel, groups), [ANY, ANY] + [VMEM] * 7,
        [(shape((length, part), F32), VMEM), (shape((length, part), BF), VMEM),
         (shape((inner, nq + kv, block // inner), BF), ANY), (shape((8, width), F32), VMEM)],
        half_scratch * 2 + [
            pltpu.VMEM((length, part), F32),
            pltpu.VMEM((groups, nq + kv, block), BF), pltpu.VMEM((groups, nq + kv, block), BF),
            pltpu.VMEM((nq + kv, block), BF),
            pltpu.VMEM((length, 128), F32), pltpu.VMEM((length, 128), F32),
            pltpu.VMEM((5, 8, width), F32),
            DMA((4,)), DMA((4,)), DMA((2 * groups,)), DMA((2 * groups,)), DMA((5,)), DMA((5,)),
            DMA((1,)), DMA((1,)), DMA((1,))], 4,
    )(d_one_parts, out_parts, d_attn, hidden_in, r_one, own_gains[0:1], d_middle, middle, gains_in)

    d_gate, d_up, d_down = comm_call(
        collect_kernel, [ANY] * 3, [(shape((shard, inner * hidden_units), BF), ANY)] * 3,
        [DMA((9,)), DMA((9,)), DMA((3,))], 5,
    )(d_gate, d_up, d_down)
    own = lax.dynamic_slice(gains_out, (0, (t_index * inner + i_index) * shard), (2, shard))

    def columns(first, last):
        return jnp.moveaxis(attn_back[:, first:last, :], 2, 0).reshape(shard, -1).astype(F32)

    return (
        block_out, d_input, own[0], columns(0, nq), columns(nq, nq + hd), columns(nq + hd, kv),
        gains_out[2, :hd], gains_out[2, hd:2 * hd],
        attn_back[:, kv:kv + nq, :].reshape(inner * nq, shard).astype(F32), own[1],
        d_gate.astype(F32), d_up.astype(F32), d_down.T.astype(F32),
    )


def solution(mesh):
    dp, halves = mesh.shape["dp"], mesh.shape["mp"]
    inner = 4
    groups = dp // inner
    fine = Mesh(mesh.devices.reshape(groups, inner, halves), ("t", "i", "m"))
    rows = P(("t", "i"))
    block = P(("t", "i"), "m")
    turned = P("m", ("t", "i"))
    body = fast_body if groups == 4 and halves == 2 else plain_body
    return jax.shard_map(
        partial(body, groups=groups, inner=inner, halves=halves),
        mesh=fine,
        in_specs=(block, P(), rows, block, block, block, P(), P(), turned, rows, block, block, turned, block),
        out_specs=(block, block, rows, block, block, block, P(), P(), turned, rows, block, block, turned),
        check_vma=False,
    )
```

```python
from functools import partial
import math

import jax
import jax.numpy as jnp
from jax import lax
from jax.experimental import pallas as pl
from jax.experimental.pallas import tpu as pltpu
from jax.sharding import Mesh, PartitionSpec as P

BF = jnp.bfloat16
F32 = jnp.float32
EPS = 1e-05
TP = ("i", "m")
ALL = ("t", "i", "m")


def dot_f32(left, right, dims):
    return lax.dot_general(left, right, (dims, ((), ())), preferred_element_type=F32)


def nn(left, right):
    return dot_f32(left, right, ((1,), (0,)))


def nt(left, right):
    return dot_f32(left, right, ((1,), (1,)))


def tn(left, right):
    return dot_f32(left, right, ((0,), (0,)))


def rms_rows(v, gain):
    return v * lax.rsqrt(jnp.mean(v * v, axis=-1, keepdims=True) + EPS) * gain


def tables(cut_row, length, head_dim):
    position = jnp.arange(length, dtype=jnp.int32)
    doc = (position >= cut_row[0]).astype(jnp.int32) + (position >= cut_row[1]).astype(jnp.int32)
    starts = jnp.where(doc == 0, 0, jnp.where(doc == 1, cut_row[0], cut_row[1]))
    places = (position - starts).astype(F32)
    freqs = jnp.exp(-math.log(1000000.0) * 2.0 * jnp.arange(head_dim // 2, dtype=F32) / head_dim)
    angles = places[:, None] * freqs[None, :]
    angles = jnp.concatenate([angles, angles], axis=-1)
    allowed = (doc[:, None] == doc[None, :]) & (position[None, :] <= position[:, None])
    return jnp.cos(angles), jnp.sin(angles), allowed


def rotate(v, cosine, sine_table):
    halfway = v.shape[-1] // 2
    turned = jnp.concatenate([-v[..., halfway:], v[..., :halfway]], axis=-1)
    return v * cosine + turned * sine_table


def head_piece(pre, gain, cosine, sine_table):
    shaped = pre.reshape(pre.shape[0], -1, gain.shape[0])
    return rotate(rms_rows(shaped, gain), cosine, sine_table)


def attend(inputs, scale):
    queries, keys, values, allowed = inputs
    scores = jnp.einsum("qgd,td->gqt", queries, keys, preferred_element_type=F32) * scale
    scores = jnp.where(allowed[None], scores, -1e30)
    highest = jnp.max(scores, axis=-1, keepdims=True)
    weights_exp = jnp.exp(scores - highest)
    totals = jnp.sum(weights_exp, axis=-1, keepdims=True)
    probs = weights_exp / totals
    log_norm = highest[..., 0] + jnp.log(totals[..., 0])
    outputs = jnp.einsum("gqt,td->qgd", probs.astype(BF), values, preferred_element_type=F32)
    return outputs.astype(BF), log_norm


def attend_grad(inputs, scale):
    queries, keys, values, d_outputs, log_norm, allowed = inputs
    scores = jnp.einsum("qgd,td->gqt", queries, keys, preferred_element_type=F32) * scale
    scores = jnp.where(allowed[None], scores, -1e30)
    probs = jnp.exp(scores - log_norm[..., None])
    d_probs = jnp.einsum("qgd,td->gqt", d_outputs, values, preferred_element_type=F32)
    inner_sum = jnp.sum(probs * d_probs, axis=-1, keepdims=True)
    d_scores = (probs * (d_probs - inner_sum)).astype(BF)
    d_queries = jnp.einsum("gqt,td->qgd", d_scores, keys, preferred_element_type=F32) * scale
    d_keys = jnp.einsum("gqt,qgd->td", d_scores, queries, preferred_element_type=F32) * scale
    d_values = jnp.einsum("gqt,qgd->td", probs.astype(BF), d_outputs, preferred_element_type=F32)
    return d_queries, d_keys, d_values


def gather_pieces(piece, ranks):
    rows, cols = piece.shape
    parts = lax.all_gather(piece, TP, axis=0)
    parts = parts.reshape(ranks[0], ranks[1], rows, cols)
    return jnp.moveaxis(parts, 1, 2).reshape(ranks[0] * rows, ranks[1] * cols)


def scatter_pieces(partial_sum, ranks):
    rows, cols = partial_sum.shape
    parts = partial_sum.astype(BF).reshape(ranks[0], rows // ranks[0], ranks[1], cols // ranks[1])
    parts = jnp.moveaxis(parts, 2, 1).reshape(-1, rows // ranks[0], cols // ranks[1])
    mine = lax.psum_scatter(parts, TP, scatter_dimension=0, tiled=False)
    return mine.astype(F32)


def spread(local, inner):
    rows, cols = local.shape
    parts = jnp.moveaxis(local.reshape(rows, inner, cols // inner), 1, 0)
    parts = lax.all_to_all(parts, "i", 0, 0, tiled=False)
    return parts.reshape(inner * rows, cols // inner)


def collect(block, inner):
    rows, cols = block.shape
    parts = lax.all_to_all(block.reshape(inner, rows // inner, cols), "i", 0, 0, tiled=False)
    return jnp.moveaxis(parts, 0, 1).reshape(rows // inner, inner * cols)


def full_rows(local, inner):
    return lax.all_gather(spread(local, inner), "t", axis=0, tiled=True)


def grad_rows(part, inner):
    mine = lax.psum_scatter(part.astype(BF), "t", scatter_dimension=0, tiled=True)
    return collect(mine, inner).astype(F32)


def plain_body(
    hidden_in, doc_starts, attn_gain, w_query, w_key, w_value, query_gain, key_gain,
    w_out, mlp_gain, w_gate, w_up, w_down, cotangent, *, groups, inner, halves,
):
    length, width_part = hidden_in.shape
    ranks = (inner, halves)
    width = width_part * halves
    head_dim = query_gain.shape[0]
    scale = head_dim ** (-0.5)
    t_index, m_index = lax.axis_index("t"), lax.axis_index("m")
    cuts = lax.dynamic_slice_in_dim(doc_starts, t_index * inner, inner, 0)
    cosine, sine_table, allowed = jax.vmap(partial(tables, length=length, head_dim=head_dim))(cuts)
    cosine = cosine.reshape(inner * length, 1, head_dim)
    sine_table = sine_table.reshape(inner * length, 1, head_dim)
    q_gain, k_gain = query_gain.astype(F32), key_gain.astype(F32)
    gains = lax.all_gather(jnp.stack([attn_gain, mlp_gain], 1), ("t", "i"), axis=0, tiled=True)
    gain_one, gain_two = gains[:, 0].astype(F32), gains[:, 1].astype(F32)

    full_in = gather_pieces(hidden_in, ranks)
    sizes = [w.shape[1] // inner for w in (w_query, w_key, w_value)] + [w_out.shape[0] // inner]
    edges = [sum(sizes[:n]) for n in range(5)]

    def by_rank(w):
        return w.reshape(w.shape[0], inner, w.shape[1] // inner)

    attn_local = jnp.concatenate([by_rank(w_query), by_rank(w_key), by_rank(w_value), by_rank(w_out.T)], 2)
    attn_cols = full_rows(attn_local.reshape(attn_local.shape[0], -1), inner)
    query_cols, key_cols, value_cols, out_t = [attn_cols[:, edges[n]:edges[n + 1]] for n in range(4)]
    resid = full_in.astype(F32)
    r_one = lax.rsqrt(jnp.mean(resid * resid, axis=-1, keepdims=True) + EPS)
    normed_one = (resid * r_one * gain_one).astype(BF)
    gate_cols = full_rows(w_gate, inner)
    up_cols = full_rows(w_up, inner)
    down_t = full_rows(w_down.T, inner)
    grad_full = gather_pieces(cotangent, ranks)

    query_pre = nn(normed_one, query_cols)
    key_pre = nn(normed_one, key_cols)
    value_low = nn(normed_one, value_cols).astype(BF)
    query_rot = head_piece(query_pre, q_gain, cosine, sine_table).astype(BF)
    key_rot = head_piece(key_pre, k_gain, cosine, sine_table).astype(BF)
    group = query_rot.shape[1]
    query_stack = query_rot.reshape(inner, length, group, head_dim)
    key_stack = key_rot.reshape(inner, length, head_dim)
    value_stack = value_low.reshape(inner, length, head_dim)
    attended, log_norm = lax.map(partial(attend, scale=scale), (query_stack, key_stack, value_stack, allowed))
    mixed = attended.reshape(inner * length, group * head_dim)
    middle = hidden_in.astype(F32) + scatter_pieces(nt(mixed, out_t), ranks)
    my_gain_one = lax.dynamic_slice_in_dim(gain_one, m_index * width_part, width_part, 0)
    my_gain_two = lax.dynamic_slice_in_dim(gain_two, m_index * width_part, width_part, 0)
    r_two = lax.rsqrt(lax.psum(jnp.sum(middle * middle, axis=-1, keepdims=True), "m") / width + EPS)
    normed_two = gather_pieces((middle * r_two * my_gain_two).astype(BF), ranks)

    gate_pre, up_pre = nn(normed_two, gate_cols), nn(normed_two, up_cols)
    d_inner = nn(grad_full, down_t)
    sigmoid_gate = jax.nn.sigmoid(gate_pre)
    inner_act = (gate_pre * sigmoid_gate * up_pre).astype(BF)
    d_gate_pre = (d_inner * up_pre * sigmoid_gate * (1.0 + gate_pre * (1.0 - sigmoid_gate))).astype(BF)
    d_up_pre = (d_inner * gate_pre * sigmoid_gate).astype(BF)
    d_normed_two = scatter_pieces(nt(d_gate_pre, gate_cols) + nt(d_up_pre, up_cols), ranks)
    mlp_out = scatter_pieces(nt(inner_act, down_t), ranks)
    block_out = (middle + mlp_out).astype(BF)

    scaled = d_normed_two * my_gain_two
    dot_two = lax.psum(jnp.sum(scaled * middle, axis=-1, keepdims=True), "m") / width
    d_gain_two = jnp.sum(d_normed_two * middle * r_two, axis=0)
    d_middle = cotangent.astype(F32) + r_two * scaled - middle * (r_two * r_two * r_two) * dot_two
    d_middle_low = gather_pieces(d_middle.astype(BF), ranks)
    d_gate = grad_rows(tn(normed_two, d_gate_pre), inner)
    d_up = grad_rows(tn(normed_two, d_up_pre), inner)
    d_down = grad_rows(tn(grad_full, inner_act), inner).T

    d_mixed = nn(d_middle_low, out_t).astype(BF)
    d_out_part = tn(d_middle_low, mixed)
    d_mixed_stack = d_mixed.reshape(inner, length, group, head_dim)
    d_query_stack, d_key_stack, d_value_stack = lax.map(
        partial(attend_grad, scale=scale),
        (query_stack, key_stack, value_stack, d_mixed_stack, log_norm, allowed),
    )
    rotary_piece = partial(head_piece, cosine=cosine, sine_table=sine_table)
    _, query_pull = jax.vjp(rotary_piece, query_pre, q_gain)
    d_query_pre, d_qgain_part = query_pull(d_query_stack.reshape(inner * length, group, head_dim))
    _, key_pull = jax.vjp(rotary_piece, key_pre, k_gain)
    d_key_pre, d_kgain_part = key_pull(d_key_stack.reshape(inner * length, 1, head_dim))
    d_heads = jnp.concatenate(
        [d_query_pre, d_key_pre, d_value_stack.reshape(inner * length, head_dim)], 1
    ).astype(BF)
    heads_cols = attn_cols[:, : edges[3]]
    d_normed_one = scatter_pieces(nt(d_heads, heads_cols), ranks)
    d_attn = jnp.concatenate([tn(normed_one, d_heads), d_out_part], 1)
    d_attn = grad_rows(d_attn, inner).reshape(-1, inner, edges[4])
    d_query, d_key, d_value, d_out_t = [
        d_attn[:, :, edges[n]:edges[n + 1]].reshape(d_attn.shape[0], -1) for n in range(4)
    ]
    mine = hidden_in.astype(F32)
    i_index = lax.axis_index("i")
    r_own = lax.dynamic_slice_in_dim(r_one, i_index * length, length, 0)
    scaled = d_normed_one * my_gain_one
    dot_one = lax.psum(jnp.sum(scaled * mine, axis=-1, keepdims=True), "m") / width
    d_gain_one = jnp.sum(d_normed_one * mine * r_own, axis=0)
    d_input = d_middle + r_own * scaled - mine * (r_own * r_own * r_own) * dot_one

    both = jnp.stack([d_gain_one, d_gain_two], 0)
    wide = lax.dynamic_update_slice(jnp.zeros((2, width), F32), both, (0, m_index * width_part))
    small = jnp.concatenate([wide.reshape(-1), d_qgain_part, d_kgain_part])
    small = lax.psum(small, ALL)
    wide = small[: 2 * width].reshape(2, width)
    shard = attn_gain.shape[0]
    own = lax.dynamic_slice(wide, (0, (t_index * inner + i_index) * shard), (2, shard))
    return (
        block_out, d_input, own[0], d_query, d_key, d_value,
        small[2 * width : 2 * width + head_dim], small[2 * width + head_dim :],
        d_out_t.T, own[1], d_gate, d_up, d_down,
    )


MESH = pl.DeviceIdType.MESH
ANY = pl.BlockSpec(memory_space=pl.ANY)
VMEM = pl.BlockSpec(memory_space=pltpu.VMEM)
SMEM = pl.BlockSpec(memory_space=pltpu.SMEM)
DMA = pltpu.SemaphoreType.DMA
LIMIT = 62 * 1024 * 1024


def flip(index, mask):
    if mask == 1:
        return index + 1 - 2 * lax.rem(index, 2)
    if mask == 2:
        return lax.rem(index + 2, 4)
    return 3 - index


def meet(peers):
    barrier = pltpu.get_barrier_semaphore()
    for peer in peers:
        pl.semaphore_signal(barrier, inc=1, device_id=peer, device_id_type=MESH)
    pl.semaphore_wait(barrier, len(peers))


def remote(src, dst, sems, k, peer):
    return pltpu.make_async_remote_copy(
        src_ref=src, dst_ref=dst, send_sem=sems[0].at[k], recv_sem=sems[1].at[k],
        device_id=peer, device_id_type=MESH,
    )


def at(start, size):
    return pl.ds(pl.multiple_of(start, size), size)


def tp_peers(i, m):
    return {"i": flip(i, 1)}, {"m": 1 - m}, {"i": flip(i, 2)}


class TpGather:
    def __init__(self, piece, full, sems, base, i, m):
        rows, cols = piece.shape
        half = rows // 2
        core, across, along = tp_peers(i, m)

        def slot(a, b, part=None):
            if part is None:
                return full.at[at(a * rows, rows), at(b * cols, cols)]
            return full.at[at(a * rows + part * half, half), at(b * cols, cols)]

        def go(src, dst, k, peer):
            return remote(src, dst, sems, base + k, peer)

        mine, far = slot(i, m), flip(i, 2)
        self.local = pltpu.make_async_copy(piece, mine, sems[2].at[base // 8])
        self.copies = [
            go(piece, mine, 0, core),
            go(piece, mine, 1, across),
            go(piece, mine, 2, along),
            go(slot(i, 1 - m, 0), slot(i, 1 - m, 0), 3, along),
            go(slot(i, 1 - m), slot(i, 1 - m), 4, core),
            go(slot(far, m, 1), slot(far, m, 1), 5, across),
            go(slot(far, m), slot(far, m), 6, core),
            go(slot(far, 1 - m), slot(far, 1 - m), 7, core),
        ]

    def start(self):
        for k in (1, 2, 0):
            self.copies[k].start()
        self.local.start()

    def relay(self):
        self.copies[1].wait_recv()
        self.copies[3].start()
        self.copies[4].start()
        self.copies[2].wait_recv()
        self.copies[5].start()
        self.copies[6].start()

    def relay_far(self):
        self.copies[3].wait_recv()
        self.copies[5].wait_recv()
        self.copies[7].start()

    def finish(self):
        for k in (0, 4, 6, 7):
            self.copies[k].wait_recv()
        for copy in self.copies:
            copy.wait_send()
        self.local.wait()


def add_rows(target, first, second, step=64):
    rows = target.shape[0]

    @pl.loop(0, rows, step=step)
    def _(r):
        span = pl.ds(pl.multiple_of(r, step), step)
        total = first[span, :].astype(F32) + second[span, :].astype(F32)
        target[span, :] = total.astype(target.dtype)


def tp_reduce_scratch(rows, cols, halves):
    return [
        pltpu.VMEM((2, rows, cols * halves), BF),
        pltpu.VMEM((2, rows, cols * halves), BF),
        pltpu.VMEM((2, rows // 2, cols), BF),
        pltpu.VMEM((rows // 2, cols * halves), BF),
        pltpu.VMEM((2, rows // 2, cols), BF),
        DMA((7,)), DMA((7,)), DMA((2,)),
    ]


class TpReduce:
    def __init__(self, parts, out, scratch, i, m):
        own, mate, by_x, by_y, last, send, recv, load = scratch
        rows, cols = out.shape
        half = rows // 2
        core, across, along = tp_peers(i, m)
        sems = (send, recv)
        self.args = (own, mate, by_x, by_y, last, out, m, rows, cols, half)

        def seq(a):
            return parts.at[at(a * rows, rows), :]

        self.loads = [
            pltpu.make_async_copy(seq(flip(i, 2)), own.at[1], load.at[1]),
            pltpu.make_async_copy(seq(i), own.at[0], load.at[0]),
        ]
        theirs = at((1 - m) * cols, cols)
        ours = at(m * cols, cols)
        low, high = pl.ds(0, half), pl.ds(half, half)
        self.copies = [
            remote(seq(flip(i, 3)), mate.at[1], sems, 0, core),
            remote(seq(flip(i, 1)), mate.at[0], sems, 1, core),
            remote(own.at[1, low, theirs], by_x.at[1], sems, 2, across),
            remote(own.at[0, low, theirs], by_x.at[0], sems, 3, across),
            remote(own.at[1, high, :], by_y, sems, 4, along),
            remote(own.at[1, low, ours], last.at[0], sems, 5, along),
            remote(own.at[0, high, theirs], last.at[1], sems, 6, across),
        ]
        self.ours = ours

    def start(self):
        for k in (0, 1):
            self.copies[k].start()
            self.loads[k].start()

    def run(self):
        own, mate, by_x, by_y, last, out, m, rows, cols, half = self.args
        copies, ours = self.copies, self.ours
        low, high = pl.ds(0, half), pl.ds(half, half)
        for side, k in ((1, 0), (0, 1)):
            self.loads[k].wait()
            copies[k].wait_recv()
            add_rows(own.at[side], own.at[side], mate.at[side])
            if side == 1:
                copies[2].start()
                copies[4].start()
            else:
                copies[3].start()
        copies[2].wait_recv()
        add_rows(own.at[1, low, ours], own.at[1, low, ours], by_x.at[1])
        copies[5].start()
        copies[4].wait_recv()
        add_rows(own.at[0, high, :], own.at[0, high, :], by_y)
        copies[6].start()
        copies[3].wait_recv()
        add_rows(own.at[0, low, ours], own.at[0, low, ours], by_x.at[0])
        copies[5].wait_recv()
        add_rows(out.at[low, :], own.at[0, low, ours], last.at[0])
        copies[6].wait_recv()
        add_rows(out.at[high, :], own.at[0, high, ours], last.at[1])
        for copy in copies:
            copy.wait_send()


def tp_fold_scratch(rows, cols, halves):
    return [
        pltpu.VMEM((2, rows, cols * halves), BF),
        pltpu.VMEM((2, rows // 2, cols), BF),
        pltpu.VMEM((rows // 2, cols * halves), BF),
        pltpu.VMEM((2, rows // 2, cols), BF),
        DMA((7,)), DMA((7,)),
    ]


class TpFold:
    def __init__(self, parts, out, scratch, i, m):
        mate, by_x, by_y, last, send, recv = scratch
        rows, cols = out.shape
        half = rows // 2
        core, across, along = tp_peers(i, m)
        sems = (send, recv)
        mate, by_x, last = [[v[k] if isinstance(v, list) else v.at[k] for k in range(2)] for v in (mate, by_x, last)]

        def seq(a):
            return parts.at[at(a * rows, rows), :]

        def piece(a, part, b):
            return parts.at[at(a * rows + part * half, half), at(b * cols, cols)]

        far = flip(i, 2)
        self.mine = [seq(i), seq(far)]
        self.copies = [
            remote(seq(flip(i, 3)), mate[1], sems, 0, core),
            remote(seq(flip(i, 1)), mate[0], sems, 1, core),
            remote(piece(far, 0, 1 - m), by_x[1], sems, 2, across),
            remote(piece(i, 0, 1 - m), by_x[0], sems, 3, across),
            remote(parts.at[at(far * rows + half, half), :], by_y, sems, 4, along),
            remote(piece(far, 0, m), last[0], sems, 5, along),
            remote(piece(i, 1, 1 - m), last[1], sems, 6, across),
        ]
        self.low_far, self.low, self.high = piece(far, 0, m), piece(i, 0, m), piece(i, 1, m)
        self.high_all = parts.at[at(i * rows + half, half), :]
        self.mate, self.by_x, self.by_y, self.last, self.out, self.half = mate, by_x, by_y, last, out, half

    def send(self, k):
        self.copies[k].start()

    def side(self, k):
        self.copies[1 - k].wait_recv()
        add_rows(self.mine[k], self.mine[k], self.mate[k])
        for n in ((2, 4) if k == 1 else (3,)):
            self.copies[n].start()

    def finish(self, meanwhile=None):
        copies, half = self.copies, self.half
        copies[2].wait_recv()
        add_rows(self.low_far, self.low_far, self.by_x[1])
        copies[5].start()
        copies[4].wait_recv()
        add_rows(self.high_all, self.high_all, self.by_y)
        copies[6].start()
        if meanwhile is not None:
            meanwhile()
        copies[3].wait_recv()
        add_rows(self.low, self.low, self.by_x[0])
        copies[5].wait_recv()
        add_rows(self.out.at[pl.ds(0, half), :], self.low, self.last[0])
        copies[6].wait_recv()
        add_rows(self.out.at[pl.ds(half, half), :], self.high, self.last[1])

    def wait_sends(self):
        for copy in self.copies:
            copy.wait_send()


def pick(step, i):
    return jnp.where(step == 0, flip(i, 3), jnp.where(step == 1, flip(i, 1), jnp.where(step == 2, flip(i, 2), i)))


class LineGather:
    def __init__(self, own, full, sems, base, groups, t):
        self.own, self.full, self.sems, self.base, self.groups, self.t = own, full, sems, base, groups, t
        self.rows = full.shape[0] // groups

    def block(self, b):
        return self.full.at[at(b * self.rows, self.rows), :]

    def go(self, b, k, step, own=False):
        n = self.base + (0 if step > 0 else self.groups - 1) + k
        src = self.own if own else self.block(b)
        return remote(src, self.block(b), self.sems, n, {"t": self.t + step})

    def send(self, k):
        t, last = self.t, self.groups - 1

        @pl.when((t < last) & (t - k >= 0))
        def _():
            self.go(t - k, k, 1, k == 0).start()

        @pl.when((t > 0) & (t + k <= last))
        def _():
            self.go(t + k, k, -1, k == 0).start()

    def arrive(self, k):
        t, last = self.t, self.groups - 1

        @pl.when(t - k - 1 >= 0)
        def _():
            self.go(t - k - 1, k, 1).wait_recv()

        @pl.when(t + k + 1 <= last)
        def _():
            self.go(t + k + 1, k, -1).wait_recv()

    def pass_on(self, k):
        self.arrive(k - 1)
        if k < self.groups - 1:
            self.send(k)

    def wait_sends(self):
        t, last = self.t, self.groups - 1
        for k in range(self.groups - 1):
            @pl.when((t < last) & (t - k >= 0))
            def _():
                self.go(t - k, k, 1, k == 0).wait_send()

            @pl.when((t > 0) & (t + k <= last))
            def _():
                self.go(t + k, k, -1, k == 0).wait_send()


class LineReduce:
    def __init__(self, grads, ups, downs, back, stage, spare, load, sems, base, move_sems, t, i, before):
        self.grads, self.ups, self.downs, self.back, self.stage, self.spare = grads, ups, downs, back, stage, spare
        self.load, self.sems, self.base, self.move_sems = load, sems, base, move_sems
        self.t, self.i, self.before = t, i, before

    def up(self, k, src):
        return remote(src, self.ups.at[k], self.sems, self.base + k, {"t": self.t + 1})

    def down(self, k, src):
        return remote(src, self.downs.at[k], self.sems, self.base + 3 + k, {"t": self.t - 1})

    def first(self, b):
        if b > 0:
            @pl.when(self.t == 0)
            def _():
                self.up(3 - b, self.grads.at[b]).start()
        if b < 3:
            @pl.when(self.t == 3)
            def _():
                self.down(b, self.grads.at[b]).start()

    def total(self, place, sources):
        loads = [pltpu.make_async_copy(sources[0], self.stage.at[place], self.load.at[0])]
        loads += [pltpu.make_async_copy(v, self.spare, self.load.at[1]) for v in sources[1:]]
        loads[0].start()
        loads[1].start()
        loads[0].wait()
        for n, copy in enumerate(loads[1:]):
            if n > 0:
                copy.start()
            copy.wait()
            add_rows(self.stage.at[place], self.stage.at[place], self.spare)

    def relay(self, place, way, k):
        make = self.up if way == "up" else self.down
        slots = self.ups if way == "up" else self.downs
        make(k, slots.at[k]).wait_recv()
        self.total(place, [slots.at[k], self.grads.at[3 - k if way == "up" else k]])
        make(k, self.stage.at[place]).start()

    def relayed(self, place, way, k):
        (self.up if way == "up" else self.down)(k, self.stage.at[place]).wait_send()

    PLAN = {1: ((0, "up", 0), (1, "up", 1), (2, "down", 0)), 2: ((0, "down", 0), (1, "up", 0), (2, "down", 1))}

    def hop(self, places):
        for t, plan in self.PLAN.items():
            @pl.when(self.t == t)
            def _():
                for place, way, k in plan:
                    if place in places:
                        if self.before is not None:
                            self.before.relayed(place, way, k)
                        self.relay(place, way, k)

    def moves(self):
        lanes = self.stage.shape[2] // 4
        found = []
        for j in (2, 3, 1):
            p = flip(self.i, j)
            view = self.stage.at[3, :, at(p * lanes, lanes)]
            found.append(remote(view, self.back.at[self.i], self.move_sems, self.base // 6 * 4 + j, {"i": p}))
        view = self.stage.at[3, :, at(self.i * lanes, lanes)]
        return found, pltpu.make_async_copy(view, self.back.at[self.i], self.load.at[2])

    def close(self):
        if self.before is not None:
            self.before.closed()
        for t in range(4):
            @pl.when(self.t == t)
            def _():
                sources = [self.grads.at[t]]
                if t > 0:
                    self.up(3 - t, self.ups.at[3 - t]).wait_recv()
                    sources.append(self.ups.at[3 - t])
                if t < 3:
                    self.down(t, self.downs.at[t]).wait_recv()
                    sources.append(self.downs.at[t])
                self.total(3, sources)

        found, keep = self.moves()
        for move in found:
            move.start()
        keep.start()

    def closed(self):
        found, keep = self.moves()
        for move in found:
            move.wait()
        keep.wait()

    def wait_firsts(self):
        @pl.when(self.t == 0)
        def _():
            for k in range(3):
                self.up(k, self.grads.at[3 - k]).wait_send()

        @pl.when(self.t == 3)
        def _():
            for k in range(3):
                self.down(k, self.grads.at[k]).wait_send()

    def wait_relays(self):
        for t, plan in self.PLAN.items():
            @pl.when(self.t == t)
            def _():
                for place, way, k in plan:
                    self.relayed(place, way, k)


def tp_group(i, m):
    return list(tp_peers(i, m))


def row_loop(rows, step=64):
    def wrap(f):
        @pl.loop(0, rows, step=step)
        def _(r):
            f(pl.ds(pl.multiple_of(r, step), step))

    return wrap


def mlp_kernel(groups, piece_in, grad_full, first_w, other_w, middle, stat, cot, gain,
               rest_w, grads, ups, downs, back, out_parts, d_middle, d_gain, piece, *scratch):
    (x, g, w, act, act_t, fresh, stage, spare, sums, other, load, g_send, g_recv, g_local, z_send, z_recv,
     r_send, r_recv, m_send, m_recv, f_send, f_recv, s_send, s_recv, free) = scratch
    t, i, m = lax.axis_index("t"), lax.axis_index("i"), lax.axis_index("m")
    others = [{"i": flip(i, j)} for j in (1, 2, 3)]
    meet(others + [{"m": 1 - m}] + [{"t": flip(t, j)} for j in (1, 2, 3)])
    tokens, wide = x.shape
    rows, part = middle.shape
    unit = w.shape[2] // 3
    two, three = 2 * unit, 3 * unit
    block = wide // groups
    gather = TpGather(piece_in, x, (g_send, g_recv, g_local), 0, i, m)
    gather.start()
    lines = [LineGather(other_w.at[c], rest_w.at[c], (z_send, z_recv), 6 * c, groups, t) for c in range(2)]
    lines[0].send(0)
    take_g = pltpu.make_async_copy(grad_full, g, load.at[3])
    take_w = [pltpu.make_async_copy(first_w.at[c], w.at[c], load.at[4 + c]) for c in range(2)]
    own = [
        pltpu.make_async_copy(other_w.at[c], rest_w.at[c, at(t * block, block), :], load.at[6 + c]) for c in range(2)
    ]
    rest = [pltpu.make_async_copy(rest_w.at[c], w.at[2 + c], load.at[8 + c]) for c in range(2)]
    for copy in [take_w[0], take_g, take_w[1]] + own:
        copy.start()
    gather.relay()
    lines[0].pass_on(1)
    gather.relay_far()
    lines[0].pass_on(2)
    lines[1].send(0)
    for copy in [take_w[0], take_g, take_w[1]] + own:
        copy.wait()
    gather.finish()
    reds = []
    for c in range(3):
        reds.append(LineReduce(
            grads.at[c], ups.at[c], downs.at[c], back.at[c], stage, spare, load, (r_send, r_recv), 6 * c,
            (m_send, m_recv), t, i, reds[-1] if reds else None))
    order = (3, 0, 2, 1)
    events = {
        (0, 3): lambda: (lines[0].pass_on(3), rest[0].start()),
        (1, 0): lambda: lines[1].pass_on(1),
        (1, 3): lambda: reds[0].hop((0,)),
        (1, 5): lambda: lines[1].pass_on(2),
        (2, 0): lambda: reds[0].hop((1, 2)),
        (2, 1): lambda: (lines[1].pass_on(3), rest[1].start()),
        (2, 5): lambda: reds[0].close(),
        (3, 0): lambda: reds[1].hop((0,)),
        (3, 5): lambda: reds[1].hop((1, 2)),
    }

    def hook(c, slot):
        for (when_c, when_slot), run in events.items():
            if when_slot == slot:
                @pl.when(c == when_c)
                def _():
                    run()

    def stored(c, n):
        return pltpu.make_async_copy(fresh.at[n % 2], grads.at[c, order[n]], load.at[10 + n % 2])

    @pl.loop(0, 4)
    def _(c):
        for n in range(2):
            @pl.when(c == 2 + n)
            def _():
                rest[n].wait()

        for n in range(4):
            span = pl.ds(n * rows, rows)
            d_inner = nn(g[span, :], w[c, :, two:three])
            both = nn(x[span, :], w[c, :, 0:two])
            gate, up = both[:, :unit], both[:, unit:]
            sig = jax.nn.sigmoid(gate)
            silu = gate * sig
            d_gate = (d_inner * up * sig * (1.0 + gate * (1.0 - sig))).astype(BF)
            d_up = (d_inner * silu).astype(BF)
            inner = (silu * up).astype(BF)
            for k, v in enumerate((d_gate, d_up, inner)):
                act[c, span, k * unit:(k + 1) * unit] = v
                act_t[k * unit:(k + 1) * unit, span] = v.T
            hook(c, n)
        for n in range(4):
            cols = pl.ds(order[n] * block, block)
            fresh[n % 2, 0:two, :] = nn(act_t[0:two, :], x[:, cols]).astype(BF)
            fresh[n % 2, two:three, :] = nn(act_t[two:three, :], g[:, cols]).astype(BF)
            stored(c, n).start()
            for done in ((n - 1,) if n < 3 else (2, 3)):
                if done >= 0:
                    stored(c, done).wait()
                    for q in range(3):
                        @pl.when(c == q)
                        def _():
                            reds[q].first(order[done])
            hook(c, 4 + n)

    for peer in tp_group(i, m):
        pl.semaphore_signal(free, inc=1, device_id=peer, device_id_type=MESH)
    quarter, half = rows // 2, part
    base = 2 * rows
    lists = [
        [g.at[pl.ds(0, rows), :], g.at[pl.ds(rows, rows), :]],
        [g.at[pl.ds(base, quarter), pl.ds(k * half, half)] for k in range(2)],
        g.at[pl.ds(base + quarter, quarter), :],
        [g.at[pl.ds(base + 2 * quarter, quarter), pl.ds(k * half, half)] for k in range(2)],
    ]
    fold = TpFold(x, d_middle, lists + [f_send, f_recv], i, m)

    def product(span, cols, low, high):
        total = nt(act[0, span, low:high], w[0, cols, low:high])
        for c in range(1, 4):
            total += nt(act[c, span, low:high], w[c, cols, low:high])
        return total.astype(BF)

    def tiles(f):
        @pl.loop(0, wide, step=512)
        def _(col):
            f(pl.ds(pl.multiple_of(col, 512), 512))

    @pl.loop(0, 4)
    def _(step):
        span = at(pick(step, i) * rows, rows)

        @tiles
        def _(cols):
            x[span, cols] = product(span, cols, 0, two)

        @pl.when(step == 0)
        def _():
            pl.semaphore_wait(free, 3)
            fold.send(0)

        @pl.when(step == 1)
        def _():
            fold.send(1)
            reds[1].close()

        @pl.when(step == 2)
        def _():
            fold.side(1)

    fold.side(0)
    reds[2].hop((0,))

    def project(first):
        @pl.loop(first, first + 2)
        def _(s):
            span = at(s * rows, rows)

            @tiles
            def _(cols):
                act_t[0:rows, cols] = product(span, cols, two, three)

            put = pltpu.make_async_copy(act_t.at[pl.ds(0, rows), :], out_parts.at[span, :], load.at[10])
            put.start()
            put.wait()

    project(0)
    fold.finish(lambda: project(2))
    d_gain[...] = jnp.zeros_like(d_gain)
    reds[2].hop((1, 2))

    @row_loop(rows)
    def _(span):
        dn, v, r = d_middle[span, :], middle[span, :], stat[span, :]
        sums[span, :] = jnp.broadcast_to(jnp.sum(dn * gain[...] * v, axis=-1, keepdims=True), r.shape)
        d_gain[0:1, :] += jnp.sum(dn * v * r[:, :1], axis=0, keepdims=True)

    swap = remote(sums, other, (s_send, s_recv), 0, {"m": 1 - m})
    swap.start()
    swap.wait()

    @row_loop(rows)
    def _(span):
        r = stat[span, :]
        factor = (r * r * r * ((sums[span, :] + other[span, :]) / wide))[:, :1]
        d = cot[span, :].astype(F32) + r[:, :1] * (d_middle[span, :] * gain[...]) - middle[span, :] * factor
        d_middle[span, :] = d
        piece[span, :] = d.astype(BF)

    fold.wait_sends()
    for line in lines:
        line.wait_sends()
    reds[2].close()
    for red in reds:
        red.wait_firsts()
    reds[2].wait_relays()
    reds[2].closed()


def shape(dims, dtype):
    return jax.ShapeDtypeStruct(dims, dtype)


def comm_call(kernel, ins, outs, scratch, number):
    return pl.pallas_call(
        kernel,
        out_shape=[s for s, _ in outs],
        in_specs=ins,
        out_specs=[b for _, b in outs],
        scratch_shapes=scratch,
        compiler_params=pltpu.CompilerParams(
            collective_id=number, has_side_effects=True, vmem_limit_bytes=LIMIT
        ),
    )


def allow(cut, q0, qn, kn):
    q = q0 + lax.broadcasted_iota(jnp.int32, (qn, kn), 0)
    k = lax.broadcasted_iota(jnp.int32, (qn, kn), 1)
    doc_q = (q >= cut[0]).astype(jnp.int32) + (q >= cut[1]).astype(jnp.int32)
    doc_k = (k >= cut[0]).astype(jnp.int32) + (k >= cut[1]).astype(jnp.int32)
    return (doc_q == doc_k) & (k <= q)


def turn(v):
    half = v.shape[1] // 2
    return jnp.concatenate([-v[:, half:], v[:, :half]], axis=1)


def turn_back(v):
    half = v.shape[1] // 2
    return jnp.concatenate([v[:, half:], -v[:, :half]], axis=1)


def fore_kernel(groups, heads, hd, cuts, pack, gate, up, down, hidden, cot, qk_gain, table,
                attn, first_w, other_w, normed_out, pre, qkv, stats, mixed, middle, stat, piece, grad_full, gain_rows,
                *scratch):
    fold_scratch, (full, weights, other, load, w_send, w_recv, w_local, z_send, z_recv,
                   g_send, g_recv, g_local, s_send, s_recv) = scratch[:6], scratch[6:]
    x = full
    t, i, m = lax.axis_index("t"), lax.axis_index("i"), lax.axis_index("m")
    rows, wide = hidden.shape[0], x.shape[1]
    nq, kv = heads * hd, (heads + 2) * hd
    shard = pack.shape[1]
    unit = first_w.shape[2] // 3
    others = [{"i": flip(i, j)} for j in (1, 2, 3)]
    meet(others + [{"m": 1 - m}] + [{"t": flip(t, j)} for j in (1, 2, 3)])
    mine = attn.at[at((t * 4 + i) * shard, shard), :]
    spread = [remote(pack.at[flip(i, j)], mine, (w_send, w_recv), j - 1, others[j - 1]) for j in (2, 3, 1)]
    own = pltpu.make_async_copy(pack.at[i], mine, w_local.at[0])
    for copy in spread:
        copy.start()
    own.start()
    gather_h = TpGather(hidden, full, (g_send, g_recv, g_local), 0, i, m)
    gather_g = TpGather(cot, grad_full, (g_send, g_recv, g_local), 8, i, m)
    gather_h.start()

    def chunk(c):
        if c < 2:
            place = first_w.at[c, at((t * 4 + i) * shard, shard), :]
        else:
            place = other_w.at[c - 2, at(i * shard, shard), :]
        found, kept = [], []
        for n, src in enumerate((gate, up, down)):
            dst = place.at[:, pl.ds(n * unit, unit)]

            def view(p):
                return src.at[:, at(p * 4 * unit + c * unit, unit)]

            for j in (2, 3, 1):
                found.append(remote(view(flip(i, j)), dst, (w_send, w_recv), 3 + 9 * c + 3 * n + j - 1, others[j - 1]))
            kept.append(pltpu.make_async_copy(view(i), dst, w_local.at[1 + 3 * c + n]))
        return found, kept

    chunks = [chunk(c) for c in range(4)]

    def begin(c):
        for copy in chunks[c][0] + chunks[c][1]:
            copy.start()

    def landed(c):
        for copy in chunks[c][0]:
            copy.wait_recv()
        for copy in chunks[c][1]:
            copy.wait()

    sems = (z_send, z_recv)
    block = 4 * shard
    line = LineGather(attn.at[at(t * block, block), :], attn, sems, 0, groups, t)
    lines = [
        LineGather(first_w.at[c, at(t * block, block), :], first_w.at[c], sems, 6 * c + 6, groups, t) for c in range(2)
    ]
    own.wait()
    for copy in spread:
        copy.wait_recv()
    line.send(0)
    begin(0)
    line.pass_on(1)
    gather_h.relay()
    begin(1)
    line.pass_on(2)
    gather_h.relay_far()
    gather_g.start()
    begin(2)
    begin(3)
    landed(0)
    lines[0].send(0)
    line.pass_on(3)
    landed(1)
    lines[1].send(0)
    fill = pltpu.make_async_copy(attn, weights, load.at[0])
    fill.start()
    gather_h.finish()
    fill.wait()
    gain_rows[...] = jnp.transpose(weights[:, kv + nq:kv + nq + 128].astype(F32))[0:8, :]
    gain = gain_rows[0:1, :]
    gain_two = gain_rows[1:2, at(m * (wide // 2), wide // 2)]
    parts = full
    fold = TpFold(parts, middle, fold_scratch, i, m)

    @pl.loop(0, 4)
    def _(step):
        s = pick(step, i)
        start = s * rows
        def sub(r, size):
            return pl.ds(pl.multiple_of(start + r, size), size)

        cut = (cuts[s, 0], cuts[s, 1])

        @pl.loop(0, rows, step=64)
        def _(r):
            span = sub(r, 64)
            v = x[span, :].astype(F32)
            scale = lax.rsqrt(jnp.mean(v * v, axis=-1, keepdims=True) + EPS)
            stats[span, :] = jnp.broadcast_to(scale, (64, stats.shape[1]))
            x[span, :] = (v * scale * gain_rows[0:1, :]).astype(BF)

        everything = sub(0, rows)
        keep = pltpu.make_async_copy(x.at[everything, :], normed_out.at[everything, :], load.at[1])
        keep.start()
        heads_pre = nn(x[everything, :], weights[:, :kv])
        pre[everything, :] = heads_pre
        c, sn = table[everything, 0:hd], table[everything, hd:2 * hd]
        for h in range(heads + 1):
            lanes = slice(h * hd, (h + 1) * hd)
            n = rms_rows(heads_pre[:, lanes], qk_gain[0:1, :] if h < heads else qk_gain[1:2, :])
            qkv[everything, lanes] = (n * c + turn(n) * sn).astype(BF)
        qkv[everything, nq + hd:kv] = heads_pre[:, nq + hd:kv].astype(BF)
        half = rows // 2
        for b in range(2):
            kn = (b + 1) * half
            span = sub(b * half, half)
            mask = allow(cut, b * half, half, kn)
            keys, values = qkv[pl.ds(start, kn), nq:nq + hd], qkv[pl.ds(start, kn), nq + hd:kv]
            for h in range(heads):
                q = qkv[span, h * hd:(h + 1) * hd]
                scores = jnp.where(mask, nt(q, keys) * (hd ** -0.5), -1e30)
                top = jnp.max(scores, axis=-1, keepdims=True)
                e = jnp.exp(scores - top)
                total = jnp.sum(e, axis=-1, keepdims=True)
                probs = (e * (1.0 / total)).astype(BF)
                stats[span, h:h + 1] = top + jnp.log(total)
                mixed[span, h * hd:(h + 1) * hd] = nn(probs, values).astype(BF)

        keep.wait()

        @pl.loop(0, wide, step=512)
        def _(col):
            cols = pl.ds(pl.multiple_of(col, 512), 512)
            parts[everything, cols] = nt(mixed[everything, :], weights[cols, kv:kv + nq]).astype(BF)

        @pl.when(step == 0)
        def _():
            fold.send(0)
            gather_g.relay()

        @pl.when(step == 1)
        def _():
            fold.send(1)
            gather_g.relay_far()
            lines[0].pass_on(1)

        @pl.when(step == 2)
        def _():
            fold.side(1)
            lines[1].pass_on(1)

    fold.side(0)
    lines[0].pass_on(2)
    fold.finish(lambda: lines[1].pass_on(2))

    @row_loop(rows)
    def _(span):
        v = middle[span, :] + hidden[span, :].astype(F32)
        middle[span, :] = v
        stat[span, :] = jnp.broadcast_to(jnp.sum(v * v, axis=-1, keepdims=True), stat[span, :].shape)

    swap = remote(stat, other, (s_send, s_recv), 0, {"m": 1 - m})
    swap.start()
    swap.wait()

    @row_loop(rows)
    def _(span):
        r = lax.rsqrt((stat[span, :] + other[span, :]) / wide + EPS)
        stat[span, :] = r
        piece[span, :] = (middle[span, :] * r[:, :1] * gain_two).astype(BF)

    gather_g.finish()
    fold.wait_sends()
    for c in range(4):
        if c >= 2:
            landed(c)
        for copy in chunks[c][0]:
            copy.wait_send()
    for copy in spread:
        copy.wait_send()
    for one in lines:
        one.pass_on(3)
    for one in [line] + lines:
        one.wait_sends()


def aft_kernel(groups, heads, hd, cuts, piece, normed, out_parts, attn, pre_in, middle, d_middle, qkv_in, stats_in,
               mixed_in, table_in, mlp_grads, qk_gain, hidden, gain, d_gain_two,
               d_input, block_out, back, gains, ups, downs, mlp_back, *scratch):
    fold_scratch, out_scratch = scratch[:6], scratch[6:14]
    (dm, nrm, pre, qkv, stats, mixed, table, weights, res, acc, grads, up_in, down_in, total, d_mix, d_pre, d_kv, qk_sum, sums, other,
     g_in, load, a_send, a_recv, a_local, send, recv, z_send, z_recv, g_send, g_recv, s_send, s_recv,
     local, stage, spare, line_load, r_send, r_recv, m_send, m_recv) = scratch[14:]
    t, i, m = lax.axis_index("t"), lax.axis_index("i"), lax.axis_index("m")
    others = [{"i": flip(i, j)} for j in (1, 2, 3)]
    meet(others + [{"m": 1 - m}] + [{"t": flip(t, j)} for j in (1, 2, 3)])
    rows, wide = hidden.shape[0], dm.shape[1]
    nq, kv = heads * hd, (heads + 2) * hd
    scale = hd ** -0.5
    gather = TpGather(piece, dm, (a_send, a_recv, a_local), 0, i, m)
    gather.start()
    red = LineReduce(mlp_grads.at[3], ups, downs, mlp_back, stage, spare, line_load, (r_send, r_recv), 0,
                     (m_send, m_recv), t, i, None)
    for b in (3, 0, 2, 1):
        red.first(b)
    fill = pltpu.make_async_copy(attn.at[:, pl.ds(0, kv + nq)], weights, load.at[2])
    fill.start()

    def fetch(step):
        span = at(pick(step, i) * rows, rows)
        return (pltpu.make_async_copy(normed.at[span, :], nrm, load.at[0]),
                *[pltpu.make_async_copy(src.at[span, :], dst, load.at[n]) for n, src, dst in (
                    (1, pre_in, pre), (4, qkv_in, qkv), (5, stats_in, stats), (6, mixed_in, mixed),
                    (7, table_in, table))])

    take = pltpu.make_async_copy(middle, d_input, load.at[3])
    take.start()
    two = TpReduce(out_parts, res, out_scratch, i, m)
    acc[...] = jnp.zeros_like(acc)
    qk_sum[...] = jnp.zeros_like(qk_sum)
    fold = TpFold(dm, d_input, fold_scratch, i, m)
    fill.wait()
    gather.relay()
    red.hop((0,))
    gather.relay_far()
    two.start()
    red.hop((1, 2))
    gather.finish()

    @pl.loop(0, 4)
    def _(step):
        s = pick(step, i)
        start = s * rows
        for copy in fetch(step):
            copy.start()

        def sub(r, size):
            return pl.ds(pl.multiple_of(start + r, size), size)

        cut = (cuts[s, 0], cuts[s, 1])
        everything = sub(0, rows)
        d_mix[...] = nn(dm[everything, :], weights[:, kv:kv + nq]).astype(BF)
        d_kv[...] = jnp.zeros_like(d_kv)
        half = rows // 2

        def undo(h, grad):
            lanes = slice(h * hd, (h + 1) * hd)
            row = 0 if h < heads else 1
            c, sn = table[:, 0:hd], table[:, hd:2 * hd]
            u = c * grad + turn_back(sn * grad)
            v = pre[:, lanes]
            r = lax.rsqrt(jnp.mean(v * v, axis=-1, keepdims=True) + EPS)
            qk_sum[0:1, row * hd:(row + 1) * hd] += jnp.sum(u * v * r, axis=0, keepdims=True)
            scaled = u * qk_gain[row:row + 1, :]
            undone = r * scaled - v * (r * r * r) * jnp.mean(scaled * v, axis=-1, keepdims=True)
            d_pre[:, lanes] = undone.astype(BF)

        for copy in fetch(step)[1:]:
            copy.wait()
        for h in range(heads):
            lanes = slice(h * hd, (h + 1) * hd)
            found = []
            for b in range(2):
                kn = (b + 1) * half
                span = slice(b * half, kn)
                mask = allow(cut, b * half, half, kn)
                keys, values = qkv[0:kn, nq:nq + hd], qkv[0:kn, nq + hd:kv]
                q, go = qkv[span, lanes], d_mix[span, lanes]
                scores = jnp.where(mask, nt(q, keys) * scale, -1e30)
                probs = jnp.exp(scores - stats[span, h:h + 1])
                d_probs = nt(go, values)
                inner = jnp.sum(probs * d_probs, axis=-1, keepdims=True)
                d_scores = (probs * (d_probs - inner)).astype(BF)
                found.append(nn(d_scores, keys) * scale)
                d_kv[0:kn, 0:hd] += tn(d_scores, q) * scale
                d_kv[0:kn, hd:2 * hd] += tn(probs.astype(BF), go)
            undo(h, jnp.concatenate(found, axis=0))
        undo(heads, d_kv[:, 0:hd])
        d_pre[:, nq + hd:kv] = d_kv[:, hd:2 * hd].astype(BF)
        fetch(step)[0].wait()

        @pl.loop(0, wide, step=512)
        def _(col):
            cols = pl.ds(pl.multiple_of(col, 512), 512)
            acc[0:kv, cols] += tn(d_pre[...], nrm[:, cols])
            acc[kv:kv + nq, cols] += tn(mixed[...], dm[everything, cols])
            dm[everything, cols] = nt(d_pre[...], weights[cols, 0:kv]).astype(BF)

        @pl.when(step < 2)
        def _():
            @pl.when(step == 0)
            def _():
                fold.send(0)

            @pl.when(step == 1)
            def _():
                fold.send(1)

        @pl.when(step == 2)
        def _():
            fold.side(1)

        @pl.when(step == 3)
        def _():
            fold.side(0)

        @pl.when(step == 0)
        def _():
            two.run()
            take.wait()

            @row_loop(rows)
            def _(span):
                block_out[span, :] = (d_input[span, :] + res[span, :]).astype(BF)

            pltpu.make_async_copy(d_middle, res, load.at[3]).start()
            red.close()

    block = wide // groups

    @pl.loop(0, groups)
    def _(b):
        cols = at(b * block, block)
        grads[b] = acc[:, cols].astype(BF)

    def up(k, src):
        return remote(src, up_in.at[k], (z_send, z_recv), k, {"t": t + 1})

    def down(k, src):
        return remote(src, down_in.at[k], (z_send, z_recv), groups + k, {"t": t - 1})

    @pl.when(t == 0)
    def _():
        for k in range(groups - 1):
            up(k, grads.at[groups - 1 - k]).start()

    @pl.when(t == groups - 1)
    def _():
        for k in range(groups - 1):
            down(k, grads.at[k]).start()

    def hop(k):
        b = groups - 1 - k

        @pl.when((t > 0) & (b > t))
        def _():
            up(k, up_in.at[k]).wait_recv()
            add_rows(up_in.at[k], up_in.at[k], grads.at[b])
            up(k, up_in.at[k]).start()

        @pl.when((t < groups - 1) & (k < t))
        def _():
            down(k, down_in.at[k]).wait_recv()
            add_rows(down_in.at[k], down_in.at[k], grads.at[k])
            down(k, down_in.at[k]).start()

    hop(0)
    pltpu.make_async_copy(d_middle, res, load.at[3]).wait()
    fold.finish(lambda: hop(1))
    gains[...] = jnp.zeros_like(gains)
    own_half = at(m * (wide // 2), wide // 2)
    gains[1:2, own_half] = d_gain_two[0:1, :]
    gains[2:3, :] = jnp.concatenate([qk_sum[0:1, :]] * (wide // (2 * hd)), axis=1)

    @row_loop(rows)
    def _(span):
        dn, v = d_input[span, :], hidden[span, :].astype(F32)
        r = stats[span, heads:heads + 1]
        sums[span, :] = jnp.broadcast_to(jnp.sum(dn * gain[...] * v, axis=-1, keepdims=True), sums[span, :].shape)
        gains[0:1, own_half] += jnp.sum(dn * v * r, axis=0, keepdims=True)

    swap = remote(sums, other, (s_send, s_recv), 0, {"m": 1 - m})
    swap.start()
    ways = [{"i": flip(i, 1)}, {"m": 1 - m}, {"i": flip(i, 2)}, {"t": flip(t, 1)}, {"t": flip(t, 2)}]

    def trade(k):
        return remote(gains, g_in.at[k], (g_send, g_recv), k, ways[k])

    trade(0).start()
    swap.wait()

    @row_loop(rows)
    def _(span):
        r = stats[span, heads:heads + 1]
        factor = r * r * r * ((sums[span, :] + other[span, :]) / wide)[:, :1]
        d = res[span, :] + r * (d_input[span, :] * gain[...])
        d_input[span, :] = d - hidden[span, :].astype(F32) * factor

    hop(2)
    for b in range(groups):
        @pl.when(t == b)
        def _():
            own = grads.at[b]
            if b > 0:
                up(groups - 1 - b, up_in.at[0]).wait_recv()
                add_rows(total, own, up_in.at[groups - 1 - b])
                own = total
            if b < groups - 1:
                down(b, down_in.at[0]).wait_recv()
                add_rows(total, own, down_in.at[b])

    sub_cols = block // 4
    moves = []
    for j in (2, 3, 1):
        view = total.at[:, at(flip(i, j) * sub_cols, sub_cols)]
        moves.append(remote(view, back.at[i], (send, recv), j, others[j - 1]))
    keep = pltpu.make_async_copy(total.at[:, at(i * sub_cols, sub_cols)], back.at[i], local.at[0])
    for move in moves:
        move.start()
    keep.start()
    for k in range(5):
        if k > 0:
            trade(k).start()
        trade(k).wait()
        gains[...] += g_in[k]
    for k in range(groups - 1):
        @pl.when(t < groups - 1 - k)
        def _():
            up(k, up_in.at[k]).wait_send()

        @pl.when(t > k)
        def _():
            down(k, down_in.at[k]).wait_send()

    fold.wait_sends()
    red.wait_firsts()
    red.wait_relays()
    red.closed()
    keep.wait()
    for move in moves:
        move.wait()


def fast_body(
    hidden_in, doc_starts, attn_gain, w_query, w_key, w_value, query_gain, key_gain,
    w_out, mlp_gain, w_gate, w_up, w_down, cotangent, *, groups, inner, halves,
):
    length, part = hidden_in.shape
    shard = w_query.shape[0]
    width, tokens = part * halves, length * inner
    hd = query_gain.shape[0]
    heads = w_query.shape[1] // inner // hd
    nq, kv = heads * hd, (heads + 2) * hd
    hidden_units = w_gate.shape[1] // inner
    t_index, i_index, m_index = lax.axis_index("t"), lax.axis_index("i"), lax.axis_index("m")
    cuts = lax.dynamic_slice_in_dim(doc_starts, t_index * inner, inner, 0)
    cosine, sine_table, _ = jax.vmap(partial(tables, length=length, head_dim=hd))(cuts)
    table = jnp.concatenate([cosine.reshape(tokens, hd), sine_table.reshape(tokens, hd)], axis=1)
    qk_gain = jnp.zeros((8, hd), F32).at[0].set(query_gain.astype(F32)).at[1].set(key_gain.astype(F32))

    def by_rank(w):
        return jnp.moveaxis(w.reshape(shard, inner, w.shape[1] // inner), 1, 0)

    gains = jnp.zeros((shard, 128), BF).at[:, 0].set(attn_gain).at[:, 1].set(mlp_gain)
    pack = jnp.concatenate(
        [by_rank(w_query), by_rank(w_key), by_rank(w_value), by_rank(w_out.T),
         jnp.broadcast_to(gains[None], (inner, shard, 128))], 2)
    cols = pack.shape[2]
    unit = hidden_units // 4
    fold_scratch = tp_fold_scratch(length, part, halves)
    block = width // groups
    (attn_w, first_w, other_w, normed_one, pre, qkv, stats, mixed, middle, r_two, piece, grad_full, gain_rows) = comm_call(
        partial(fore_kernel, groups, heads, hd), [SMEM] + [ANY] * 4 + [VMEM, ANY, VMEM, VMEM],
        [(shape((width, cols), BF), ANY), (shape((2, width, 3 * unit), BF), ANY), (shape((2, block, 3 * unit), BF), ANY),
         (shape((tokens, width), BF), ANY), (shape((tokens, kv), F32), VMEM), (shape((tokens, kv), BF), VMEM),
         (shape((tokens, 128), F32), VMEM), (shape((tokens, nq), BF), VMEM), (shape((length, part), F32), VMEM),
         (shape((length, 128), F32), VMEM), (shape((length, part), BF), VMEM), (shape((tokens, width), BF), ANY),
         (shape((8, width), F32), VMEM)],
        fold_scratch + [
            pltpu.VMEM((tokens, width), BF), pltpu.VMEM((width, cols), BF), pltpu.VMEM((length, 128), F32), DMA((2,)),
            DMA((39,)), DMA((39,)), DMA((13,)), DMA((18,)), DMA((18,)),
            DMA((16,)), DMA((16,)), DMA((2,)), DMA((1,)), DMA((1,))], 0,
    )(cuts, pack, w_gate, w_up, w_down.T, hidden_in, cotangent, qk_gain, table)
    own_gains = lax.dynamic_slice(gain_rows, (0, m_index * part), (2, part))

    (_, mlp_grads, _, _, mlp_back, out_parts, d_middle, d_gain_two, d_low) = comm_call(
        partial(mlp_kernel, groups), [ANY] * 4 + [VMEM] * 4,
        [(shape((2, width, 3 * unit), BF), ANY), (shape((4, groups, 3 * unit, block), BF), ANY),
         (shape((3, 3, 3 * unit, block), BF), ANY), (shape((3, 3, 3 * unit, block), BF), ANY),
         (shape((3, inner, 3 * unit, shard), BF), ANY), (shape((tokens, width), BF), ANY),
         (shape((length, part), F32), VMEM), (shape((8, part), F32), VMEM), (shape((length, part), BF), VMEM)],
        [pltpu.VMEM((tokens, width), BF), pltpu.VMEM((tokens, width), BF), pltpu.VMEM((4, width, 3 * unit), BF),
         pltpu.VMEM((4, tokens, 3 * unit), BF), pltpu.VMEM((3 * unit, tokens), BF),
         pltpu.VMEM((2, 3 * unit, block), BF), pltpu.VMEM((4, 3 * unit, block), BF), pltpu.VMEM((3 * unit, block), BF),
         pltpu.VMEM((length, 128), F32), pltpu.VMEM((length, 128), F32), DMA((12,)),
         DMA((8,)), DMA((8,)), DMA((1,)), DMA((12,)), DMA((12,)), DMA((18,)), DMA((18,)), DMA((12,)), DMA((12,)),
         DMA((7,)), DMA((7,)), DMA((1,)), DMA((1,)), pltpu.SemaphoreType.REGULAR], 1,
    )(piece, grad_full, first_w, other_w, middle, r_two, cotangent, own_gains[1:2])

    d_input, block_out, attn_back, gains_out, _, _, last_back = comm_call(
        partial(aft_kernel, groups, heads, hd), [SMEM] + [ANY] * 12 + [VMEM] * 4,
        [(shape((length, part), F32), VMEM), (shape((length, part), BF), VMEM),
         (shape((inner, nq + kv, block // inner), BF), ANY), (shape((8, width), F32), VMEM),
         (shape((3, 3 * unit, block), BF), ANY), (shape((3, 3 * unit, block), BF), ANY),
         (shape((inner, 3 * unit, shard), BF), ANY)],
        fold_scratch + tp_reduce_scratch(length, part, halves) + [
            pltpu.VMEM((tokens, width), BF), pltpu.VMEM((length, width), BF), pltpu.VMEM((length, kv), F32),
            pltpu.VMEM((length, kv), BF), pltpu.VMEM((length, 128), F32), pltpu.VMEM((length, nq), BF),
            pltpu.VMEM((length, 128), F32),
            pltpu.VMEM((width, nq + kv), BF), pltpu.VMEM((length, part), F32), pltpu.VMEM((nq + kv, width), F32),
            pltpu.VMEM((groups, nq + kv, block), BF),
            pltpu.VMEM((groups - 1, nq + kv, block), BF), pltpu.VMEM((groups - 1, nq + kv, block), BF),
            pltpu.VMEM((nq + kv, block), BF), pltpu.VMEM((length, nq), BF), pltpu.VMEM((length, kv), BF),
            pltpu.VMEM((length, 2 * hd), F32), pltpu.VMEM((8, 2 * hd), F32),
            pltpu.VMEM((length, 128), F32), pltpu.VMEM((length, 128), F32), pltpu.VMEM((5, 8, width), F32),
            DMA((8,)), DMA((8,)), DMA((8,)), DMA((1,)),
            DMA((4,)), DMA((4,)), DMA((2 * groups,)), DMA((2 * groups,)), DMA((5,)), DMA((5,)),
            DMA((1,)), DMA((1,)), DMA((1,)),
            pltpu.VMEM((4, 3 * unit, block), BF), pltpu.VMEM((3 * unit, block), BF), DMA((3,)),
            DMA((6,)), DMA((6,)), DMA((4,)), DMA((4,))], 2,
    )(cuts, d_low, normed_one, out_parts, attn_w, pre, middle, d_middle, qkv, stats, mixed, table, mlp_grads,
      qk_gain, hidden_in, own_gains[0:1], d_gain_two)
    all_back = jnp.concatenate([mlp_back, last_back[None]], axis=0)

    def mlp_columns(first):
        part_of = all_back[:, :, first:first + unit, :]
        return jnp.transpose(part_of, (3, 1, 0, 2)).reshape(shard, inner * hidden_units).astype(F32)

    d_down = jnp.transpose(all_back[:, :, 2 * unit:, :], (1, 0, 2, 3)).reshape(inner * hidden_units, shard).astype(F32)
    own = lax.dynamic_slice(gains_out, (0, (t_index * inner + i_index) * shard), (2, shard))

    def columns(first, last):
        return jnp.moveaxis(attn_back[:, first:last, :], 2, 0).reshape(shard, -1).astype(F32)

    return (
        block_out, d_input, own[0], columns(0, nq), columns(nq, nq + hd), columns(nq + hd, kv),
        gains_out[2, :hd], gains_out[2, hd:2 * hd],
        attn_back[:, kv:kv + nq, :].reshape(inner * nq, shard).astype(F32), own[1],
        mlp_columns(0), mlp_columns(unit), d_down,
    )


def solution(mesh):
    dp, halves = mesh.shape["dp"], mesh.shape["mp"]
    inner = 4
    groups = dp // inner
    fine = Mesh(mesh.devices.reshape(groups, inner, halves), ("t", "i", "m"))
    rows = P(("t", "i"))
    block = P(("t", "i"), "m")
    turned = P("m", ("t", "i"))
    body = fast_body if groups == 4 and halves == 2 else plain_body
    return jax.shard_map(
        partial(body, groups=groups, inner=inner, halves=halves),
        mesh=fine,
        in_specs=(block, P(), rows, block, block, block, P(), P(), turned, rows, block, block, turned, block),
        out_specs=(block, block, rows, block, block, block, P(), P(), turned, rows, block, block, turned),
        check_vma=False,
    )
```

```python
from functools import partial
import math

import jax
import jax.numpy as jnp
from jax import lax
from jax.experimental import pallas as pl
from jax.experimental.pallas import tpu as pltpu
from jax.sharding import Mesh, PartitionSpec as P

BF = jnp.bfloat16
F32 = jnp.float32
EPS = 1e-05
TP = ("i", "m")
ALL = ("t", "i", "m")


def dot_f32(left, right, dims):
    return lax.dot_general(left, right, (dims, ((), ())), preferred_element_type=F32)


def nn(left, right):
    return dot_f32(left, right, ((1,), (0,)))


def nt(left, right):
    return dot_f32(left, right, ((1,), (1,)))


def tn(left, right):
    return dot_f32(left, right, ((0,), (0,)))


def rms_rows(v, gain):
    return v * lax.rsqrt(jnp.mean(v * v, axis=-1, keepdims=True) + EPS) * gain


def tables(cut_row, length, head_dim):
    position = jnp.arange(length, dtype=jnp.int32)
    doc = (position >= cut_row[0]).astype(jnp.int32) + (position >= cut_row[1]).astype(jnp.int32)
    starts = jnp.where(doc == 0, 0, jnp.where(doc == 1, cut_row[0], cut_row[1]))
    places = (position - starts).astype(F32)
    freqs = jnp.exp(-math.log(1000000.0) * 2.0 * jnp.arange(head_dim // 2, dtype=F32) / head_dim)
    angles = places[:, None] * freqs[None, :]
    angles = jnp.concatenate([angles, angles], axis=-1)
    allowed = (doc[:, None] == doc[None, :]) & (position[None, :] <= position[:, None])
    return jnp.cos(angles), jnp.sin(angles), allowed


def rotate(v, cosine, sine_table):
    halfway = v.shape[-1] // 2
    turned = jnp.concatenate([-v[..., halfway:], v[..., :halfway]], axis=-1)
    return v * cosine + turned * sine_table


def head_piece(pre, gain, cosine, sine_table):
    shaped = pre.reshape(pre.shape[0], -1, gain.shape[0])
    return rotate(rms_rows(shaped, gain), cosine, sine_table)


def attend(inputs, scale):
    queries, keys, values, allowed = inputs
    scores = jnp.einsum("qgd,td->gqt", queries, keys, preferred_element_type=F32) * scale
    scores = jnp.where(allowed[None], scores, -1e30)
    highest = jnp.max(scores, axis=-1, keepdims=True)
    weights_exp = jnp.exp(scores - highest)
    totals = jnp.sum(weights_exp, axis=-1, keepdims=True)
    probs = weights_exp / totals
    log_norm = highest[..., 0] + jnp.log(totals[..., 0])
    outputs = jnp.einsum("gqt,td->qgd", probs.astype(BF), values, preferred_element_type=F32)
    return outputs.astype(BF), log_norm


def attend_grad(inputs, scale):
    queries, keys, values, d_outputs, log_norm, allowed = inputs
    scores = jnp.einsum("qgd,td->gqt", queries, keys, preferred_element_type=F32) * scale
    scores = jnp.where(allowed[None], scores, -1e30)
    probs = jnp.exp(scores - log_norm[..., None])
    d_probs = jnp.einsum("qgd,td->gqt", d_outputs, values, preferred_element_type=F32)
    inner_sum = jnp.sum(probs * d_probs, axis=-1, keepdims=True)
    d_scores = (probs * (d_probs - inner_sum)).astype(BF)
    d_queries = jnp.einsum("gqt,td->qgd", d_scores, keys, preferred_element_type=F32) * scale
    d_keys = jnp.einsum("gqt,qgd->td", d_scores, queries, preferred_element_type=F32) * scale
    d_values = jnp.einsum("gqt,qgd->td", probs.astype(BF), d_outputs, preferred_element_type=F32)
    return d_queries, d_keys, d_values


def gather_pieces(piece, ranks):
    rows, cols = piece.shape
    parts = lax.all_gather(piece, TP, axis=0)
    parts = parts.reshape(ranks[0], ranks[1], rows, cols)
    return jnp.moveaxis(parts, 1, 2).reshape(ranks[0] * rows, ranks[1] * cols)


def scatter_pieces(partial_sum, ranks):
    rows, cols = partial_sum.shape
    parts = partial_sum.astype(BF).reshape(ranks[0], rows // ranks[0], ranks[1], cols // ranks[1])
    parts = jnp.moveaxis(parts, 2, 1).reshape(-1, rows // ranks[0], cols // ranks[1])
    mine = lax.psum_scatter(parts, TP, scatter_dimension=0, tiled=False)
    return mine.astype(F32)


def spread(local, inner):
    rows, cols = local.shape
    parts = jnp.moveaxis(local.reshape(rows, inner, cols // inner), 1, 0)
    parts = lax.all_to_all(parts, "i", 0, 0, tiled=False)
    return parts.reshape(inner * rows, cols // inner)


def collect(block, inner):
    rows, cols = block.shape
    parts = lax.all_to_all(block.reshape(inner, rows // inner, cols), "i", 0, 0, tiled=False)
    return jnp.moveaxis(parts, 0, 1).reshape(rows // inner, inner * cols)


def full_rows(local, inner):
    return lax.all_gather(spread(local, inner), "t", axis=0, tiled=True)


def grad_rows(part, inner):
    mine = lax.psum_scatter(part.astype(BF), "t", scatter_dimension=0, tiled=True)
    return collect(mine, inner).astype(F32)


def plain_body(
    hidden_in, doc_starts, attn_gain, w_query, w_key, w_value, query_gain, key_gain,
    w_out, mlp_gain, w_gate, w_up, w_down, cotangent, *, groups, inner, halves,
):
    length, width_part = hidden_in.shape
    ranks = (inner, halves)
    width = width_part * halves
    head_dim = query_gain.shape[0]
    scale = head_dim ** (-0.5)
    t_index, m_index = lax.axis_index("t"), lax.axis_index("m")
    cuts = lax.dynamic_slice_in_dim(doc_starts, t_index * inner, inner, 0)
    cosine, sine_table, allowed = jax.vmap(partial(tables, length=length, head_dim=head_dim))(cuts)
    cosine = cosine.reshape(inner * length, 1, head_dim)
    sine_table = sine_table.reshape(inner * length, 1, head_dim)
    q_gain, k_gain = query_gain.astype(F32), key_gain.astype(F32)
    gains = lax.all_gather(jnp.stack([attn_gain, mlp_gain], 1), ("t", "i"), axis=0, tiled=True)
    gain_one, gain_two = gains[:, 0].astype(F32), gains[:, 1].astype(F32)

    full_in = gather_pieces(hidden_in, ranks)
    sizes = [w.shape[1] // inner for w in (w_query, w_key, w_value)] + [w_out.shape[0] // inner]
    edges = [sum(sizes[:n]) for n in range(5)]

    def by_rank(w):
        return w.reshape(w.shape[0], inner, w.shape[1] // inner)

    attn_local = jnp.concatenate([by_rank(w_query), by_rank(w_key), by_rank(w_value), by_rank(w_out.T)], 2)
    attn_cols = full_rows(attn_local.reshape(attn_local.shape[0], -1), inner)
    query_cols, key_cols, value_cols, out_t = [attn_cols[:, edges[n]:edges[n + 1]] for n in range(4)]
    resid = full_in.astype(F32)
    r_one = lax.rsqrt(jnp.mean(resid * resid, axis=-1, keepdims=True) + EPS)
    normed_one = (resid * r_one * gain_one).astype(BF)
    gate_cols = full_rows(w_gate, inner)
    up_cols = full_rows(w_up, inner)
    down_t = full_rows(w_down.T, inner)
    grad_full = gather_pieces(cotangent, ranks)

    query_pre = nn(normed_one, query_cols)
    key_pre = nn(normed_one, key_cols)
    value_low = nn(normed_one, value_cols).astype(BF)
    query_rot = head_piece(query_pre, q_gain, cosine, sine_table).astype(BF)
    key_rot = head_piece(key_pre, k_gain, cosine, sine_table).astype(BF)
    group = query_rot.shape[1]
    query_stack = query_rot.reshape(inner, length, group, head_dim)
    key_stack = key_rot.reshape(inner, length, head_dim)
    value_stack = value_low.reshape(inner, length, head_dim)
    attended, log_norm = lax.map(partial(attend, scale=scale), (query_stack, key_stack, value_stack, allowed))
    mixed = attended.reshape(inner * length, group * head_dim)
    middle = hidden_in.astype(F32) + scatter_pieces(nt(mixed, out_t), ranks)
    my_gain_one = lax.dynamic_slice_in_dim(gain_one, m_index * width_part, width_part, 0)
    my_gain_two = lax.dynamic_slice_in_dim(gain_two, m_index * width_part, width_part, 0)
    r_two = lax.rsqrt(lax.psum(jnp.sum(middle * middle, axis=-1, keepdims=True), "m") / width + EPS)
    normed_two = gather_pieces((middle * r_two * my_gain_two).astype(BF), ranks)

    gate_pre, up_pre = nn(normed_two, gate_cols), nn(normed_two, up_cols)
    d_inner = nn(grad_full, down_t)
    sigmoid_gate = jax.nn.sigmoid(gate_pre)
    inner_act = (gate_pre * sigmoid_gate * up_pre).astype(BF)
    d_gate_pre = (d_inner * up_pre * sigmoid_gate * (1.0 + gate_pre * (1.0 - sigmoid_gate))).astype(BF)
    d_up_pre = (d_inner * gate_pre * sigmoid_gate).astype(BF)
    d_normed_two = scatter_pieces(nt(d_gate_pre, gate_cols) + nt(d_up_pre, up_cols), ranks)
    mlp_out = scatter_pieces(nt(inner_act, down_t), ranks)
    block_out = (middle + mlp_out).astype(BF)

    scaled = d_normed_two * my_gain_two
    dot_two = lax.psum(jnp.sum(scaled * middle, axis=-1, keepdims=True), "m") / width
    d_gain_two = jnp.sum(d_normed_two * middle * r_two, axis=0)
    d_middle = cotangent.astype(F32) + r_two * scaled - middle * (r_two * r_two * r_two) * dot_two
    d_middle_low = gather_pieces(d_middle.astype(BF), ranks)
    d_gate = grad_rows(tn(normed_two, d_gate_pre), inner)
    d_up = grad_rows(tn(normed_two, d_up_pre), inner)
    d_down = grad_rows(tn(grad_full, inner_act), inner).T

    d_mixed = nn(d_middle_low, out_t).astype(BF)
    d_out_part = tn(d_middle_low, mixed)
    d_mixed_stack = d_mixed.reshape(inner, length, group, head_dim)
    d_query_stack, d_key_stack, d_value_stack = lax.map(
        partial(attend_grad, scale=scale),
        (query_stack, key_stack, value_stack, d_mixed_stack, log_norm, allowed),
    )
    rotary_piece = partial(head_piece, cosine=cosine, sine_table=sine_table)
    _, query_pull = jax.vjp(rotary_piece, query_pre, q_gain)
    d_query_pre, d_qgain_part = query_pull(d_query_stack.reshape(inner * length, group, head_dim))
    _, key_pull = jax.vjp(rotary_piece, key_pre, k_gain)
    d_key_pre, d_kgain_part = key_pull(d_key_stack.reshape(inner * length, 1, head_dim))
    d_heads = jnp.concatenate(
        [d_query_pre, d_key_pre, d_value_stack.reshape(inner * length, head_dim)], 1
    ).astype(BF)
    heads_cols = attn_cols[:, : edges[3]]
    d_normed_one = scatter_pieces(nt(d_heads, heads_cols), ranks)
    d_attn = jnp.concatenate([tn(normed_one, d_heads), d_out_part], 1)
    d_attn = grad_rows(d_attn, inner).reshape(-1, inner, edges[4])
    d_query, d_key, d_value, d_out_t = [
        d_attn[:, :, edges[n]:edges[n + 1]].reshape(d_attn.shape[0], -1) for n in range(4)
    ]
    mine = hidden_in.astype(F32)
    i_index = lax.axis_index("i")
    r_own = lax.dynamic_slice_in_dim(r_one, i_index * length, length, 0)
    scaled = d_normed_one * my_gain_one
    dot_one = lax.psum(jnp.sum(scaled * mine, axis=-1, keepdims=True), "m") / width
    d_gain_one = jnp.sum(d_normed_one * mine * r_own, axis=0)
    d_input = d_middle + r_own * scaled - mine * (r_own * r_own * r_own) * dot_one

    both = jnp.stack([d_gain_one, d_gain_two], 0)
    wide = lax.dynamic_update_slice(jnp.zeros((2, width), F32), both, (0, m_index * width_part))
    small = jnp.concatenate([wide.reshape(-1), d_qgain_part, d_kgain_part])
    small = lax.psum(small, ALL)
    wide = small[: 2 * width].reshape(2, width)
    shard = attn_gain.shape[0]
    own = lax.dynamic_slice(wide, (0, (t_index * inner + i_index) * shard), (2, shard))
    return (
        block_out, d_input, own[0], d_query, d_key, d_value,
        small[2 * width : 2 * width + head_dim], small[2 * width + head_dim :],
        d_out_t.T, own[1], d_gate, d_up, d_down,
    )


MESH = pl.DeviceIdType.MESH
ANY = pl.BlockSpec(memory_space=pl.ANY)
VMEM = pl.BlockSpec(memory_space=pltpu.VMEM)
SMEM = pl.BlockSpec(memory_space=pltpu.SMEM)
DMA = pltpu.SemaphoreType.DMA
LIMIT = 62 * 1024 * 1024


def flip(index, mask):
    if mask == 1:
        return index + 1 - 2 * lax.rem(index, 2)
    if mask == 2:
        return lax.rem(index + 2, 4)
    return 3 - index


def meet(peers):
    barrier = pltpu.get_barrier_semaphore()
    for peer in peers:
        pl.semaphore_signal(barrier, inc=1, device_id=peer, device_id_type=MESH)
    pl.semaphore_wait(barrier, len(peers))


def remote(src, dst, sems, k, peer):
    return pltpu.make_async_remote_copy(
        src_ref=src, dst_ref=dst, send_sem=sems[0].at[k], recv_sem=sems[1].at[k],
        device_id=peer, device_id_type=MESH,
    )


def at(start, size):
    return pl.ds(pl.multiple_of(start, size), size)


def tp_peers(i, m):
    return {"i": flip(i, 1)}, {"m": 1 - m}, {"i": flip(i, 2)}


class TpGather:
    def __init__(self, piece, full, sems, base, i, m):
        rows, cols = piece.shape
        half = rows // 2
        core, across, along = tp_peers(i, m)

        def slot(a, b, part=None):
            if part is None:
                return full.at[at(a * rows, rows), at(b * cols, cols)]
            return full.at[at(a * rows + part * half, half), at(b * cols, cols)]

        def go(src, dst, k, peer):
            return remote(src, dst, sems, base + k, peer)

        mine, far = slot(i, m), flip(i, 2)
        self.local = pltpu.make_async_copy(piece, mine, sems[2].at[base // 8])
        self.copies = [
            go(piece, mine, 0, core),
            go(piece, mine, 1, across),
            go(piece, mine, 2, along),
            go(slot(i, 1 - m, 0), slot(i, 1 - m, 0), 3, along),
            go(slot(i, 1 - m), slot(i, 1 - m), 4, core),
            go(slot(far, m, 1), slot(far, m, 1), 5, across),
            go(slot(far, m), slot(far, m), 6, core),
            go(slot(far, 1 - m), slot(far, 1 - m), 7, core),
        ]

    def start(self):
        for k in (1, 2, 0):
            self.copies[k].start()
        self.local.start()

    def relay(self):
        self.copies[1].wait_recv()
        self.copies[3].start()
        self.copies[4].start()
        self.copies[2].wait_recv()
        self.copies[5].start()
        self.copies[6].start()

    def relay_far(self):
        self.copies[3].wait_recv()
        self.copies[5].wait_recv()
        self.copies[7].start()

    def finish(self):
        for k in (0, 4, 6, 7):
            self.copies[k].wait_recv()
        for copy in self.copies:
            copy.wait_send()
        self.local.wait()


def add_rows(target, first, second, step=64):
    rows = target.shape[0]

    @pl.loop(0, rows, step=step)
    def _(r):
        span = pl.ds(pl.multiple_of(r, step), step)
        total = first[span, :].astype(F32) + second[span, :].astype(F32)
        target[span, :] = total.astype(target.dtype)


def tp_reduce_scratch(rows, cols, halves):
    return [
        pltpu.VMEM((2, rows, cols * halves), BF),
        pltpu.VMEM((2, rows, cols * halves), BF),
        pltpu.VMEM((2, rows // 2, cols), BF),
        pltpu.VMEM((rows // 2, cols * halves), BF),
        pltpu.VMEM((2, rows // 2, cols), BF),
        DMA((7,)), DMA((7,)), DMA((2,)),
    ]


class TpReduce:
    def __init__(self, parts, out, scratch, i, m):
        own, mate, by_x, by_y, last, send, recv, load = scratch
        rows, cols = out.shape
        half = rows // 2
        core, across, along = tp_peers(i, m)
        sems = (send, recv)
        self.args = (own, mate, by_x, by_y, last, out, m, rows, cols, half)

        def seq(a):
            return parts.at[at(a * rows, rows), :]

        self.loads = [
            pltpu.make_async_copy(seq(flip(i, 2)), own.at[1], load.at[1]),
            pltpu.make_async_copy(seq(i), own.at[0], load.at[0]),
        ]
        theirs = at((1 - m) * cols, cols)
        ours = at(m * cols, cols)
        low, high = pl.ds(0, half), pl.ds(half, half)
        self.copies = [
            remote(seq(flip(i, 3)), mate.at[1], sems, 0, core),
            remote(seq(flip(i, 1)), mate.at[0], sems, 1, core),
            remote(own.at[1, low, theirs], by_x.at[1], sems, 2, across),
            remote(own.at[0, low, theirs], by_x.at[0], sems, 3, across),
            remote(own.at[1, high, :], by_y, sems, 4, along),
            remote(own.at[1, low, ours], last.at[0], sems, 5, along),
            remote(own.at[0, high, theirs], last.at[1], sems, 6, across),
        ]
        self.ours = ours

    def start(self):
        for k in (0, 1):
            self.copies[k].start()
            self.loads[k].start()

    def fold_pair(self):
        own, mate = self.args[:2]
        copies = self.copies
        for side, k in ((1, 0), (0, 1)):
            self.loads[k].wait()
            copies[k].wait_recv()
            add_rows(own.at[side], own.at[side], mate.at[side])
            if side == 1:
                copies[2].start()
                copies[4].start()
            else:
                copies[3].start()

    def fold_links(self):
        own, mate, by_x, by_y, last, out, m, rows, cols, half = self.args
        copies, ours = self.copies, self.ours
        low, high = pl.ds(0, half), pl.ds(half, half)
        copies[2].wait_recv()
        add_rows(own.at[1, low, ours], own.at[1, low, ours], by_x.at[1])
        copies[5].start()
        copies[4].wait_recv()
        add_rows(own.at[0, high, :], own.at[0, high, :], by_y)
        copies[6].start()
        copies[3].wait_recv()
        add_rows(own.at[0, low, ours], own.at[0, low, ours], by_x.at[0])
        copies[5].wait_recv()
        add_rows(out.at[low, :], own.at[0, low, ours], last.at[0])
        copies[6].wait_recv()
        add_rows(out.at[high, :], own.at[0, high, ours], last.at[1])
        for copy in copies:
            copy.wait_send()


def tp_fold_scratch(rows, cols, halves):
    return [
        pltpu.VMEM((2, rows, cols * halves), BF),
        pltpu.VMEM((2, rows // 2, cols), BF),
        pltpu.VMEM((rows // 2, cols * halves), BF),
        pltpu.VMEM((2, rows // 2, cols), BF),
        DMA((7,)), DMA((7,)),
    ]


class TpFold:
    def __init__(self, parts, out, scratch, i, m):
        mate, by_x, by_y, last, send, recv = scratch
        rows, cols = out.shape
        half = rows // 2
        core, across, along = tp_peers(i, m)
        sems = (send, recv)
        mate, by_x, last = [[v[k] if isinstance(v, list) else v.at[k] for k in range(2)] for v in (mate, by_x, last)]

        def seq(a):
            return parts.at[at(a * rows, rows), :]

        def piece(a, part, b):
            return parts.at[at(a * rows + part * half, half), at(b * cols, cols)]

        far = flip(i, 2)
        self.mine = [seq(i), seq(far)]
        self.copies = [
            remote(seq(flip(i, 3)), mate[1], sems, 0, core),
            remote(seq(flip(i, 1)), mate[0], sems, 1, core),
            remote(piece(far, 0, 1 - m), by_x[1], sems, 2, across),
            remote(piece(i, 0, 1 - m), by_x[0], sems, 3, across),
            remote(parts.at[at(far * rows + half, half), :], by_y, sems, 4, along),
            remote(piece(far, 0, m), last[0], sems, 5, along),
            remote(piece(i, 1, 1 - m), last[1], sems, 6, across),
        ]
        self.low_far, self.low, self.high = piece(far, 0, m), piece(i, 0, m), piece(i, 1, m)
        self.high_all = parts.at[at(i * rows + half, half), :]
        self.mate, self.by_x, self.by_y, self.last, self.out, self.half = mate, by_x, by_y, last, out, half

    def send(self, k):
        self.copies[k].start()

    def side(self, k):
        self.copies[1 - k].wait_recv()
        add_rows(self.mine[k], self.mine[k], self.mate[k])
        for n in ((2, 4) if k == 1 else (3,)):
            self.copies[n].start()

    def finish(self, meanwhile=None):
        copies, half = self.copies, self.half
        copies[2].wait_recv()
        add_rows(self.low_far, self.low_far, self.by_x[1])
        copies[5].start()
        copies[4].wait_recv()
        add_rows(self.high_all, self.high_all, self.by_y)
        copies[6].start()
        if meanwhile is not None:
            meanwhile()
        copies[3].wait_recv()
        add_rows(self.low, self.low, self.by_x[0])
        copies[5].wait_recv()
        add_rows(self.out.at[pl.ds(0, half), :], self.low, self.last[0])
        copies[6].wait_recv()
        add_rows(self.out.at[pl.ds(half, half), :], self.high, self.last[1])

    def wait_sends(self):
        for copy in self.copies:
            copy.wait_send()


def pick(step, i):
    return jnp.where(step == 0, flip(i, 3), jnp.where(step == 1, flip(i, 1), jnp.where(step == 2, flip(i, 2), i)))


class LineGather:
    def __init__(self, own, full, sems, base, groups, t, near=None):
        self.near = near
        self.own, self.full, self.sems, self.base, self.groups, self.t = own, full, sems, base, groups, t
        self.rows = full.shape[0] // groups

    def block(self, b):
        return self.full.at[at(b * self.rows, self.rows), :]

    def go(self, b, k, step, own=False):
        n = self.base + (0 if step > 0 else self.groups - 1) + k
        src = self.own if own else self.block(b)
        if self.near is not None and k == 1:
            src = self.near[0 if step > 0 else 1]
        return remote(src, self.block(b), self.sems, n, {"t": self.t + step})

    def send(self, k):
        t, last = self.t, self.groups - 1

        @pl.when((t < last) & (t - k >= 0))
        def _():
            self.go(t - k, k, 1, k == 0).start()

        @pl.when((t > 0) & (t + k <= last))
        def _():
            self.go(t + k, k, -1, k == 0).start()

    def arrive(self, k):
        t, last = self.t, self.groups - 1

        @pl.when(t - k - 1 >= 0)
        def _():
            self.go(t - k - 1, k, 1).wait_recv()

        @pl.when(t + k + 1 <= last)
        def _():
            self.go(t + k + 1, k, -1).wait_recv()

    def pass_on(self, k):
        if self.near is None or k > 1:
            self.arrive(k - 1)
        if k < self.groups - 1:
            self.send(k)

    def wait_sends(self):
        t, last = self.t, self.groups - 1
        for k in range(0 if self.near is None else 1, self.groups - 1):
            @pl.when((t < last) & (t - k >= 0))
            def _():
                self.go(t - k, k, 1, k == 0).wait_send()

            @pl.when((t > 0) & (t + k <= last))
            def _():
                self.go(t + k, k, -1, k == 0).wait_send()


class LineReduce:
    def __init__(self, grads, ups, downs, back, stage, spare, load, sems, base, move_sems, t, i, before, early=None):
        self.grads, self.ups, self.downs, self.back, self.stage, self.spare = grads, ups, downs, back, stage, spare
        self.load, self.sems, self.base, self.move_sems = load, sems, base, move_sems
        self.t, self.i, self.before, self.early = t, i, before, early

    def up(self, k, src):
        return remote(src, self.ups.at[k], self.sems, self.base + k, {"t": self.t + 1})

    def down(self, k, src):
        return remote(src, self.downs.at[k], self.sems, self.base + 3 + k, {"t": self.t - 1})

    def first(self, b):
        if b > 0:
            @pl.when(self.t == 0)
            def _():
                self.up(3 - b, self.grads.at[b]).start()
        if b < 3:
            @pl.when(self.t == 3)
            def _():
                self.down(b, self.grads.at[b]).start()

    def total(self, place, sources):
        loads = [pltpu.make_async_copy(sources[0], self.stage.at[place], self.load.at[0])]
        loads += [pltpu.make_async_copy(v, self.spare, self.load.at[1]) for v in sources[1:]]
        loads[0].start()
        loads[1].start()
        loads[0].wait()
        for n, copy in enumerate(loads[1:]):
            if n > 0:
                copy.start()
            copy.wait()
            add_rows(self.stage.at[place], self.stage.at[place], self.spare)

    def relay(self, place, way, k):
        make = self.up if way == "up" else self.down
        slots = self.ups if way == "up" else self.downs
        if self.early is not None and place == 0:
            slots = self.early[0 if way == "up" else 1]
        else:
            make(k, slots.at[k]).wait_recv()
        self.total(place, [slots.at[k], self.grads.at[3 - k if way == "up" else k]])
        make(k, self.stage.at[place]).start()

    def relayed(self, place, way, k):
        (self.up if way == "up" else self.down)(k, self.stage.at[place]).wait_send()

    PLAN = {1: ((0, "up", 0), (1, "up", 1), (2, "down", 0)), 2: ((0, "down", 0), (1, "up", 0), (2, "down", 1))}

    def hop(self, places):
        for t, plan in self.PLAN.items():
            @pl.when(self.t == t)
            def _():
                for place, way, k in plan:
                    if place in places:
                        if self.before is not None:
                            self.before.relayed(place, way, k)
                        self.relay(place, way, k)

    def moves(self):
        lanes = self.stage.shape[2] // 4
        found = []
        for j in (2, 3, 1):
            p = flip(self.i, j)
            view = self.stage.at[3, :, at(p * lanes, lanes)]
            found.append(remote(view, self.back.at[self.i], self.move_sems, self.base // 6 * 4 + j, {"i": p}))
        view = self.stage.at[3, :, at(self.i * lanes, lanes)]
        return found, pltpu.make_async_copy(view, self.back.at[self.i], self.load.at[2])

    def close(self):
        if self.before is not None:
            self.before.closed()
        for t in range(4):
            @pl.when(self.t == t)
            def _():
                sources = [self.grads.at[t]]
                if t > 0:
                    self.up(3 - t, self.ups.at[3 - t]).wait_recv()
                    sources.append(self.ups.at[3 - t])
                if t < 3:
                    self.down(t, self.downs.at[t]).wait_recv()
                    sources.append(self.downs.at[t])
                self.total(3, sources)

        found, keep = self.moves()
        for move in found:
            move.start()
        keep.start()

    def closed(self):
        found, keep = self.moves()
        for move in found:
            move.wait()
        keep.wait()

    def wait_firsts(self, ks=(0, 1, 2)):
        @pl.when(self.t == 0)
        def _():
            for k in ks:
                self.up(k, self.grads.at[3 - k]).wait_send()

        @pl.when(self.t == 3)
        def _():
            for k in ks:
                self.down(k, self.grads.at[k]).wait_send()

    def wait_early(self):
        @pl.when(self.t == 1)
        def _():
            self.up(0, self.ups.at[0]).wait_recv()

        @pl.when(self.t == 2)
        def _():
            self.down(0, self.downs.at[0]).wait_recv()

    def wait_relays(self):
        for t, plan in self.PLAN.items():
            @pl.when(self.t == t)
            def _():
                for place, way, k in plan:
                    self.relayed(place, way, k)


def tp_group(i, m):
    return list(tp_peers(i, m))


def row_loop(rows, step=64):
    def wrap(f):
        @pl.loop(0, rows, step=step)
        def _(r):
            f(pl.ds(pl.multiple_of(r, step), step))

    return wrap


def mlp_kernel(groups, two_full, grad_full, first_w, other_w, near_w, middle, stat, cot, gain,
               rest_w, grads, ups, downs, next_up, next_down, back, out_parts, d_middle, d_gain, piece, *scratch):
    (x, g, w, act, act_t, fresh, stage, spare, sums, other, load, z_send, z_recv,
     r_send, r_recv, m_send, m_recv, f_send, f_recv, s_send, s_recv, free) = scratch
    t, i, m = lax.axis_index("t"), lax.axis_index("i"), lax.axis_index("m")
    others = [{"i": flip(i, j)} for j in (1, 2, 3)]
    meet(others + [{"m": 1 - m}] + [{"t": flip(t, j)} for j in (1, 2, 3)])
    tokens, wide = x.shape
    rows, part = middle.shape
    unit = w.shape[2] // 3
    two, three = 2 * unit, 3 * unit
    block = wide // groups
    sems = (z_send, z_recv)
    lines = [
        LineGather(other_w.at[c], rest_w.at[c], sems, 6 * c, groups, t, [near_w.at[0], near_w.at[1]] if c == 0 else None)
        for c in range(2)
    ]
    lines[0].pass_on(1)
    lines[1].send(0)
    take_g = pltpu.make_async_copy(grad_full, g, load.at[3])
    take_x = pltpu.make_async_copy(two_full, x, load.at[8])
    take_w = [pltpu.make_async_copy(first_w.at[c], w.at[c], load.at[4 + c]) for c in range(2)]
    own = [
        pltpu.make_async_copy(other_w.at[c], w.at[2 + c, at(t * block, block), :], load.at[6 + c]) for c in range(2)
    ]

    def rest(c):
        spans = [at(flip(t, j) * block, block) for j in (1, 2, 3)]
        return [
            pltpu.make_async_copy(rest_w.at[c, span, :], w.at[2 + c, span, :], load.at[9 + 3 * c + j])
            for j, span in enumerate(spans)
        ]

    def fetch(c):
        for j, copy in enumerate(rest(c)):
            if c == 1:
                copy.start()
                continue
            b = flip(t, j + 1)
            span = at(b * block, block)
            for step, side in ((-1, 0), (1, 1)):
                @pl.when(b == t + step)
                def _():
                    pltpu.make_async_copy(near_w.at[side], w.at[2, span, :], load.at[9 + j]).start()

            @pl.when((b != t - 1) & (b != t + 1))
            def _():
                copy.start()

    first = [take_w[0], take_x, take_g, take_w[1]] + own
    for copy in first:
        copy.start()
    for copy in first:
        copy.wait()
    reds = []
    for c in range(2):
        reds.append(LineReduce(
            grads.at[c], ups.at[c], downs.at[c], back.at[c], stage, spare, load, (r_send, r_recv), 6 * c,
            (m_send, m_recv), t, i, reds[-1] if reds else None))
    ahead = LineReduce(grads.at[2], next_up, next_down, None, stage, spare, load, (r_send, r_recv), 12,
                       (m_send, m_recv), t, i, None)
    order = (3, 0, 2, 1)
    events = {
        (1, 0): lambda: lines[0].pass_on(2),
        (1, 4): lambda: lines[1].pass_on(1),
        (1, 7): lambda: (lines[0].pass_on(3), fetch(0), reds[0].hop((0,))),
        (2, 7): lambda: (lines[1].pass_on(2), reds[0].hop((1, 2)), lines[1].pass_on(3), fetch(1)),
        (3, 0): lambda: reds[0].close(),
        (3, 4): lambda: reds[1].hop((0,)),
    }

    def hook(c, slot):
        for (when_c, when_slot), run in events.items():
            if when_slot == slot:
                @pl.when(c == when_c)
                def _():
                    run()

    def stored(c, n):
        return pltpu.make_async_copy(fresh.at[n % 2], grads.at[c, order[n]], load.at[15 + n % 2])

    @pl.loop(0, 4)
    def _(c):
        for n in range(2):
            @pl.when(c == 2 + n)
            def _():
                for copy in rest(n):
                    copy.wait()

        for n in range(4):
            span = pl.ds(n * rows, rows)
            d_inner = nn(g[span, :], w[c, :, two:three])
            both = nn(x[span, :], w[c, :, 0:two])
            gate, up = both[:, :unit], both[:, unit:]
            sig = jax.nn.sigmoid(gate)
            silu = gate * sig
            d_gate = (d_inner * up * sig * (1.0 + gate * (1.0 - sig))).astype(BF)
            d_up = (d_inner * silu).astype(BF)
            inner = (silu * up).astype(BF)
            for k, v in enumerate((d_gate, d_up, inner)):
                act[c, span, k * unit:(k + 1) * unit] = v
                act_t[k * unit:(k + 1) * unit, span] = v.T
            hook(c, n)
        for n in range(4):
            cols = pl.ds(order[n] * block, block)
            fresh[n % 2, 0:two, :] = nn(act_t[0:two, :], x[:, cols]).astype(BF)
            fresh[n % 2, two:three, :] = nn(act_t[two:three, :], g[:, cols]).astype(BF)
            stored(c, n).start()
            for done in ((n - 1,) if n < 3 else (2, 3)):
                if done >= 0:
                    stored(c, done).wait()
                    for q in range(2):
                        @pl.when(c == q)
                        def _():
                            reds[q].first(order[done])

                    if done < 2:
                        @pl.when(c == 2)
                        def _():
                            ahead.first(order[done])
            hook(c, 4 + n)

    for peer in tp_group(i, m):
        pl.semaphore_signal(free, inc=1, device_id=peer, device_id_type=MESH)
    quarter, half = rows // 2, part
    base = 2 * rows
    lists = [
        [g.at[pl.ds(0, rows), :], g.at[pl.ds(rows, rows), :]],
        [g.at[pl.ds(base, quarter), pl.ds(k * half, half)] for k in range(2)],
        g.at[pl.ds(base + quarter, quarter), :],
        [g.at[pl.ds(base + 2 * quarter, quarter), pl.ds(k * half, half)] for k in range(2)],
    ]
    fold = TpFold(x, d_middle, lists + [f_send, f_recv], i, m)

    def product(span, cols, low, high):
        total = nt(act[0, span, low:high], w[0, cols, low:high])
        for c in range(1, 4):
            total += nt(act[c, span, low:high], w[c, cols, low:high])
        return total.astype(BF)

    def tiles(f):
        @pl.loop(0, wide, step=512)
        def _(col):
            f(pl.ds(pl.multiple_of(col, 512), 512))

    @pl.loop(0, 4)
    def _(step):
        span = at(pick(step, i) * rows, rows)

        @tiles
        def _(cols):
            x[span, cols] = product(span, cols, 0, two)

        @pl.when(step == 0)
        def _():
            pl.semaphore_wait(free, 3)
            fold.send(0)

        @pl.when(step == 1)
        def _():
            fold.send(1)
            reds[1].hop((1, 2))

        @pl.when(step == 2)
        def _():
            fold.side(1)

    fold.side(0)

    def project(first):
        @pl.loop(first, first + 2)
        def _(s):
            span = at(s * rows, rows)

            @tiles
            def _(cols):
                act_t[0:rows, cols] = product(span, cols, two, three)

            put = pltpu.make_async_copy(act_t.at[pl.ds(0, rows), :], out_parts.at[span, :], load.at[15])
            put.start()
            put.wait()

    project(0)
    fold.finish(lambda: (project(2), reds[1].close()))
    d_gain[...] = jnp.zeros_like(d_gain)

    @row_loop(rows)
    def _(span):
        dn, v, r = d_middle[span, :], middle[span, :], stat[span, :]
        sums[span, :] = jnp.broadcast_to(jnp.sum(dn * gain[...] * v, axis=-1, keepdims=True), r.shape)
        d_gain[0:1, :] += jnp.sum(dn * v * r[:, :1], axis=0, keepdims=True)

    swap = remote(sums, other, (s_send, s_recv), 0, {"m": 1 - m})
    swap.start()
    swap.wait()

    @row_loop(rows)
    def _(span):
        r = stat[span, :]
        factor = (r * r * r * ((sums[span, :] + other[span, :]) / wide))[:, :1]
        d = cot[span, :].astype(F32) + r[:, :1] * (d_middle[span, :] * gain[...]) - middle[span, :] * factor
        d_middle[span, :] = d
        piece[span, :] = d.astype(BF)

    fold.wait_sends()
    for line in lines:
        line.wait_sends()
    ahead.wait_early()
    ahead.wait_firsts((0,))
    for red in reds:
        red.wait_firsts()
    reds[1].wait_relays()
    reds[1].closed()


def shape(dims, dtype):
    return jax.ShapeDtypeStruct(dims, dtype)


def comm_call(kernel, ins, outs, scratch, number):
    return pl.pallas_call(
        kernel,
        out_shape=[s for s, _ in outs],
        in_specs=ins,
        out_specs=[b for _, b in outs],
        scratch_shapes=scratch,
        compiler_params=pltpu.CompilerParams(
            collective_id=number, has_side_effects=True, vmem_limit_bytes=LIMIT
        ),
    )


def allow(cut, q0, qn, kn):
    q = q0 + lax.broadcasted_iota(jnp.int32, (qn, kn), 0)
    k = lax.broadcasted_iota(jnp.int32, (qn, kn), 1)
    doc_q = (q >= cut[0]).astype(jnp.int32) + (q >= cut[1]).astype(jnp.int32)
    doc_k = (k >= cut[0]).astype(jnp.int32) + (k >= cut[1]).astype(jnp.int32)
    return (doc_q == doc_k) & (k <= q)


def turn(v):
    half = v.shape[1] // 2
    return jnp.concatenate([-v[:, half:], v[:, :half]], axis=1)


def turn_back(v):
    half = v.shape[1] // 2
    return jnp.concatenate([v[:, half:], -v[:, :half]], axis=1)


def fore_kernel(groups, heads, hd, cuts, pack, gate, up, down, hidden, cot, qk_gain, table,
                attn, first_w, other_w, near_w, normed_out, pre, qkv, stats, mixed, middle, stat, two_full, grad_full,
                gain_rows,
                *scratch):
    fold_scratch, (full, weights, piece, other, load, w_send, w_recv, w_local, z_send, z_recv,
                   g_send, g_recv, g_local, s_send, s_recv) = scratch[:6], scratch[6:]
    x = full
    t, i, m = lax.axis_index("t"), lax.axis_index("i"), lax.axis_index("m")
    rows, wide = hidden.shape[0], x.shape[1]
    nq, kv = heads * hd, (heads + 2) * hd
    shard = pack.shape[1]
    unit = first_w.shape[2] // 3
    others = [{"i": flip(i, j)} for j in (1, 2, 3)]
    meet(others + [{"m": 1 - m}] + [{"t": flip(t, j)} for j in (1, 2, 3)])
    mine = attn.at[at((t * 4 + i) * shard, shard), :]
    spread = [remote(pack.at[flip(i, j)], mine, (w_send, w_recv), j - 1, others[j - 1]) for j in (2, 3, 1)]
    own = pltpu.make_async_copy(pack.at[i], mine, w_local.at[0])
    for copy in spread:
        copy.start()
    own.start()
    gather_h = TpGather(hidden, full, (g_send, g_recv, g_local), 0, i, m)
    gather_g = TpGather(cot, grad_full, (g_send, g_recv, g_local), 8, i, m)
    gather_h.start()

    def chunk(c):
        if c < 2:
            place = first_w.at[c, at((t * 4 + i) * shard, shard), :]
        else:
            place = other_w.at[c - 2, at(i * shard, shard), :]
        found, kept = [], []
        for n, src in enumerate((gate, up, down)):
            dst = place.at[:, pl.ds(n * unit, unit)]

            def view(p):
                return src.at[:, at(p * 4 * unit + c * unit, unit)]

            for j in (2, 3, 1):
                found.append(remote(view(flip(i, j)), dst, (w_send, w_recv), 3 + 9 * c + 3 * n + j - 1, others[j - 1]))
            kept.append(pltpu.make_async_copy(view(i), dst, w_local.at[1 + 3 * c + n]))
        return found, kept

    chunks = [chunk(c) for c in range(4)]

    def begin(c):
        for copy in chunks[c][0] + chunks[c][1]:
            copy.start()

    def landed(c):
        for copy in chunks[c][0]:
            copy.wait_recv()
        for copy in chunks[c][1]:
            copy.wait()

    sems = (z_send, z_recv)
    block = 4 * shard
    line = LineGather(attn.at[at(t * block, block), :], attn, sems, 0, groups, t)
    lines = [
        LineGather(first_w.at[c, at(t * block, block), :], first_w.at[c], sems, 6 * c + 6, groups, t) for c in range(2)
    ]
    above = remote(other_w.at[0], near_w.at[0], sems, 18, {"t": t + 1})
    below = remote(other_w.at[0], near_w.at[1], sems, 19, {"t": t - 1})

    def near_start():
        @pl.when(t < groups - 1)
        def _():
            above.start()

        @pl.when(t > 0)
        def _():
            below.start()

    own.wait()
    for copy in spread:
        copy.wait_recv()
    line.send(0)
    begin(0)
    line.pass_on(1)
    gather_h.relay()
    begin(1)
    line.pass_on(2)
    gather_h.relay_far()
    gather_g.start()
    begin(2)
    begin(3)
    landed(0)
    lines[0].send(0)
    line.pass_on(3)
    landed(1)
    lines[1].send(0)
    fill = pltpu.make_async_copy(attn, weights, load.at[0])
    fill.start()
    gather_h.finish()
    fill.wait()
    gain_rows[...] = jnp.transpose(weights[:, kv + nq:kv + nq + 128].astype(F32))[0:8, :]
    gain = gain_rows[0:1, :]
    gain_two = gain_rows[1:2, at(m * (wide // 2), wide // 2)]
    parts = full
    fold = TpFold(parts, middle, fold_scratch, i, m)

    @pl.loop(0, 4)
    def _(step):
        s = pick(step, i)
        start = s * rows
        def sub(r, size):
            return pl.ds(pl.multiple_of(start + r, size), size)

        cut = (cuts[s, 0], cuts[s, 1])

        @pl.loop(0, rows, step=64)
        def _(r):
            span = sub(r, 64)
            v = x[span, :].astype(F32)
            scale = lax.rsqrt(jnp.mean(v * v, axis=-1, keepdims=True) + EPS)
            stats[span, :] = jnp.broadcast_to(scale, (64, stats.shape[1]))
            x[span, :] = (v * scale * gain_rows[0:1, :]).astype(BF)

        everything = sub(0, rows)
        keep = pltpu.make_async_copy(x.at[everything, :], normed_out.at[everything, :], load.at[1])
        keep.start()
        heads_pre = nn(x[everything, :], weights[:, :kv])
        pre[everything, :] = heads_pre
        c, sn = table[everything, 0:hd], table[everything, hd:2 * hd]
        for h in range(heads + 1):
            lanes = slice(h * hd, (h + 1) * hd)
            n = rms_rows(heads_pre[:, lanes], qk_gain[0:1, :] if h < heads else qk_gain[1:2, :])
            qkv[everything, lanes] = (n * c + turn(n) * sn).astype(BF)
        qkv[everything, nq + hd:kv] = heads_pre[:, nq + hd:kv].astype(BF)
        half = rows // 2
        for b in range(2):
            kn = (b + 1) * half
            span = sub(b * half, half)
            mask = allow(cut, b * half, half, kn)
            keys, values = qkv[pl.ds(start, kn), nq:nq + hd], qkv[pl.ds(start, kn), nq + hd:kv]
            for h in range(heads):
                q = qkv[span, h * hd:(h + 1) * hd]
                scores = jnp.where(mask, nt(q, keys) * (hd ** -0.5), -1e30)
                top = jnp.max(scores, axis=-1, keepdims=True)
                e = jnp.exp(scores - top)
                total = jnp.sum(e, axis=-1, keepdims=True)
                probs = (e * (1.0 / total)).astype(BF)
                stats[span, h:h + 1] = top + jnp.log(total)
                mixed[span, h * hd:(h + 1) * hd] = nn(probs, values).astype(BF)

        keep.wait()

        @pl.loop(0, wide, step=512)
        def _(col):
            cols = pl.ds(pl.multiple_of(col, 512), 512)
            parts[everything, cols] = nt(mixed[everything, :], weights[cols, kv:kv + nq]).astype(BF)

        @pl.when(step == 0)
        def _():
            fold.send(0)

        @pl.when(step == 1)
        def _():
            fold.send(1)
            lines[0].pass_on(1)
            gather_g.relay()

        @pl.when(step == 2)
        def _():
            fold.side(1)
            lines[1].pass_on(1)

    fold.side(0)
    lines[0].pass_on(2)
    gather_g.relay_far()
    fold.finish(lambda: (lines[1].pass_on(2), landed(2), near_start()))

    @row_loop(rows)
    def _(span):
        v = middle[span, :] + hidden[span, :].astype(F32)
        middle[span, :] = v
        stat[span, :] = jnp.broadcast_to(jnp.sum(v * v, axis=-1, keepdims=True), stat[span, :].shape)

    swap = remote(stat, other, (s_send, s_recv), 0, {"m": 1 - m})
    swap.start()
    swap.wait()

    @row_loop(rows)
    def _(span):
        r = lax.rsqrt((stat[span, :] + other[span, :]) / wide + EPS)
        stat[span, :] = r
        piece[span, :] = (middle[span, :] * r[:, :1] * gain_two).astype(BF)

    gather = TpGather(piece, two_full, (g_send, g_recv, g_local), 16, i, m)
    gather.start()
    gather_g.finish()
    fold.wait_sends()
    lines[0].pass_on(3)
    landed(3)
    for c in range(4):
        for copy in chunks[c][0]:
            copy.wait_send()
    for copy in spread:
        copy.wait_send()
    gather.relay()
    lines[1].pass_on(3)
    gather.relay_far()
    for one in [line] + lines:
        one.wait_sends()

    @pl.when(t > 0)
    def _():
        above.wait_recv()
        below.wait_send()

    @pl.when(t < groups - 1)
    def _():
        below.wait_recv()
        above.wait_send()

    gather.finish()


def aft_kernel(groups, heads, hd, cuts, piece, normed, out_parts, attn, pre_in, middle, d_middle, qkv_in, stats_in,
               mixed_in, table_in, mlp_grads, early_up, early_down, qk_gain, hidden, gain, d_gain_two,
               d_input, block_out, back, gains, ups, downs, mlp_back, *scratch):
    fold_scratch, out_scratch = scratch[:6], scratch[6:14]
    (dm, nrm, pre, qkv, stats, mixed, table, weights, res, acc, grads, up_in, down_in, total, d_mix, d_pre, d_kv, qk_sum, sums, other,
     g_in, load, a_send, a_recv, a_local, send, recv, z_send, z_recv, g_send, g_recv, s_send, s_recv,
     local, stage, spare, line_load, r_send, r_recv, m_send, m_recv) = scratch[14:]
    t, i, m = lax.axis_index("t"), lax.axis_index("i"), lax.axis_index("m")
    others = [{"i": flip(i, j)} for j in (1, 2, 3)]
    meet(others + [{"m": 1 - m}] + [{"t": flip(t, j)} for j in (1, 2, 3)])
    rows, wide = hidden.shape[0], dm.shape[1]
    nq, kv = heads * hd, (heads + 2) * hd
    scale = hd ** -0.5
    gather = TpGather(piece, dm, (a_send, a_recv, a_local), 0, i, m)
    gather.start()
    reds = []
    for c in range(2):
        reds.append(LineReduce(
            mlp_grads.at[2 + c], ups.at[c], downs.at[c], mlp_back.at[c], stage, spare, line_load, (r_send, r_recv),
            6 * c, (m_send, m_recv), t, i, reds[-1] if reds else None, (early_up, early_down) if c == 0 else None))
    for b in (2, 1):
        reds[0].first(b)
    for b in (3, 0, 2, 1):
        reds[1].first(b)
    reds[0].hop((0,))
    fill = pltpu.make_async_copy(attn.at[:, pl.ds(0, kv + nq)], weights, load.at[2])
    fill.start()

    def fetch(step):
        span = at(pick(step, i) * rows, rows)
        return (pltpu.make_async_copy(normed.at[span, :], nrm, load.at[0]),
                *[pltpu.make_async_copy(src.at[span, :], dst, load.at[n]) for n, src, dst in (
                    (1, pre_in, pre), (4, qkv_in, qkv), (5, stats_in, stats),
                    (7, table_in, table))])

    two = TpReduce(out_parts, res, out_scratch, i, m)
    acc[...] = jnp.zeros_like(acc)
    qk_sum[...] = jnp.zeros_like(qk_sum)
    fold = TpFold(dm, d_input, fold_scratch, i, m)
    gather.relay()
    reds[0].hop((1, 2))
    gather.relay_far()
    two.start()
    reds[0].close()
    fill.wait()
    gather.finish()

    block = wide // groups
    spans = (slice(0, kv), slice(kv, kv + nq))

    def settle(which):
        for b in range(groups):
            grads[b, spans[which], :] = acc[spans[which], b * block:(b + 1) * block].astype(BF)

    def up(k, src, which):
        dst = up_in.at[k, spans[which], :]
        return remote(src, dst, (z_send, z_recv), 8 * which + k, {"t": t + 1})

    def down(k, src, which):
        dst = down_in.at[k, spans[which], :]
        return remote(src, dst, (z_send, z_recv), 8 * which + 4 + k, {"t": t - 1})

    def own_grads(b, which):
        return grads.at[b, spans[which], :]

    def begin(which):
        @pl.when(t == 0)
        def _():
            for k in range(groups - 1):
                up(k, own_grads(groups - 1 - k, which), which).start()

        @pl.when(t == groups - 1)
        def _():
            for k in range(groups - 1):
                down(k, own_grads(k, which), which).start()

    @pl.loop(0, 4)
    def _(s):
        span = at(s * rows, rows)
        take = pltpu.make_async_copy(mixed_in.at[span, :], mixed, load.at[6])
        take.start()
        take.wait()

        @pl.loop(0, wide, step=512)
        def _(col):
            cols = pl.ds(pl.multiple_of(col, 512), 512)
            acc[kv:kv + nq, cols] += tn(mixed[...], dm[span, cols])

    settle(1)
    begin(1)

    @pl.loop(0, 4)
    def _(step):
        s = pick(step, i)
        start = s * rows
        for copy in fetch(step):
            copy.start()

        def sub(r, size):
            return pl.ds(pl.multiple_of(start + r, size), size)

        cut = (cuts[s, 0], cuts[s, 1])
        everything = sub(0, rows)
        d_mix[...] = nn(dm[everything, :], weights[:, kv:kv + nq]).astype(BF)
        d_kv[...] = jnp.zeros_like(d_kv)
        half = rows // 2

        def undo(h, grad):
            lanes = slice(h * hd, (h + 1) * hd)
            row = 0 if h < heads else 1
            c, sn = table[:, 0:hd], table[:, hd:2 * hd]
            u = c * grad + turn_back(sn * grad)
            v = pre[:, lanes]
            r = lax.rsqrt(jnp.mean(v * v, axis=-1, keepdims=True) + EPS)
            qk_sum[0:1, row * hd:(row + 1) * hd] += jnp.sum(u * v * r, axis=0, keepdims=True)
            scaled = u * qk_gain[row:row + 1, :]
            undone = r * scaled - v * (r * r * r) * jnp.mean(scaled * v, axis=-1, keepdims=True)
            d_pre[:, lanes] = undone.astype(BF)

        for copy in fetch(step)[1:]:
            copy.wait()
        for h in range(heads):
            lanes = slice(h * hd, (h + 1) * hd)
            found = []
            for b in range(2):
                kn = (b + 1) * half
                span = slice(b * half, kn)
                mask = allow(cut, b * half, half, kn)
                keys, values = qkv[0:kn, nq:nq + hd], qkv[0:kn, nq + hd:kv]
                q, go = qkv[span, lanes], d_mix[span, lanes]
                scores = jnp.where(mask, nt(q, keys) * scale, -1e30)
                probs = jnp.exp(scores - stats[span, h:h + 1])
                d_probs = nt(go, values)
                inner = jnp.sum(probs * d_probs, axis=-1, keepdims=True)
                d_scores = (probs * (d_probs - inner)).astype(BF)
                found.append(nn(d_scores, keys) * scale)
                d_kv[0:kn, 0:hd] += tn(d_scores, q) * scale
                d_kv[0:kn, hd:2 * hd] += tn(probs.astype(BF), go)
            undo(h, jnp.concatenate(found, axis=0))
        undo(heads, d_kv[:, 0:hd])
        d_pre[:, nq + hd:kv] = d_kv[:, hd:2 * hd].astype(BF)
        fetch(step)[0].wait()

        @pl.loop(0, wide, step=512)
        def _(col):
            cols = pl.ds(pl.multiple_of(col, 512), 512)
            acc[0:kv, cols] += tn(d_pre[...], nrm[:, cols])
            dm[everything, cols] = nt(d_pre[...], weights[cols, 0:kv]).astype(BF)

        @pl.when(step == 0)
        def _():
            fold.send(0)
            two.fold_pair()
            reds[1].hop((0,))

        @pl.when(step == 1)
        def _():
            fold.send(1)
            reds[1].hop((1, 2))

        @pl.when(step == 2)
        def _():
            fold.side(1)

        @pl.when(step == 3)
        def _():
            fold.side(0)

    settle(0)
    begin(0)
    part = hidden.shape[1]
    kept = [acc.at[pl.ds(0, rows), pl.ds(n * part, part)] for n in range(2)]
    takes = [pltpu.make_async_copy(src, kept[n], load.at[2 + n]) for n, src in enumerate((middle, d_middle))]
    for take in takes:
        take.start()

    def hop(places, which):
        for at_t, plan in LineReduce.PLAN.items():
            @pl.when(t == at_t)
            def _():
                for place, way, n in plan:
                    if place in places:
                        make, slots = (up, up_in) if way == "up" else (down, down_in)
                        slot = slots.at[n, spans[which], :]
                        make(n, slot, which).wait_recv()
                        add_rows(slot, slot, own_grads(groups - 1 - n if way == "up" else n, which))
                        make(n, slot, which).start()

    hop((0,), 1)
    reds[1].close()
    for take in takes:
        take.wait()
    hop((1, 2), 1)
    fold.finish(lambda: hop((0,), 0))
    gains[...] = jnp.zeros_like(gains)
    own_half = at(m * (wide // 2), wide // 2)
    gains[1:2, own_half] = d_gain_two[0:1, :]
    gains[2:3, :] = jnp.concatenate([qk_sum[0:1, :]] * (wide // (2 * hd)), axis=1)

    @row_loop(rows)
    def _(span):
        dn, v = d_input[span, :], hidden[span, :].astype(F32)
        r = stats[span, heads:heads + 1]
        sums[span, :] = jnp.broadcast_to(jnp.sum(dn * gain[...] * v, axis=-1, keepdims=True), sums[span, :].shape)
        gains[0:1, own_half] += jnp.sum(dn * v * r, axis=0, keepdims=True)

    swap = remote(sums, other, (s_send, s_recv), 0, {"m": 1 - m})
    swap.start()
    ways = [{"i": flip(i, 1)}, {"m": 1 - m}, {"i": flip(i, 2)}, {"t": flip(t, 1)}, {"t": flip(t, 2)}]

    def trade(k):
        return remote(gains, g_in.at[k], (g_send, g_recv), k, ways[k])

    def give(n):
        trade(n).start()
        trade(n).wait()
        gains[...] += g_in[n]

    give(0)
    swap.wait()

    @row_loop(rows)
    def _(span):
        r = stats[span, heads:heads + 1]
        factor = r * r * r * ((sums[span, :] + other[span, :]) / wide)[:, :1]
        d = kept[1][span, :] + r * (d_input[span, :] * gain[...])
        d_input[span, :] = d - hidden[span, :].astype(F32) * factor

    give(1)
    hop((1, 2), 0)
    give(2)
    give(3)
    give(4)
    two.fold_links()

    @row_loop(rows)
    def _(span):
        block_out[span, :] = (kept[0][span, :] + res[span, :]).astype(BF)

    for b in range(groups):
        @pl.when(t == b)
        def _():
            for which in (1, 0):
                final = total.at[spans[which], :]
                own = own_grads(b, which)
                if b > 0:
                    slot = up_in.at[groups - 1 - b, spans[which], :]
                    up(groups - 1 - b, slot, which).wait_recv()
                    add_rows(final, own, slot)
                    own = final
                if b < groups - 1:
                    slot = down_in.at[b, spans[which], :]
                    down(b, slot, which).wait_recv()
                    add_rows(final, own, slot)

    sub_cols = block // 4
    moves = []
    for j in (2, 3, 1):
        view = total.at[:, at(flip(i, j) * sub_cols, sub_cols)]
        moves.append(remote(view, back.at[i], (send, recv), j, others[j - 1]))
    keep = pltpu.make_async_copy(total.at[:, at(i * sub_cols, sub_cols)], back.at[i], local.at[0])
    for move in moves:
        move.start()
    keep.start()
    for which in range(2):
        for k in range(groups - 1):
            @pl.when(t < groups - 1 - k)
            def _():
                up(k, up_in.at[k, spans[which], :], which).wait_send()

            @pl.when(t > k)
            def _():
                down(k, down_in.at[k, spans[which], :], which).wait_send()

    fold.wait_sends()
    reds[0].wait_firsts((1, 2))
    reds[1].wait_firsts()
    reds[1].wait_relays()
    reds[1].closed()
    keep.wait()
    for move in moves:
        move.wait()


class Dims:
    def __init__(self, length, part, halves, inner, groups, hd, nq, shard, hidden_units):
        self.length, self.part, self.halves, self.inner, self.groups, self.hd = length, part, halves, inner, groups, hd
        self.nq, self.shard, self.heads, self.kv = nq, shard, nq // hd, nq + 2 * hd
        self.width, self.tokens = part * halves, length * inner
        self.unit, self.block, self.cols = hidden_units // 4, part * halves // groups, nq + 2 * hd + nq + 128

    def values(self):
        return (self.length, self.part, self.halves, self.inner, self.groups, self.hd, self.nq, self.shard,
                self.heads, self.kv, self.width, self.tokens, self.unit, self.block, self.cols)


def call_fore(dims, *args):
    (length, part, halves, inner, groups, hd, nq, shard, heads, kv, width, tokens, unit, block, cols) = dims.values()
    fold_scratch = tp_fold_scratch(length, part, halves)
    return comm_call(
        partial(fore_kernel, groups, heads, hd), [SMEM] + [VMEM] * 8,
        [(shape((width, cols), BF), ANY), (shape((2, width, 3 * unit), BF), ANY), (shape((2, block, 3 * unit), BF), ANY),
         (shape((2, block, 3 * unit), BF), ANY),
         (shape((tokens, width), BF), ANY), (shape((tokens, kv), F32), VMEM), (shape((tokens, kv), BF), VMEM),
         (shape((tokens, 128), F32), VMEM), (shape((tokens, nq), BF), VMEM), (shape((length, part), F32), VMEM),
         (shape((length, 128), F32), VMEM), (shape((tokens, width), BF), ANY), (shape((tokens, width), BF), ANY),
         (shape((8, width), F32), VMEM)],
        fold_scratch + [
            pltpu.VMEM((tokens, width), BF), pltpu.VMEM((width, cols), BF), pltpu.VMEM((length, part), BF),
            pltpu.VMEM((length, 128), F32), DMA((2,)),
            DMA((39,)), DMA((39,)), DMA((13,)), DMA((20,)), DMA((20,)),
            DMA((24,)), DMA((24,)), DMA((3,)), DMA((1,)), DMA((1,))], 0,
    )(*args)


def call_mlp(dims, *args):
    (length, part, halves, inner, groups, hd, nq, shard, heads, kv, width, tokens, unit, block, cols) = dims.values()
    return comm_call(
        partial(mlp_kernel, groups), [ANY] * 5 + [VMEM] * 4,
        [(shape((2, width, 3 * unit), BF), ANY), (shape((4, groups, 3 * unit, block), BF), ANY),
         (shape((2, 3, 3 * unit, block), BF), ANY), (shape((2, 3, 3 * unit, block), BF), ANY),
         (shape((1, 3 * unit, block), BF), ANY), (shape((1, 3 * unit, block), BF), ANY),
         (shape((2, inner, 3 * unit, shard), BF), ANY), (shape((tokens, width), BF), ANY),
         (shape((length, part), F32), VMEM), (shape((8, part), F32), VMEM), (shape((length, part), BF), VMEM)],
        [pltpu.VMEM((tokens, width), BF), pltpu.VMEM((tokens, width), BF), pltpu.VMEM((4, width, 3 * unit), BF),
         pltpu.VMEM((4, tokens, 3 * unit), BF), pltpu.VMEM((3 * unit, tokens), BF),
         pltpu.VMEM((2, 3 * unit, block), BF), pltpu.VMEM((4, 3 * unit, block), BF), pltpu.VMEM((3 * unit, block), BF),
         pltpu.VMEM((length, 128), F32), pltpu.VMEM((length, 128), F32), DMA((17,)),
         DMA((12,)), DMA((12,)), DMA((18,)), DMA((18,)), DMA((8,)), DMA((8,)),
         DMA((7,)), DMA((7,)), DMA((1,)), DMA((1,)), pltpu.SemaphoreType.REGULAR], 1,
    )(*args)


def call_aft(dims, *args):
    (length, part, halves, inner, groups, hd, nq, shard, heads, kv, width, tokens, unit, block, cols) = dims.values()
    fold_scratch = tp_fold_scratch(length, part, halves)
    return comm_call(
        partial(aft_kernel, groups, heads, hd), [SMEM] + [ANY] * 14 + [VMEM] * 4,
        [(shape((length, part), F32), VMEM), (shape((length, part), BF), VMEM),
         (shape((inner, nq + kv, block // inner), BF), ANY), (shape((8, width), F32), VMEM),
         (shape((2, 3, 3 * unit, block), BF), ANY), (shape((2, 3, 3 * unit, block), BF), ANY),
         (shape((2, inner, 3 * unit, shard), BF), ANY)],
        fold_scratch + tp_reduce_scratch(length, part, halves) + [
            pltpu.VMEM((tokens, width), BF), pltpu.VMEM((length, width), BF), pltpu.VMEM((length, kv), F32),
            pltpu.VMEM((length, kv), BF), pltpu.VMEM((length, 128), F32), pltpu.VMEM((length, nq), BF),
            pltpu.VMEM((length, 128), F32),
            pltpu.VMEM((width, nq + kv), BF), pltpu.VMEM((length, part), F32), pltpu.VMEM((nq + kv, width), F32),
            pltpu.VMEM((groups, nq + kv, block), BF),
            pltpu.VMEM((groups - 1, nq + kv, block), BF), pltpu.VMEM((groups - 1, nq + kv, block), BF),
            pltpu.VMEM((nq + kv, block), BF), pltpu.VMEM((length, nq), BF), pltpu.VMEM((length, kv), BF),
            pltpu.VMEM((length, 2 * hd), F32), pltpu.VMEM((8, 2 * hd), F32),
            pltpu.VMEM((length, 128), F32), pltpu.VMEM((length, 128), F32), pltpu.VMEM((5, 8, width), F32),
            DMA((8,)), DMA((8,)), DMA((8,)), DMA((1,)),
            DMA((4,)), DMA((4,)), DMA((16,)), DMA((16,)), DMA((5,)), DMA((5,)),
            DMA((1,)), DMA((1,)), DMA((1,)),
            pltpu.VMEM((4, 3 * unit, block), BF), pltpu.VMEM((3 * unit, block), BF), DMA((3,)),
            DMA((12,)), DMA((12,)), DMA((8,)), DMA((8,))], 2,
    )(*args)


def fast_body(
    hidden_in, doc_starts, attn_gain, w_query, w_key, w_value, query_gain, key_gain,
    w_out, mlp_gain, w_gate, w_up, w_down, cotangent, *, groups, inner, halves,
):
    length, part = hidden_in.shape
    shard = w_query.shape[0]
    width, tokens = part * halves, length * inner
    hd = query_gain.shape[0]
    heads = w_query.shape[1] // inner // hd
    nq, kv = heads * hd, (heads + 2) * hd
    hidden_units = w_gate.shape[1] // inner
    t_index, i_index, m_index = lax.axis_index("t"), lax.axis_index("i"), lax.axis_index("m")
    cuts = lax.dynamic_slice_in_dim(doc_starts, t_index * inner, inner, 0)
    cosine, sine_table, _ = jax.vmap(partial(tables, length=length, head_dim=hd))(cuts)
    table = jnp.concatenate([cosine.reshape(tokens, hd), sine_table.reshape(tokens, hd)], axis=1)
    qk_gain = jnp.zeros((8, hd), F32).at[0].set(query_gain.astype(F32)).at[1].set(key_gain.astype(F32))

    def by_rank(w):
        return jnp.moveaxis(w.reshape(shard, inner, w.shape[1] // inner), 1, 0)

    gains = jnp.zeros((shard, 128), BF).at[:, 0].set(attn_gain).at[:, 1].set(mlp_gain)
    pack = jnp.concatenate(
        [by_rank(w_query), by_rank(w_key), by_rank(w_value), by_rank(w_out.T),
         jnp.broadcast_to(gains[None], (inner, shard, 128))], 2)
    dims = Dims(length, part, halves, inner, groups, hd, nq, shard, hidden_units)
    unit = dims.unit
    (attn_w, first_w, other_w, near_w, normed_one, pre, qkv, stats, mixed, middle, r_two, two_full, grad_full, gain_rows) = call_fore(
        dims, cuts, pack, w_gate, w_up, w_down.T, hidden_in, cotangent, qk_gain, table)

    own_gains = lax.dynamic_slice(gain_rows, (0, m_index * part), (2, part))

    (_, mlp_grads, _, _, next_up, next_down, mlp_back, out_parts, d_middle, d_gain_two, d_low) = call_mlp(
        dims, two_full, grad_full, first_w, other_w, near_w, middle, r_two, cotangent, own_gains[1:2])

    d_input, block_out, attn_back, gains_out, _, _, last_back = call_aft(
        dims, cuts, d_low, normed_one, out_parts, attn_w, pre, middle, d_middle, qkv, stats, mixed, table, mlp_grads, next_up, next_down, qk_gain, hidden_in, own_gains[0:1], d_gain_two)

    all_back = jnp.concatenate([mlp_back, last_back], axis=0)

    def mlp_columns(first):
        part_of = all_back[:, :, first:first + unit, :]
        return jnp.transpose(part_of, (3, 1, 0, 2)).reshape(shard, inner * hidden_units).astype(F32)

    d_down = jnp.transpose(all_back[:, :, 2 * unit:, :], (1, 0, 2, 3)).reshape(inner * hidden_units, shard).astype(F32)
    own = lax.dynamic_slice(gains_out, (0, (t_index * inner + i_index) * shard), (2, shard))

    def columns(first, last):
        return jnp.moveaxis(attn_back[:, first:last, :], 2, 0).reshape(shard, -1).astype(F32)

    return (
        block_out, d_input, own[0], columns(0, nq), columns(nq, nq + hd), columns(nq + hd, kv),
        gains_out[2, :hd], gains_out[2, hd:2 * hd],
        attn_back[:, kv:kv + nq, :].reshape(inner * nq, shard).astype(F32), own[1],
        mlp_columns(0), mlp_columns(unit), d_down,
    )


def solution(mesh):
    dp, halves = mesh.shape["dp"], mesh.shape["mp"]
    inner = 4
    groups = dp // inner
    fine = Mesh(mesh.devices.reshape(groups, inner, halves), ("t", "i", "m"))
    rows = P(("t", "i"))
    block = P(("t", "i"), "m")
    turned = P("m", ("t", "i"))
    body = fast_body if groups == 4 and halves == 2 else plain_body
    return jax.shard_map(
        partial(body, groups=groups, inner=inner, halves=halves),
        mesh=fine,
        in_specs=(block, P(), rows, block, block, block, P(), P(), turned, rows, block, block, turned, block),
        out_specs=(block, block, rows, block, block, block, P(), P(), turned, rows, block, block, turned),
        check_vma=False,
    )
```

```python
from functools import partial
import math

import jax
import jax.numpy as jnp
from jax import lax
from jax.experimental import pallas as pl
from jax.experimental.pallas import tpu as pltpu
from jax.sharding import Mesh, PartitionSpec as P

BF = jnp.bfloat16
F32 = jnp.float32
EPS = 1e-05
TP = ("i", "m")
ALL = ("t", "i", "m")


def dot_f32(left, right, dims):
    return lax.dot_general(left, right, (dims, ((), ())), preferred_element_type=F32)


def nn(left, right):
    return dot_f32(left, right, ((1,), (0,)))


def nt(left, right):
    return dot_f32(left, right, ((1,), (1,)))


def tn(left, right):
    return dot_f32(left, right, ((0,), (0,)))


def rms_rows(v, gain):
    return v * lax.rsqrt(jnp.mean(v * v, axis=-1, keepdims=True) + EPS) * gain


def tables(cut_row, length, head_dim):
    position = jnp.arange(length, dtype=jnp.int32)
    doc = (position >= cut_row[0]).astype(jnp.int32) + (position >= cut_row[1]).astype(jnp.int32)
    starts = jnp.where(doc == 0, 0, jnp.where(doc == 1, cut_row[0], cut_row[1]))
    places = (position - starts).astype(F32)
    freqs = jnp.exp(-math.log(1000000.0) * 2.0 * jnp.arange(head_dim // 2, dtype=F32) / head_dim)
    angles = places[:, None] * freqs[None, :]
    angles = jnp.concatenate([angles, angles], axis=-1)
    allowed = (doc[:, None] == doc[None, :]) & (position[None, :] <= position[:, None])
    return jnp.cos(angles), jnp.sin(angles), allowed


def rotate(v, cosine, sine_table):
    halfway = v.shape[-1] // 2
    turned = jnp.concatenate([-v[..., halfway:], v[..., :halfway]], axis=-1)
    return v * cosine + turned * sine_table


def head_piece(pre, gain, cosine, sine_table):
    shaped = pre.reshape(pre.shape[0], -1, gain.shape[0])
    return rotate(rms_rows(shaped, gain), cosine, sine_table)


def attend(inputs, scale):
    queries, keys, values, allowed = inputs
    scores = jnp.einsum("qgd,td->gqt", queries, keys, preferred_element_type=F32) * scale
    scores = jnp.where(allowed[None], scores, -1e30)
    highest = jnp.max(scores, axis=-1, keepdims=True)
    weights_exp = jnp.exp(scores - highest)
    totals = jnp.sum(weights_exp, axis=-1, keepdims=True)
    probs = weights_exp / totals
    log_norm = highest[..., 0] + jnp.log(totals[..., 0])
    outputs = jnp.einsum("gqt,td->qgd", probs.astype(BF), values, preferred_element_type=F32)
    return outputs.astype(BF), log_norm


def attend_grad(inputs, scale):
    queries, keys, values, d_outputs, log_norm, allowed = inputs
    scores = jnp.einsum("qgd,td->gqt", queries, keys, preferred_element_type=F32) * scale
    scores = jnp.where(allowed[None], scores, -1e30)
    probs = jnp.exp(scores - log_norm[..., None])
    d_probs = jnp.einsum("qgd,td->gqt", d_outputs, values, preferred_element_type=F32)
    inner_sum = jnp.sum(probs * d_probs, axis=-1, keepdims=True)
    d_scores = (probs * (d_probs - inner_sum)).astype(BF)
    d_queries = jnp.einsum("gqt,td->qgd", d_scores, keys, preferred_element_type=F32) * scale
    d_keys = jnp.einsum("gqt,qgd->td", d_scores, queries, preferred_element_type=F32) * scale
    d_values = jnp.einsum("gqt,qgd->td", probs.astype(BF), d_outputs, preferred_element_type=F32)
    return d_queries, d_keys, d_values


def gather_pieces(piece, ranks):
    rows, cols = piece.shape
    parts = lax.all_gather(piece, TP, axis=0)
    parts = parts.reshape(ranks[0], ranks[1], rows, cols)
    return jnp.moveaxis(parts, 1, 2).reshape(ranks[0] * rows, ranks[1] * cols)


def scatter_pieces(partial_sum, ranks):
    rows, cols = partial_sum.shape
    parts = partial_sum.astype(BF).reshape(ranks[0], rows // ranks[0], ranks[1], cols // ranks[1])
    parts = jnp.moveaxis(parts, 2, 1).reshape(-1, rows // ranks[0], cols // ranks[1])
    mine = lax.psum_scatter(parts, TP, scatter_dimension=0, tiled=False)
    return mine.astype(F32)


def spread(local, inner):
    rows, cols = local.shape
    parts = jnp.moveaxis(local.reshape(rows, inner, cols // inner), 1, 0)
    parts = lax.all_to_all(parts, "i", 0, 0, tiled=False)
    return parts.reshape(inner * rows, cols // inner)


def collect(block, inner):
    rows, cols = block.shape
    parts = lax.all_to_all(block.reshape(inner, rows // inner, cols), "i", 0, 0, tiled=False)
    return jnp.moveaxis(parts, 0, 1).reshape(rows // inner, inner * cols)


def full_rows(local, inner):
    return lax.all_gather(spread(local, inner), "t", axis=0, tiled=True)


def grad_rows(part, inner):
    mine = lax.psum_scatter(part.astype(BF), "t", scatter_dimension=0, tiled=True)
    return collect(mine, inner).astype(F32)


def plain_body(
    hidden_in, doc_starts, attn_gain, w_query, w_key, w_value, query_gain, key_gain,
    w_out, mlp_gain, w_gate, w_up, w_down, cotangent, *, groups, inner, halves,
):
    length, width_part = hidden_in.shape
    ranks = (inner, halves)
    width = width_part * halves
    head_dim = query_gain.shape[0]
    scale = head_dim ** (-0.5)
    t_index, m_index = lax.axis_index("t"), lax.axis_index("m")
    cuts = lax.dynamic_slice_in_dim(doc_starts, t_index * inner, inner, 0)
    cosine, sine_table, allowed = jax.vmap(partial(tables, length=length, head_dim=head_dim))(cuts)
    cosine = cosine.reshape(inner * length, 1, head_dim)
    sine_table = sine_table.reshape(inner * length, 1, head_dim)
    q_gain, k_gain = query_gain.astype(F32), key_gain.astype(F32)
    gains = lax.all_gather(jnp.stack([attn_gain, mlp_gain], 1), ("t", "i"), axis=0, tiled=True)
    gain_one, gain_two = gains[:, 0].astype(F32), gains[:, 1].astype(F32)

    full_in = gather_pieces(hidden_in, ranks)
    sizes = [w.shape[1] // inner for w in (w_query, w_key, w_value)] + [w_out.shape[0] // inner]
    edges = [sum(sizes[:n]) for n in range(5)]

    def by_rank(w):
        return w.reshape(w.shape[0], inner, w.shape[1] // inner)

    attn_local = jnp.concatenate([by_rank(w_query), by_rank(w_key), by_rank(w_value), by_rank(w_out.T)], 2)
    attn_cols = full_rows(attn_local.reshape(attn_local.shape[0], -1), inner)
    query_cols, key_cols, value_cols, out_t = [attn_cols[:, edges[n]:edges[n + 1]] for n in range(4)]
    resid = full_in.astype(F32)
    r_one = lax.rsqrt(jnp.mean(resid * resid, axis=-1, keepdims=True) + EPS)
    normed_one = (resid * r_one * gain_one).astype(BF)
    gate_cols = full_rows(w_gate, inner)
    up_cols = full_rows(w_up, inner)
    down_t = full_rows(w_down.T, inner)
    grad_full = gather_pieces(cotangent, ranks)

    query_pre = nn(normed_one, query_cols)
    key_pre = nn(normed_one, key_cols)
    value_low = nn(normed_one, value_cols).astype(BF)
    query_rot = head_piece(query_pre, q_gain, cosine, sine_table).astype(BF)
    key_rot = head_piece(key_pre, k_gain, cosine, sine_table).astype(BF)
    group = query_rot.shape[1]
    query_stack = query_rot.reshape(inner, length, group, head_dim)
    key_stack = key_rot.reshape(inner, length, head_dim)
    value_stack = value_low.reshape(inner, length, head_dim)
    attended, log_norm = lax.map(partial(attend, scale=scale), (query_stack, key_stack, value_stack, allowed))
    mixed = attended.reshape(inner * length, group * head_dim)
    middle = hidden_in.astype(F32) + scatter_pieces(nt(mixed, out_t), ranks)
    my_gain_one = lax.dynamic_slice_in_dim(gain_one, m_index * width_part, width_part, 0)
    my_gain_two = lax.dynamic_slice_in_dim(gain_two, m_index * width_part, width_part, 0)
    r_two = lax.rsqrt(lax.psum(jnp.sum(middle * middle, axis=-1, keepdims=True), "m") / width + EPS)
    normed_two = gather_pieces((middle * r_two * my_gain_two).astype(BF), ranks)

    gate_pre, up_pre = nn(normed_two, gate_cols), nn(normed_two, up_cols)
    d_inner = nn(grad_full, down_t)
    sigmoid_gate = jax.nn.sigmoid(gate_pre)
    inner_act = (gate_pre * sigmoid_gate * up_pre).astype(BF)
    d_gate_pre = (d_inner * up_pre * sigmoid_gate * (1.0 + gate_pre * (1.0 - sigmoid_gate))).astype(BF)
    d_up_pre = (d_inner * gate_pre * sigmoid_gate).astype(BF)
    d_normed_two = scatter_pieces(nt(d_gate_pre, gate_cols) + nt(d_up_pre, up_cols), ranks)
    mlp_out = scatter_pieces(nt(inner_act, down_t), ranks)
    block_out = (middle + mlp_out).astype(BF)

    scaled = d_normed_two * my_gain_two
    dot_two = lax.psum(jnp.sum(scaled * middle, axis=-1, keepdims=True), "m") / width
    d_gain_two = jnp.sum(d_normed_two * middle * r_two, axis=0)
    d_middle = cotangent.astype(F32) + r_two * scaled - middle * (r_two * r_two * r_two) * dot_two
    d_middle_low = gather_pieces(d_middle.astype(BF), ranks)
    d_gate = grad_rows(tn(normed_two, d_gate_pre), inner)
    d_up = grad_rows(tn(normed_two, d_up_pre), inner)
    d_down = grad_rows(tn(grad_full, inner_act), inner).T

    d_mixed = nn(d_middle_low, out_t).astype(BF)
    d_out_part = tn(d_middle_low, mixed)
    d_mixed_stack = d_mixed.reshape(inner, length, group, head_dim)
    d_query_stack, d_key_stack, d_value_stack = lax.map(
        partial(attend_grad, scale=scale),
        (query_stack, key_stack, value_stack, d_mixed_stack, log_norm, allowed),
    )
    rotary_piece = partial(head_piece, cosine=cosine, sine_table=sine_table)
    _, query_pull = jax.vjp(rotary_piece, query_pre, q_gain)
    d_query_pre, d_qgain_part = query_pull(d_query_stack.reshape(inner * length, group, head_dim))
    _, key_pull = jax.vjp(rotary_piece, key_pre, k_gain)
    d_key_pre, d_kgain_part = key_pull(d_key_stack.reshape(inner * length, 1, head_dim))
    d_heads = jnp.concatenate(
        [d_query_pre, d_key_pre, d_value_stack.reshape(inner * length, head_dim)], 1
    ).astype(BF)
    heads_cols = attn_cols[:, : edges[3]]
    d_normed_one = scatter_pieces(nt(d_heads, heads_cols), ranks)
    d_attn = jnp.concatenate([tn(normed_one, d_heads), d_out_part], 1)
    d_attn = grad_rows(d_attn, inner).reshape(-1, inner, edges[4])
    d_query, d_key, d_value, d_out_t = [
        d_attn[:, :, edges[n]:edges[n + 1]].reshape(d_attn.shape[0], -1) for n in range(4)
    ]
    mine = hidden_in.astype(F32)
    i_index = lax.axis_index("i")
    r_own = lax.dynamic_slice_in_dim(r_one, i_index * length, length, 0)
    scaled = d_normed_one * my_gain_one
    dot_one = lax.psum(jnp.sum(scaled * mine, axis=-1, keepdims=True), "m") / width
    d_gain_one = jnp.sum(d_normed_one * mine * r_own, axis=0)
    d_input = d_middle + r_own * scaled - mine * (r_own * r_own * r_own) * dot_one

    both = jnp.stack([d_gain_one, d_gain_two], 0)
    wide = lax.dynamic_update_slice(jnp.zeros((2, width), F32), both, (0, m_index * width_part))
    small = jnp.concatenate([wide.reshape(-1), d_qgain_part, d_kgain_part])
    small = lax.psum(small, ALL)
    wide = small[: 2 * width].reshape(2, width)
    shard = attn_gain.shape[0]
    own = lax.dynamic_slice(wide, (0, (t_index * inner + i_index) * shard), (2, shard))
    return (
        block_out, d_input, own[0], d_query, d_key, d_value,
        small[2 * width : 2 * width + head_dim], small[2 * width + head_dim :],
        d_out_t.T, own[1], d_gate, d_up, d_down,
    )


MESH = pl.DeviceIdType.MESH
ANY = pl.BlockSpec(memory_space=pl.ANY)
VMEM = pl.BlockSpec(memory_space=pltpu.VMEM)
SMEM = pl.BlockSpec(memory_space=pltpu.SMEM)
DMA = pltpu.SemaphoreType.DMA
LIMIT = 62 * 1024 * 1024


def flip(index, mask):
    if mask == 1:
        return index + 1 - 2 * lax.rem(index, 2)
    if mask == 2:
        return lax.rem(index + 2, 4)
    return 3 - index


def meet(peers):
    barrier = pltpu.get_barrier_semaphore()
    for peer in peers:
        pl.semaphore_signal(barrier, inc=1, device_id=peer, device_id_type=MESH)
    pl.semaphore_wait(barrier, len(peers))


def remote(src, dst, sems, k, peer):
    return pltpu.make_async_remote_copy(
        src_ref=src, dst_ref=dst, send_sem=sems[0].at[k], recv_sem=sems[1].at[k],
        device_id=peer, device_id_type=MESH,
    )


def at(start, size):
    return pl.ds(pl.multiple_of(start, size), size)


def tp_peers(i, m):
    return {"i": flip(i, 1)}, {"m": 1 - m}, {"i": flip(i, 2)}


class TpGather:
    def __init__(self, piece, full, sems, base, i, m, lean=False):
        self.lean = lean
        rows, cols = piece.shape
        half = rows // 2
        core, across, along = tp_peers(i, m)

        def slot(a, b, part=None):
            if part is None:
                return full.at[at(a * rows, rows), at(b * cols, cols)]
            return full.at[at(a * rows + part * half, half), at(b * cols, cols)]

        def go(src, dst, k, peer):
            return remote(src, dst, sems, base + k, peer)

        mine, far = slot(i, m), flip(i, 2)
        self.local = pltpu.make_async_copy(piece, mine, sems[2].at[base // 8])
        self.copies = [
            go(piece, mine, 0, core),
            go(piece, mine, 1, across),
            go(piece, mine, 2, along),
            go(slot(i, 1 - m, 0), slot(i, 1 - m, 0), 3, along),
            go(slot(i, 1 - m), slot(i, 1 - m), 4, core),
            go(slot(far, m, None if lean else 1), slot(far, m, None if lean else 1), 5, across),
            go(slot(far, m), slot(far, m), 6, core),
            go(slot(far, 1 - m), slot(far, 1 - m), 7, core),
        ]

    def start(self):
        for k in (1, 2, 0):
            self.copies[k].start()
        self.local.start()

    def relay(self):
        self.copies[1].wait_recv()
        if not self.lean:
            self.copies[3].start()
        self.copies[4].start()
        self.copies[2].wait_recv()
        self.copies[5].start()
        self.copies[6].start()

    def relay_far(self):
        if not self.lean:
            self.copies[3].wait_recv()
        self.copies[5].wait_recv()
        self.copies[7].start()

    def finish(self):
        for k in (0, 4, 6, 7):
            self.copies[k].wait_recv()
        for k, copy in enumerate(self.copies):
            if k != 3 or not self.lean:
                copy.wait_send()
        self.local.wait()


def add_rows(target, first, second, step=64):
    rows = target.shape[0]

    @pl.loop(0, rows, step=step)
    def _(r):
        span = pl.ds(pl.multiple_of(r, step), step)
        total = first[span, :].astype(F32) + second[span, :].astype(F32)
        target[span, :] = total.astype(target.dtype)


def tp_reduce_scratch(rows, cols, halves):
    return [
        pltpu.VMEM((2, rows, cols * halves), BF),
        pltpu.VMEM((2, rows, cols * halves), BF),
        pltpu.VMEM((2, rows // 2, cols), BF),
        pltpu.VMEM((rows // 2, cols * halves), BF),
        pltpu.VMEM((2, rows // 2, cols), BF),
        DMA((7,)), DMA((7,)), DMA((2,)),
    ]


class TpReduce:
    def __init__(self, parts, out, scratch, i, m):
        own, mate, by_x, by_y, last, send, recv, load = scratch
        rows, cols = out.shape
        half = rows // 2
        core, across, along = tp_peers(i, m)
        sems = (send, recv)
        self.args = (own, mate, by_x, by_y, last, out, m, rows, cols, half)

        def seq(a):
            return parts.at[at(a * rows, rows), :]

        self.loads = [
            pltpu.make_async_copy(seq(flip(i, 2)), own.at[1], load.at[1]),
            pltpu.make_async_copy(seq(i), own.at[0], load.at[0]),
        ]
        theirs = at((1 - m) * cols, cols)
        ours = at(m * cols, cols)
        low, high = pl.ds(0, half), pl.ds(half, half)
        self.copies = [
            remote(seq(flip(i, 3)), mate.at[1], sems, 0, core),
            remote(seq(flip(i, 1)), mate.at[0], sems, 1, core),
            remote(own.at[1, low, theirs], by_x.at[1], sems, 2, across),
            remote(own.at[0, low, theirs], by_x.at[0], sems, 3, across),
            remote(own.at[1, high, :], by_y, sems, 4, along),
            remote(own.at[1, low, ours], last.at[0], sems, 5, along),
            remote(own.at[0, high, theirs], last.at[1], sems, 6, across),
        ]
        self.ours = ours

    def start(self):
        for k in (0, 1):
            self.copies[k].start()
            self.loads[k].start()

    def fold_pair(self):
        own, mate = self.args[:2]
        copies = self.copies
        for side, k in ((1, 0), (0, 1)):
            self.loads[k].wait()
            copies[k].wait_recv()
            add_rows(own.at[side], own.at[side], mate.at[side])
            if side == 1:
                copies[2].start()
                copies[4].start()
            else:
                copies[3].start()

    def fold_links(self):
        own, mate, by_x, by_y, last, out, m, rows, cols, half = self.args
        copies, ours = self.copies, self.ours
        low, high = pl.ds(0, half), pl.ds(half, half)
        copies[2].wait_recv()
        add_rows(own.at[1, low, ours], own.at[1, low, ours], by_x.at[1])
        copies[5].start()
        copies[4].wait_recv()
        add_rows(own.at[0, high, :], own.at[0, high, :], by_y)
        copies[6].start()
        copies[3].wait_recv()
        add_rows(own.at[0, low, ours], own.at[0, low, ours], by_x.at[0])
        copies[5].wait_recv()
        add_rows(out.at[low, :], own.at[0, low, ours], last.at[0])
        copies[6].wait_recv()
        add_rows(out.at[high, :], own.at[0, high, ours], last.at[1])
        for copy in copies:
            copy.wait_send()


def tp_fold_scratch(rows, cols, halves):
    return [
        pltpu.VMEM((2, rows, cols * halves), BF),
        pltpu.VMEM((2, rows // 2, cols), BF),
        pltpu.VMEM((rows // 2, cols * halves), BF),
        pltpu.VMEM((2, rows // 2, cols), BF),
        DMA((7,)), DMA((7,)),
    ]


class TpFold:
    def __init__(self, parts, out, scratch, i, m):
        mate, by_x, by_y, last, send, recv = scratch
        rows, cols = out.shape
        half = rows // 2
        core, across, along = tp_peers(i, m)
        sems = (send, recv)
        mate, by_x, last = [[v[k] if isinstance(v, list) else v.at[k] for k in range(2)] for v in (mate, by_x, last)]

        def seq(a):
            return parts.at[at(a * rows, rows), :]

        def piece(a, part, b):
            return parts.at[at(a * rows + part * half, half), at(b * cols, cols)]

        far = flip(i, 2)
        self.mine = [seq(i), seq(far)]
        self.copies = [
            remote(seq(flip(i, 3)), mate[1], sems, 0, core),
            remote(seq(flip(i, 1)), mate[0], sems, 1, core),
            remote(piece(far, 0, 1 - m), by_x[1], sems, 2, across),
            remote(piece(i, 0, 1 - m), by_x[0], sems, 3, across),
            remote(parts.at[at(far * rows + half, half), :], by_y, sems, 4, along),
            remote(piece(far, 0, m), last[0], sems, 5, along),
            remote(piece(i, 1, 1 - m), last[1], sems, 6, across),
        ]
        self.low_far, self.low, self.high = piece(far, 0, m), piece(i, 0, m), piece(i, 1, m)
        self.high_all = parts.at[at(i * rows + half, half), :]
        self.mate, self.by_x, self.by_y, self.last, self.out, self.half = mate, by_x, by_y, last, out, half

    def send(self, k):
        self.copies[k].start()

    def side(self, k):
        self.copies[1 - k].wait_recv()
        add_rows(self.mine[k], self.mine[k], self.mate[k])
        for n in ((2, 4) if k == 1 else (3,)):
            self.copies[n].start()

    def finish(self, meanwhile=None):
        copies, half = self.copies, self.half
        copies[2].wait_recv()
        add_rows(self.low_far, self.low_far, self.by_x[1])
        copies[5].start()
        copies[4].wait_recv()
        add_rows(self.high_all, self.high_all, self.by_y)
        copies[6].start()
        if meanwhile is not None:
            meanwhile()
        copies[3].wait_recv()
        add_rows(self.low, self.low, self.by_x[0])
        copies[5].wait_recv()
        add_rows(self.out.at[pl.ds(0, half), :], self.low, self.last[0])
        copies[6].wait_recv()
        add_rows(self.out.at[pl.ds(half, half), :], self.high, self.last[1])

    def wait_sends(self):
        for copy in self.copies:
            copy.wait_send()


def pick(step, i):
    return jnp.where(step == 0, flip(i, 3), jnp.where(step == 1, flip(i, 2), jnp.where(step == 2, flip(i, 1), i)))


class LineGather:
    def __init__(self, own, full, sems, base, groups, t, near=None):
        self.near = near
        self.own, self.full, self.sems, self.base, self.groups, self.t = own, full, sems, base, groups, t
        self.rows = full.shape[0] // groups

    def block(self, b):
        return self.full.at[at(b * self.rows, self.rows), :]

    def go(self, b, k, step, own=False):
        n = self.base + (0 if step > 0 else self.groups - 1) + k
        src = self.own if own else self.block(b)
        if self.near is not None and k == 1:
            src = self.near[0 if step > 0 else 1]
        return remote(src, self.block(b), self.sems, n, {"t": self.t + step})

    def send(self, k):
        t, last = self.t, self.groups - 1

        @pl.when((t < last) & (t - k >= 0))
        def _():
            self.go(t - k, k, 1, k == 0).start()

        @pl.when((t > 0) & (t + k <= last))
        def _():
            self.go(t + k, k, -1, k == 0).start()

    def arrive(self, k):
        t, last = self.t, self.groups - 1

        @pl.when(t - k - 1 >= 0)
        def _():
            self.go(t - k - 1, k, 1).wait_recv()

        @pl.when(t + k + 1 <= last)
        def _():
            self.go(t + k + 1, k, -1).wait_recv()

    def pass_on(self, k):
        if self.near is None or k > 1:
            self.arrive(k - 1)
        if k < self.groups - 1:
            self.send(k)

    def wait_sends(self):
        t, last = self.t, self.groups - 1
        for k in range(0 if self.near is None else 1, self.groups - 1):
            @pl.when((t < last) & (t - k >= 0))
            def _():
                self.go(t - k, k, 1, k == 0).wait_send()

            @pl.when((t > 0) & (t + k <= last))
            def _():
                self.go(t + k, k, -1, k == 0).wait_send()


class LineReduce:
    def __init__(self, grads, ups, downs, back, stage, spare, load, sems, base, move_sems, t, i, before, early=None):
        self.grads, self.ups, self.downs, self.back, self.stage, self.spare = grads, ups, downs, back, stage, spare
        self.load, self.sems, self.base, self.move_sems = load, sems, base, move_sems
        self.t, self.i, self.before, self.early = t, i, before, early

    def up(self, k, src):
        return remote(src, self.ups.at[k], self.sems, self.base + k, {"t": self.t + 1})

    def down(self, k, src):
        return remote(src, self.downs.at[k], self.sems, self.base + 3 + k, {"t": self.t - 1})

    def first(self, b):
        if b > 0:
            @pl.when(self.t == 0)
            def _():
                self.up(3 - b, self.grads.at[b]).start()
        if b < 3:
            @pl.when(self.t == 3)
            def _():
                self.down(b, self.grads.at[b]).start()

    def total(self, place, sources):
        loads = [pltpu.make_async_copy(sources[0], self.stage.at[place], self.load.at[0])]
        loads += [pltpu.make_async_copy(v, self.spare, self.load.at[1]) for v in sources[1:]]
        loads[0].start()
        loads[1].start()
        loads[0].wait()
        for n, copy in enumerate(loads[1:]):
            if n > 0:
                copy.start()
            copy.wait()
            add_rows(self.stage.at[place], self.stage.at[place], self.spare)

    def relay(self, place, way, k):
        make = self.up if way == "up" else self.down
        slots = self.ups if way == "up" else self.downs
        if self.early is not None and place == 0:
            slots = self.early[0 if way == "up" else 1]
        else:
            make(k, slots.at[k]).wait_recv()
        self.total(place, [slots.at[k], self.grads.at[3 - k if way == "up" else k]])
        make(k, self.stage.at[place]).start()

    def relayed(self, place, way, k):
        (self.up if way == "up" else self.down)(k, self.stage.at[place]).wait_send()

    PLAN = {1: ((0, "up", 0), (1, "up", 1), (2, "down", 0)), 2: ((0, "down", 0), (1, "up", 0), (2, "down", 1))}

    def hop(self, places):
        for t, plan in self.PLAN.items():
            @pl.when(self.t == t)
            def _():
                for place, way, k in plan:
                    if place in places:
                        if self.before is not None:
                            self.before.relayed(place, way, k)
                        self.relay(place, way, k)

    def moves(self):
        lanes = self.stage.shape[2] // 4
        found = []
        for j in (2, 3, 1):
            p = flip(self.i, j)
            view = self.stage.at[3, :, at(p * lanes, lanes)]
            found.append(remote(view, self.back.at[self.i], self.move_sems, self.base // 6 * 4 + j, {"i": p}))
        view = self.stage.at[3, :, at(self.i * lanes, lanes)]
        return found, pltpu.make_async_copy(view, self.back.at[self.i], self.load.at[2])

    def close(self):
        if self.before is not None:
            self.before.closed()
        for t in range(4):
            @pl.when(self.t == t)
            def _():
                sources = [self.grads.at[t]]
                if t > 0:
                    self.up(3 - t, self.ups.at[3 - t]).wait_recv()
                    sources.append(self.ups.at[3 - t])
                if t < 3:
                    self.down(t, self.downs.at[t]).wait_recv()
                    sources.append(self.downs.at[t])
                self.total(3, sources)

        found, keep = self.moves()
        for move in found:
            move.start()
        keep.start()

    def closed(self):
        found, keep = self.moves()
        for move in found:
            move.wait()
        keep.wait()

    def wait_firsts(self, ks=(0, 1, 2)):
        @pl.when(self.t == 0)
        def _():
            for k in ks:
                self.up(k, self.grads.at[3 - k]).wait_send()

        @pl.when(self.t == 3)
        def _():
            for k in ks:
                self.down(k, self.grads.at[k]).wait_send()

    def wait_early(self):
        @pl.when(self.t == 1)
        def _():
            self.up(0, self.ups.at[0]).wait_recv()

        @pl.when(self.t == 2)
        def _():
            self.down(0, self.downs.at[0]).wait_recv()

    def wait_relays(self):
        for t, plan in self.PLAN.items():
            @pl.when(self.t == t)
            def _():
                for place, way, k in plan:
                    self.relayed(place, way, k)


def tp_group(i, m):
    return list(tp_peers(i, m))


def row_loop(rows, step=64):
    def wrap(f):
        @pl.loop(0, rows, step=step)
        def _(r):
            f(pl.ds(pl.multiple_of(r, step), step))

    return wrap


def mlp_kernel(groups, two_full, grad_full, first_w, other_w, near_w, middle, stat, cot, gain_rows,
               rest_w, grads, ups, downs, next_up, next_down, back, out_parts, d_middle, d_gain, piece, *scratch):
    (x, g, w, act, act_t, fresh, stage, spare, sums, other, load, z_send, z_recv,
     r_send, r_recv, m_send, m_recv, f_send, f_recv, s_send, s_recv, free) = scratch
    t, i, m = lax.axis_index("t"), lax.axis_index("i"), lax.axis_index("m")
    others = [{"i": flip(i, j)} for j in (1, 2, 3)]
    meet(others + [{"m": 1 - m}] + [{"t": flip(t, j)} for j in (1, 2, 3)])
    tokens, wide = x.shape
    rows, part = middle.shape
    unit = w.shape[2] // 3
    gain = gain_rows[1:2, at(m * part, part)]
    two, three = 2 * unit, 3 * unit
    block = wide // groups
    sems = (z_send, z_recv)
    lines = [
        LineGather(other_w.at[c], rest_w.at[c], sems, 6 * c, groups, t, [near_w.at[0], near_w.at[1]] if c == 0 else None)
        for c in range(2)
    ]
    lines[0].pass_on(1)
    lines[1].send(0)
    take_g = pltpu.make_async_copy(grad_full, g, load.at[3])
    take_x = pltpu.make_async_copy(two_full, x, load.at[8])
    take_w = [pltpu.make_async_copy(first_w.at[c], w.at[c], load.at[4 + c]) for c in range(2)]
    own = [
        pltpu.make_async_copy(other_w.at[c], w.at[2 + c, at(t * block, block), :], load.at[6 + c]) for c in range(2)
    ]

    def rest(c):
        spans = [at(flip(t, j) * block, block) for j in (1, 2, 3)]
        return [
            pltpu.make_async_copy(rest_w.at[c, span, :], w.at[2 + c, span, :], load.at[9 + 3 * c + j])
            for j, span in enumerate(spans)
        ]

    def fetch(c):
        for j, copy in enumerate(rest(c)):
            if c == 1:
                copy.start()
                continue
            b = flip(t, j + 1)
            span = at(b * block, block)
            for step, side in ((-1, 0), (1, 1)):
                @pl.when(b == t + step)
                def _():
                    pltpu.make_async_copy(near_w.at[side], w.at[2, span, :], load.at[9 + j]).start()

            @pl.when((b != t - 1) & (b != t + 1))
            def _():
                copy.start()

    first = [take_w[0], take_x, take_g, take_w[1]] + own
    for copy in first:
        copy.start()
    for copy in first:
        copy.wait()
    reds = []
    for c in range(2):
        reds.append(LineReduce(
            grads.at[c], ups.at[c], downs.at[c], back.at[c], stage, spare, load, (r_send, r_recv), 6 * c,
            (m_send, m_recv), t, i, reds[-1] if reds else None))
    ahead = LineReduce(grads.at[2], next_up, next_down, None, stage, spare, load, (r_send, r_recv), 12,
                       (m_send, m_recv), t, i, None)
    order = (3, 0, 2, 1)
    events = {
        (1, 0): lambda: lines[0].pass_on(2),
        (1, 4): lambda: lines[1].pass_on(1),
        (1, 7): lambda: (lines[0].pass_on(3), fetch(0), reds[0].hop((0,))),
        (2, 7): lambda: (lines[1].pass_on(2), reds[0].hop((1, 2)), lines[1].pass_on(3), fetch(1)),
        (3, 0): lambda: reds[0].close(),
        (3, 4): lambda: reds[1].hop((0,)),
    }

    def hook(c, slot):
        for (when_c, when_slot), run in events.items():
            if when_slot == slot:
                @pl.when(c == when_c)
                def _():
                    run()

    def stored(c, n):
        return pltpu.make_async_copy(fresh.at[n % 2], grads.at[c, order[n]], load.at[15 + n % 2])

    @pl.loop(0, 4)
    def _(c):
        for n in range(2):
            @pl.when(c == 2 + n)
            def _():
                for copy in rest(n):
                    copy.wait()

        for n in range(4):
            span = pl.ds(n * rows, rows)
            d_inner = nn(g[span, :], w[c, :, two:three])
            both = nn(x[span, :], w[c, :, 0:two])
            gate, up = both[:, :unit], both[:, unit:]
            sig = jax.nn.sigmoid(gate)
            silu = gate * sig
            d_gate = (d_inner * up * sig * (1.0 + gate * (1.0 - sig))).astype(BF)
            d_up = (d_inner * silu).astype(BF)
            inner = (silu * up).astype(BF)
            for k, v in enumerate((d_gate, d_up, inner)):
                act[c, span, k * unit:(k + 1) * unit] = v
                act_t[k * unit:(k + 1) * unit, span] = v.T
            hook(c, n)
        for n in range(4):
            cols = pl.ds(order[n] * block, block)
            fresh[n % 2, 0:two, :] = nn(act_t[0:two, :], x[:, cols]).astype(BF)
            fresh[n % 2, two:three, :] = nn(act_t[two:three, :], g[:, cols]).astype(BF)
            stored(c, n).start()
            for done in ((n - 1,) if n < 3 else (2, 3)):
                if done >= 0:
                    stored(c, done).wait()
                    for q in range(2):
                        @pl.when(c == q)
                        def _():
                            reds[q].first(order[done])

                    if done < 2:
                        @pl.when(c == 2)
                        def _():
                            ahead.first(order[done])
            hook(c, 4 + n)

    for peer in tp_group(i, m):
        pl.semaphore_signal(free, inc=1, device_id=peer, device_id_type=MESH)
    quarter, half = rows // 2, part
    base = 2 * rows
    lists = [
        [g.at[pl.ds(0, rows), :], g.at[pl.ds(rows, rows), :]],
        [g.at[pl.ds(base, quarter), pl.ds(k * half, half)] for k in range(2)],
        g.at[pl.ds(base + quarter, quarter), :],
        [g.at[pl.ds(base + 2 * quarter, quarter), pl.ds(k * half, half)] for k in range(2)],
    ]
    fold = TpFold(x, d_middle, lists + [f_send, f_recv], i, m)

    def product(span, cols, low, high):
        total = nt(act[0, span, low:high], w[0, cols, low:high])
        for c in range(1, 4):
            total += nt(act[c, span, low:high], w[c, cols, low:high])
        return total.astype(BF)

    def tiles(f):
        @pl.loop(0, wide, step=512)
        def _(col):
            f(pl.ds(pl.multiple_of(col, 512), 512))

    @pl.loop(0, 4)
    def _(step):
        span = at(pick(step, i) * rows, rows)

        @tiles
        def _(cols):
            x[span, cols] = product(span, cols, 0, two)

        @pl.when(step == 0)
        def _():
            pl.semaphore_wait(free, 3)
            fold.send(0)

        @pl.when(step == 1)
        def _():
            fold.side(1)
            reds[1].hop((1, 2))

        @pl.when(step == 2)
        def _():
            fold.send(1)

    fold.side(0)

    def project(first):
        @pl.loop(first, first + 2)
        def _(s):
            span = at(s * rows, rows)

            @tiles
            def _(cols):
                act_t[0:rows, cols] = product(span, cols, two, three)

            put = pltpu.make_async_copy(act_t.at[pl.ds(0, rows), :], out_parts.at[span, :], load.at[15])
            put.start()
            put.wait()

    project(0)
    fold.finish(lambda: (project(2), reds[1].close()))
    d_gain[...] = jnp.zeros_like(d_gain)

    @row_loop(rows)
    def _(span):
        dn, v, r = d_middle[span, :], middle[span, :], stat[span, :]
        sums[span, :] = jnp.broadcast_to(jnp.sum(dn * gain * v, axis=-1, keepdims=True), r.shape)
        d_gain[0:1, :] += jnp.sum(dn * v * r[:, :1], axis=0, keepdims=True)

    swap = remote(sums, other, (s_send, s_recv), 0, {"m": 1 - m})
    swap.start()
    swap.wait()

    @row_loop(rows)
    def _(span):
        r = stat[span, :]
        factor = (r * r * r * ((sums[span, :] + other[span, :]) / wide))[:, :1]
        d = cot[span, :].astype(F32) + r[:, :1] * (d_middle[span, :] * gain) - middle[span, :] * factor
        d_middle[span, :] = d
        piece[span, :] = d.astype(BF)

    fold.wait_sends()
    for line in lines:
        line.wait_sends()
    ahead.wait_early()
    ahead.wait_firsts((0,))
    for red in reds:
        red.wait_firsts()
    reds[1].wait_relays()
    reds[1].closed()


def shape(dims, dtype):
    return jax.ShapeDtypeStruct(dims, dtype)


def comm_call(kernel, ins, outs, scratch, number):
    return pl.pallas_call(
        kernel,
        out_shape=[s for s, _ in outs],
        in_specs=ins,
        out_specs=[b for _, b in outs],
        scratch_shapes=scratch,
        compiler_params=pltpu.CompilerParams(
            collective_id=number, has_side_effects=True, vmem_limit_bytes=LIMIT
        ),
    )


def allow(cut, q0, qn, kn):
    q = q0 + lax.broadcasted_iota(jnp.int32, (qn, kn), 0)
    k = lax.broadcasted_iota(jnp.int32, (qn, kn), 1)
    doc_q = (q >= cut[0]).astype(jnp.int32) + (q >= cut[1]).astype(jnp.int32)
    doc_k = (k >= cut[0]).astype(jnp.int32) + (k >= cut[1]).astype(jnp.int32)
    return (doc_q == doc_k) & (k <= q)


def turn(v):
    half = v.shape[1] // 2
    return jnp.concatenate([-v[:, half:], v[:, :half]], axis=1)


def turn_back(v):
    half = v.shape[1] // 2
    return jnp.concatenate([v[:, half:], -v[:, :half]], axis=1)


def fore_kernel(groups, heads, hd, cuts, w_query, w_key, w_value, w_out, gain_a, gain_b, gate, up, w_down, hidden,
                cot, gain_q, gain_k, table, attn, first_w, other_w, near_w, normed_out, pre, qkv, stats, mixed, middle, stat, two_full, grad_full,
                gain_rows,
                *scratch):
    fold_scratch, (full, weights, pack, down, marks, piece, other, load, c_send, c_recv, w_send, w_recv, w_local, z_send, z_recv,
                   g_send, g_recv, g_local, s_send, s_recv) = scratch[:6], scratch[6:]
    x = full
    t, i, m = lax.axis_index("t"), lax.axis_index("i"), lax.axis_index("m")
    rows, wide = hidden.shape[0], x.shape[1]
    nq, kv = heads * hd, (heads + 2) * hd
    shard = pack.shape[1]
    unit = first_w.shape[2] // 3
    others = [{"i": flip(i, j)} for j in (1, 2, 3)]
    away = [(a, b) for a in range(4) for b in range(4) if a + b > 0]
    places = {(a, b): {"t": flip(t, a) if a else t, "i": flip(i, b) if b else i} for a, b in away}
    meet([{"m": 1 - m}] + [places[ab] for ab in away])
    for p in range(4):
        pack[p, :, 0:nq] = w_query[:, p * nq:(p + 1) * nq]
        pack[p, :, nq:nq + hd] = w_key[:, p * hd:(p + 1) * hd]
        pack[p, :, nq + hd:kv] = w_value[:, p * hd:(p + 1) * hd]
        pack[p, :, kv:kv + nq] = w_out[p * nq:(p + 1) * nq, :].T
    mine = attn.at[at((t * 4 + i) * shard, shard), :]
    spread = [remote(pack.at[flip(i, j)], mine, (w_send, w_recv), j - 1, others[j - 1]) for j in (2, 3, 1)]
    own = pltpu.make_async_copy(pack.at[i], mine, w_local.at[0])
    for copy in spread:
        copy.start()
    own.start()
    gather_h = TpGather(hidden, full, (g_send, g_recv, g_local), 0, i, m, True)
    gather_g = TpGather(cot, grad_full, (g_send, g_recv, g_local), 8, i, m, True)
    gather_h.start()
    here = t * 4 + i
    marks[here] = jnp.concatenate([gain_a[...], gain_b[...], jnp.zeros((14, shard), BF)], axis=0)
    mark = [remote(marks.at[here], marks.at[here], (c_send, c_recv), 4 * a + b, places[(a, b)]) for a, b in away]
    for copy in mark:
        copy.start()
    for r in range(0, w_down.shape[0], 512):
        down[:, r:r + 512] = w_down[r:r + 512, :].T
    gq, gk = gain_q[...].astype(F32), gain_k[...].astype(F32)

    def chunk(c):
        if c < 2:
            place = first_w.at[c, at((t * 4 + i) * shard, shard), :]
        else:
            place = other_w.at[c - 2, at(i * shard, shard), :]
        found, kept = [], []
        for n, src in enumerate((gate, up, down)):
            dst = place.at[:, pl.ds(n * unit, unit)]

            def view(p):
                return src.at[:, at(p * 4 * unit + c * unit, unit)]

            for j in (2, 3, 1):
                found.append(remote(view(flip(i, j)), dst, (w_send, w_recv), 3 + 9 * c + 3 * n + j - 1, others[j - 1]))
            kept.append(pltpu.make_async_copy(view(i), dst, w_local.at[1 + 3 * c + n]))
        return found, kept

    chunks = [chunk(c) for c in range(4)]

    def begin(c):
        for copy in chunks[c][0] + chunks[c][1]:
            copy.start()

    def landed(c):
        for copy in chunks[c][0]:
            copy.wait_recv()
        for copy in chunks[c][1]:
            copy.wait()

    sems = (z_send, z_recv)
    block = 4 * shard
    line = LineGather(attn.at[at(t * block, block), :], attn, sems, 0, groups, t)
    lines = [
        LineGather(first_w.at[c, at(t * block, block), :], first_w.at[c], sems, 6 * c + 6, groups, t) for c in range(2)
    ]
    above = remote(other_w.at[0], near_w.at[0], sems, 18, {"t": t + 1})
    below = remote(other_w.at[0], near_w.at[1], sems, 19, {"t": t - 1})

    def near_start():
        @pl.when(t < groups - 1)
        def _():
            above.start()

        @pl.when(t > 0)
        def _():
            below.start()

    own.wait()
    for copy in spread:
        copy.wait_recv()
    line.send(0)
    begin(0)
    lane = lax.rem(lax.broadcasted_iota(jnp.int32, (1, hd), 1), hd // 2).astype(F32)
    freqs = jnp.exp(lane * (-math.log(1000000.0) * 2.0 / hd))

    @pl.loop(0, 4)
    def _(s):
        c1, c2 = cuts[t * 4 + s, 0], cuts[t * 4 + s, 1]
        position = lax.broadcasted_iota(jnp.int32, (rows, hd), 0)
        start = jnp.where(position >= c2, c2, jnp.where(position >= c1, c1, 0))
        angle = (position - start).astype(F32) * freqs
        table[at(s * rows, rows), 0:hd] = jnp.cos(angle)
        table[at(s * rows, rows), hd:2 * hd] = jnp.sin(angle)

    line.pass_on(1)
    gather_h.relay()
    begin(1)
    line.pass_on(2)
    gather_h.relay_far()
    gather_g.start()
    begin(2)
    begin(3)
    landed(0)
    lines[0].send(0)
    line.pass_on(3)
    landed(1)
    lines[1].send(0)
    fill = pltpu.make_async_copy(attn, weights, load.at[0])
    fill.start()
    gather_h.finish()
    fill.wait()
    for copy in mark:
        copy.wait()
    for n in range(4 * groups):
        gain_rows[:, n * shard:(n + 1) * shard] = marks[n].astype(F32)[0:8, :]
    gain_two = gain_rows[1:2, at(m * (wide // 2), wide // 2)]
    parts = full
    fold = TpFold(parts, middle, fold_scratch, i, m)

    @pl.loop(0, 4)
    def _(step):
        s = pick(step, i)
        start = s * rows
        def sub(r, size):
            return pl.ds(pl.multiple_of(start + r, size), size)

        cut = (cuts[t * 4 + s, 0], cuts[t * 4 + s, 1])

        @pl.loop(0, rows, step=64)
        def _(r):
            span = sub(r, 64)
            v = x[span, :].astype(F32)
            scale = lax.rsqrt(jnp.mean(v * v, axis=-1, keepdims=True) + EPS)
            stats[span, :] = jnp.broadcast_to(scale, (64, stats.shape[1]))
            x[span, :] = (v * scale * gain_rows[0:1, :]).astype(BF)

        everything = sub(0, rows)
        keep = pltpu.make_async_copy(x.at[everything, :], normed_out.at[everything, :], load.at[1])
        keep.start()
        heads_pre = nn(x[everything, :], weights[:, :kv])
        pre[everything, :] = heads_pre
        c, sn = table[everything, 0:hd], table[everything, hd:2 * hd]
        for h in range(heads + 1):
            lanes = slice(h * hd, (h + 1) * hd)
            n = rms_rows(heads_pre[:, lanes], gq if h < heads else gk)
            qkv[everything, lanes] = (n * c + turn(n) * sn).astype(BF)
        qkv[everything, nq + hd:kv] = heads_pre[:, nq + hd:kv].astype(BF)
        half = rows // 2
        for b in range(2):
            kn = (b + 1) * half
            span = sub(b * half, half)
            mask = allow(cut, b * half, half, kn)
            keys, values = qkv[pl.ds(start, kn), nq:nq + hd], qkv[pl.ds(start, kn), nq + hd:kv]
            for h in range(heads):
                q = qkv[span, h * hd:(h + 1) * hd]
                scores = jnp.where(mask, nt(q, keys) * (hd ** -0.5), -1e30)
                top = jnp.max(scores, axis=-1, keepdims=True)
                e = jnp.exp(scores - top)
                total = jnp.sum(e, axis=-1, keepdims=True)
                probs = (e * (1.0 / total)).astype(BF)
                stats[span, h:h + 1] = top + jnp.log(total)
                mixed[span, h * hd:(h + 1) * hd] = nn(probs, values).astype(BF)

        keep.wait()

        @pl.loop(0, wide, step=512)
        def _(col):
            cols = pl.ds(pl.multiple_of(col, 512), 512)
            parts[everything, cols] = nt(mixed[everything, :], weights[cols, kv:kv + nq]).astype(BF)

        @pl.when(step == 0)
        def _():
            fold.send(0)

        @pl.when(step == 1)
        def _():
            fold.side(1)
            lines[0].pass_on(1)

        @pl.when(step == 2)
        def _():
            fold.send(1)
            lines[1].pass_on(1)
            gather_g.relay()

    fold.side(0)
    lines[0].pass_on(2)
    gather_g.relay_far()
    fold.finish(lambda: (lines[1].pass_on(2), landed(2), near_start()))

    @row_loop(rows)
    def _(span):
        v = middle[span, :] + hidden[span, :].astype(F32)
        middle[span, :] = v
        stat[span, :] = jnp.broadcast_to(jnp.sum(v * v, axis=-1, keepdims=True), stat[span, :].shape)

    swap = remote(stat, other, (s_send, s_recv), 0, {"m": 1 - m})
    swap.start()
    swap.wait()

    @row_loop(rows)
    def _(span):
        r = lax.rsqrt((stat[span, :] + other[span, :]) / wide + EPS)
        stat[span, :] = r
        piece[span, :] = (middle[span, :] * r[:, :1] * gain_two).astype(BF)

    gather = TpGather(piece, two_full, (g_send, g_recv, g_local), 16, i, m)
    gather.start()
    gather_g.finish()
    fold.wait_sends()
    lines[0].pass_on(3)
    landed(3)
    for c in range(4):
        for copy in chunks[c][0]:
            copy.wait_send()
    for copy in spread:
        copy.wait_send()
    gather.relay()
    lines[1].pass_on(3)
    gather.relay_far()
    for one in [line] + lines:
        one.wait_sends()

    @pl.when(t > 0)
    def _():
        above.wait_recv()
        below.wait_send()

    @pl.when(t < groups - 1)
    def _():
        below.wait_recv()
        above.wait_send()

    gather.finish()


def aft_kernel(groups, heads, hd, cuts, piece, normed, out_parts, attn, pre_in, middle, d_middle, qkv_in, stats_in,
               mixed_in, table_in, mlp_grads, early_up, early_down, gain_q, gain_k, hidden, gain_rows, d_gain_two,
               d_input, block_out, back, gains, ups, downs, mlp_back, *scratch):
    fold_scratch, out_scratch = scratch[:6], scratch[6:14]
    (dm, nrm, pre, qkv, stats, mixed, table, weights, res, acc, grads, up_in, down_in, total, d_mix, d_pre, d_kv, qk_sum, sums, other,
     g_in, load, a_send, a_recv, a_local, send, recv, z_send, z_recv, g_send, g_recv, s_send, s_recv,
     local, stage, spare, line_load, r_send, r_recv, m_send, m_recv) = scratch[14:]
    t, i, m = lax.axis_index("t"), lax.axis_index("i"), lax.axis_index("m")
    others = [{"i": flip(i, j)} for j in (1, 2, 3)]
    meet(others + [{"m": 1 - m}] + [{"t": flip(t, j)} for j in (1, 2, 3)])
    rows, wide = hidden.shape[0], dm.shape[1]
    nq, kv = heads * hd, (heads + 2) * hd
    scale = hd ** -0.5
    gain = gain_rows[0:1, at(m * (wide // 2), wide // 2)]
    qk_gain = (gain_q[...].astype(F32), gain_k[...].astype(F32))
    gather = TpGather(piece, dm, (a_send, a_recv, a_local), 0, i, m)
    gather.start()
    reds = []
    for c in range(2):
        reds.append(LineReduce(
            mlp_grads.at[2 + c], ups.at[c], downs.at[c], mlp_back.at[c], stage, spare, line_load, (r_send, r_recv),
            6 * c, (m_send, m_recv), t, i, reds[-1] if reds else None, (early_up, early_down) if c == 0 else None))
    for b in (2, 1):
        reds[0].first(b)
    for b in (3, 0, 2, 1):
        reds[1].first(b)
    reds[0].hop((0,))
    fill = pltpu.make_async_copy(attn, weights, load.at[2])
    fill.start()

    def fetch(step):
        span = at(pick(step, i) * rows, rows)
        return (pltpu.make_async_copy(normed.at[span, :], nrm, load.at[0]),
                *[pltpu.make_async_copy(src.at[span, :], dst, load.at[n]) for n, src, dst in (
                    (1, pre_in, pre), (4, qkv_in, qkv), (5, stats_in, stats),
                    (7, table_in, table))])

    two = TpReduce(out_parts, res, out_scratch, i, m)
    acc[...] = jnp.zeros_like(acc)
    qk_sum[...] = jnp.zeros_like(qk_sum)
    fold = TpFold(dm, d_input, fold_scratch, i, m)
    gather.relay()
    reds[0].hop((1, 2))
    gather.relay_far()
    two.start()
    reds[0].close()
    fill.wait()
    for copy in fetch(0)[1:]:
        copy.start()
    gather.finish()

    block = wide // groups
    spans = (slice(0, kv), slice(kv, kv + nq))

    def settle(which):
        for b in range(groups):
            grads[b, spans[which], :] = acc[spans[which], b * block:(b + 1) * block].astype(BF)

    def up(k, src, which):
        dst = up_in.at[k, spans[which], :]
        return remote(src, dst, (z_send, z_recv), 8 * which + k, {"t": t + 1})

    def down(k, src, which):
        dst = down_in.at[k, spans[which], :]
        return remote(src, dst, (z_send, z_recv), 8 * which + 4 + k, {"t": t - 1})

    def own_grads(b, which):
        return grads.at[b, spans[which], :]

    def begin(which):
        @pl.when(t == 0)
        def _():
            for k in range(groups - 1):
                up(k, own_grads(groups - 1 - k, which), which).start()

        @pl.when(t == groups - 1)
        def _():
            for k in range(groups - 1):
                down(k, own_grads(k, which), which).start()

    @pl.loop(0, 4)
    def _(s):
        span = at(s * rows, rows)
        take = pltpu.make_async_copy(mixed_in.at[span, :], mixed, load.at[6])
        take.start()
        take.wait()

        @pl.loop(0, wide, step=512)
        def _(col):
            cols = pl.ds(pl.multiple_of(col, 512), 512)
            acc[kv:kv + nq, cols] += tn(mixed[...], dm[span, cols])

    settle(1)
    begin(1)

    @pl.loop(0, 4)
    def _(step):
        s = pick(step, i)
        start = s * rows
        fetch(step)[0].start()

        def sub(r, size):
            return pl.ds(pl.multiple_of(start + r, size), size)

        cut = (cuts[t * 4 + s, 0], cuts[t * 4 + s, 1])
        everything = sub(0, rows)
        d_mix[...] = nn(dm[everything, :], weights[:, kv:kv + nq]).astype(BF)
        d_kv[...] = jnp.zeros_like(d_kv)
        half = rows // 2

        def undo(h, grad):
            lanes = slice(h * hd, (h + 1) * hd)
            row = 0 if h < heads else 1
            c, sn = table[:, 0:hd], table[:, hd:2 * hd]
            u = c * grad + turn_back(sn * grad)
            v = pre[:, lanes]
            r = lax.rsqrt(jnp.mean(v * v, axis=-1, keepdims=True) + EPS)
            qk_sum[0:1, row * hd:(row + 1) * hd] += jnp.sum(u * v * r, axis=0, keepdims=True)
            scaled = u * qk_gain[row]
            undone = r * scaled - v * (r * r * r) * jnp.mean(scaled * v, axis=-1, keepdims=True)
            d_pre[:, lanes] = undone.astype(BF)

        for copy in fetch(step)[1:]:
            copy.wait()
        for h in range(heads):
            lanes = slice(h * hd, (h + 1) * hd)
            found = []
            for b in range(2):
                kn = (b + 1) * half
                span = slice(b * half, kn)
                mask = allow(cut, b * half, half, kn)
                keys, values = qkv[0:kn, nq:nq + hd], qkv[0:kn, nq + hd:kv]
                q, go = qkv[span, lanes], d_mix[span, lanes]
                scores = jnp.where(mask, nt(q, keys) * scale, -1e30)
                probs = jnp.exp(scores - stats[span, h:h + 1])
                d_probs = nt(go, values)
                inner = jnp.sum(probs * d_probs, axis=-1, keepdims=True)
                d_scores = (probs * (d_probs - inner)).astype(BF)
                found.append(nn(d_scores, keys) * scale)
                d_kv[0:kn, 0:hd] += tn(d_scores, q) * scale
                d_kv[0:kn, hd:2 * hd] += tn(probs.astype(BF), go)
            undo(h, jnp.concatenate(found, axis=0))
        undo(heads, d_kv[:, 0:hd])
        d_pre[:, nq + hd:kv] = d_kv[:, hd:2 * hd].astype(BF)

        @pl.when(step < 3)
        def _():
            for copy in fetch(step + 1)[1:]:
                copy.start()

        fetch(step)[0].wait()

        @pl.loop(0, wide, step=512)
        def _(col):
            cols = pl.ds(pl.multiple_of(col, 512), 512)
            acc[0:kv, cols] += tn(d_pre[...], nrm[:, cols])
            dm[everything, cols] = nt(d_pre[...], weights[cols, 0:kv]).astype(BF)

        @pl.when(step == 0)
        def _():
            fold.send(0)
            two.fold_pair()
            reds[1].hop((0,))

        @pl.when(step == 1)
        def _():
            fold.side(1)
            reds[1].hop((1, 2))

        @pl.when(step == 2)
        def _():
            fold.send(1)

        @pl.when(step == 3)
        def _():
            fold.side(0)

    settle(0)
    begin(0)
    part = hidden.shape[1]
    kept = [acc.at[pl.ds(0, rows), pl.ds(n * part, part)] for n in range(2)]
    takes = [pltpu.make_async_copy(src, kept[n], load.at[2 + n]) for n, src in enumerate((middle, d_middle))]
    for take in takes:
        take.start()

    def hop(places, which):
        for at_t, plan in LineReduce.PLAN.items():
            @pl.when(t == at_t)
            def _():
                for place, way, n in plan:
                    if place in places:
                        make, slots = (up, up_in) if way == "up" else (down, down_in)
                        slot = slots.at[n, spans[which], :]
                        make(n, slot, which).wait_recv()
                        add_rows(slot, slot, own_grads(groups - 1 - n if way == "up" else n, which))
                        make(n, slot, which).start()

    hop((0,), 1)
    reds[1].close()
    for take in takes:
        take.wait()
    hop((1, 2), 1)
    fold.finish(lambda: hop((0,), 0))
    gains[...] = jnp.zeros_like(gains)
    own_half = at(m * (wide // 2), wide // 2)
    gains[1:2, own_half] = d_gain_two[0:1, :]
    gains[2:3, :] = jnp.concatenate([qk_sum[0:1, :]] * (wide // (2 * hd)), axis=1)

    @row_loop(rows)
    def _(span):
        dn, v = d_input[span, :], hidden[span, :].astype(F32)
        r = stats[span, heads:heads + 1]
        sums[span, :] = jnp.broadcast_to(jnp.sum(dn * gain * v, axis=-1, keepdims=True), sums[span, :].shape)
        gains[0:1, own_half] += jnp.sum(dn * v * r, axis=0, keepdims=True)

    swap = remote(sums, other, (s_send, s_recv), 0, {"m": 1 - m})
    swap.start()
    ways = [{"i": flip(i, 1)}, {"m": 1 - m}, {"i": flip(i, 2)}, {"t": flip(t, 1)}, {"t": flip(t, 2)}]

    def trade(k):
        return remote(gains, g_in.at[k], (g_send, g_recv), k, ways[k])

    def give(n):
        trade(n).start()
        trade(n).wait()
        gains[...] += g_in[n]

    give(0)
    swap.wait()

    @row_loop(rows)
    def _(span):
        r = stats[span, heads:heads + 1]
        factor = r * r * r * ((sums[span, :] + other[span, :]) / wide)[:, :1]
        d = kept[1][span, :] + r * (d_input[span, :] * gain)
        d_input[span, :] = d - hidden[span, :].astype(F32) * factor

    give(1)
    hop((1, 2), 0)
    give(2)
    give(3)
    give(4)
    two.fold_links()

    @row_loop(rows)
    def _(span):
        block_out[span, :] = (kept[0][span, :] + res[span, :]).astype(BF)

    for b in range(groups):
        @pl.when(t == b)
        def _():
            for which in (1, 0):
                final = total.at[spans[which], :]
                own = own_grads(b, which)
                if b > 0:
                    slot = up_in.at[groups - 1 - b, spans[which], :]
                    up(groups - 1 - b, slot, which).wait_recv()
                    add_rows(final, own, slot)
                    own = final
                if b < groups - 1:
                    slot = down_in.at[b, spans[which], :]
                    down(b, slot, which).wait_recv()
                    add_rows(final, own, slot)

    sub_cols = block // 4
    moves = []
    for j in (2, 3, 1):
        view = total.at[:, at(flip(i, j) * sub_cols, sub_cols)]
        moves.append(remote(view, back.at[i], (send, recv), j, others[j - 1]))
    keep = pltpu.make_async_copy(total.at[:, at(i * sub_cols, sub_cols)], back.at[i], local.at[0])
    for move in moves:
        move.start()
    keep.start()
    for which in range(2):
        for k in range(groups - 1):
            @pl.when(t < groups - 1 - k)
            def _():
                up(k, up_in.at[k, spans[which], :], which).wait_send()

            @pl.when(t > k)
            def _():
                down(k, down_in.at[k, spans[which], :], which).wait_send()

    fold.wait_sends()
    reds[0].wait_firsts((1, 2))
    reds[1].wait_firsts()
    reds[1].wait_relays()
    reds[1].closed()
    keep.wait()
    for move in moves:
        move.wait()


class Dims:
    def __init__(self, length, part, halves, inner, groups, hd, nq, shard, hidden_units):
        self.length, self.part, self.halves, self.inner, self.groups, self.hd = length, part, halves, inner, groups, hd
        self.nq, self.shard, self.heads, self.kv = nq, shard, nq // hd, nq + 2 * hd
        self.width, self.tokens = part * halves, length * inner
        self.unit, self.block, self.cols = hidden_units // 4, part * halves // groups, nq + 2 * hd + nq

    def values(self):
        return (self.length, self.part, self.halves, self.inner, self.groups, self.hd, self.nq, self.shard,
                self.heads, self.kv, self.width, self.tokens, self.unit, self.block, self.cols)


def call_fore(dims, *args):
    (length, part, halves, inner, groups, hd, nq, shard, heads, kv, width, tokens, unit, block, cols) = dims.values()
    fold_scratch = tp_fold_scratch(length, part, halves)
    return comm_call(
        partial(fore_kernel, groups, heads, hd), [SMEM] + [VMEM] * 13,
        [(shape((tokens, 2 * hd), F32), VMEM), (shape((width, cols), BF), ANY), (shape((2, width, 3 * unit), BF), ANY), (shape((2, block, 3 * unit), BF), ANY),
         (shape((2, block, 3 * unit), BF), ANY),
         (shape((tokens, width), BF), ANY), (shape((tokens, kv), F32), VMEM), (shape((tokens, kv), BF), VMEM),
         (shape((tokens, 128), F32), VMEM), (shape((tokens, nq), BF), VMEM), (shape((length, part), F32), VMEM),
         (shape((length, 128), F32), VMEM), (shape((tokens, width), BF), ANY), (shape((tokens, width), BF), ANY),
         (shape((8, width), F32), VMEM)],
        fold_scratch + [
            pltpu.VMEM((tokens, width), BF), pltpu.VMEM((width, cols), BF), pltpu.VMEM((inner, shard, cols), BF),
            pltpu.VMEM((shard, 4 * inner * unit), BF), pltpu.VMEM((inner * groups, 16, shard), BF),
            pltpu.VMEM((length, part), BF),
            pltpu.VMEM((length, 128), F32), DMA((2,)), DMA((16,)), DMA((16,)),
            DMA((39,)), DMA((39,)), DMA((13,)), DMA((20,)), DMA((20,)),
            DMA((24,)), DMA((24,)), DMA((3,)), DMA((1,)), DMA((1,))], 0,
    )(*args)


def call_mlp(dims, *args):
    (length, part, halves, inner, groups, hd, nq, shard, heads, kv, width, tokens, unit, block, cols) = dims.values()
    return comm_call(
        partial(mlp_kernel, groups), [ANY] * 5 + [VMEM] * 4,
        [(shape((2, width, 3 * unit), BF), ANY), (shape((4, groups, 3 * unit, block), BF), ANY),
         (shape((2, 3, 3 * unit, block), BF), ANY), (shape((2, 3, 3 * unit, block), BF), ANY),
         (shape((1, 3 * unit, block), BF), ANY), (shape((1, 3 * unit, block), BF), ANY),
         (shape((2, inner, 3 * unit, shard), BF), ANY), (shape((tokens, width), BF), ANY),
         (shape((length, part), F32), VMEM), (shape((8, part), F32), VMEM), (shape((length, part), BF), VMEM)],
        [pltpu.VMEM((tokens, width), BF), pltpu.VMEM((tokens, width), BF), pltpu.VMEM((4, width, 3 * unit), BF),
         pltpu.VMEM((4, tokens, 3 * unit), BF), pltpu.VMEM((3 * unit, tokens), BF),
         pltpu.VMEM((2, 3 * unit, block), BF), pltpu.VMEM((4, 3 * unit, block), BF), pltpu.VMEM((3 * unit, block), BF),
         pltpu.VMEM((length, 128), F32), pltpu.VMEM((length, 128), F32), DMA((17,)),
         DMA((12,)), DMA((12,)), DMA((18,)), DMA((18,)), DMA((8,)), DMA((8,)),
         DMA((7,)), DMA((7,)), DMA((1,)), DMA((1,)), pltpu.SemaphoreType.REGULAR], 1,
    )(*args)


def call_aft(dims, *args):
    (length, part, halves, inner, groups, hd, nq, shard, heads, kv, width, tokens, unit, block, cols) = dims.values()
    fold_scratch = tp_fold_scratch(length, part, halves)
    return comm_call(
        partial(aft_kernel, groups, heads, hd), [SMEM] + [ANY] * 14 + [VMEM] * 5,
        [(shape((length, part), F32), VMEM), (shape((length, part), BF), VMEM),
         (shape((inner, nq + kv, block // inner), BF), ANY), (shape((8, width), F32), VMEM),
         (shape((2, 3, 3 * unit, block), BF), ANY), (shape((2, 3, 3 * unit, block), BF), ANY),
         (shape((2, inner, 3 * unit, shard), BF), ANY)],
        fold_scratch + tp_reduce_scratch(length, part, halves) + [
            pltpu.VMEM((tokens, width), BF), pltpu.VMEM((length, width), BF), pltpu.VMEM((length, kv), F32),
            pltpu.VMEM((length, kv), BF), pltpu.VMEM((length, 128), F32), pltpu.VMEM((length, nq), BF),
            pltpu.VMEM((length, 128), F32),
            pltpu.VMEM((width, nq + kv), BF), pltpu.VMEM((length, part), F32), pltpu.VMEM((nq + kv, width), F32),
            pltpu.VMEM((groups, nq + kv, block), BF),
            pltpu.VMEM((groups - 1, nq + kv, block), BF), pltpu.VMEM((groups - 1, nq + kv, block), BF),
            pltpu.VMEM((nq + kv, block), BF), pltpu.VMEM((length, nq), BF), pltpu.VMEM((length, kv), BF),
            pltpu.VMEM((length, 2 * hd), F32), pltpu.VMEM((8, 2 * hd), F32),
            pltpu.VMEM((length, 128), F32), pltpu.VMEM((length, 128), F32), pltpu.VMEM((5, 8, width), F32),
            DMA((8,)), DMA((8,)), DMA((8,)), DMA((1,)),
            DMA((4,)), DMA((4,)), DMA((16,)), DMA((16,)), DMA((5,)), DMA((5,)),
            DMA((1,)), DMA((1,)), DMA((1,)),
            pltpu.VMEM((4, 3 * unit, block), BF), pltpu.VMEM((3 * unit, block), BF), DMA((3,)),
            DMA((12,)), DMA((12,)), DMA((8,)), DMA((8,))], 2,
    )(*args)


def fast_body(
    hidden_in, doc_starts, attn_gain, w_query, w_key, w_value, query_gain, key_gain,
    w_out, mlp_gain, w_gate, w_up, w_down, cotangent, *, groups, inner, halves,
):
    length, part = hidden_in.shape
    shard = w_query.shape[0]
    width, tokens = part * halves, length * inner
    hd = query_gain.shape[0]
    heads = w_query.shape[1] // inner // hd
    nq, kv = heads * hd, (heads + 2) * hd
    hidden_units = w_gate.shape[1] // inner
    t_index, i_index = lax.axis_index("t"), lax.axis_index("i")
    gain_q, gain_k = query_gain[None], key_gain[None]
    dims = Dims(length, part, halves, inner, groups, hd, nq, shard, hidden_units)
    unit = dims.unit
    (table, attn_w, first_w, other_w, near_w, normed_one, pre, qkv, stats, mixed, middle, r_two, two_full, grad_full,
     gain_rows) = call_fore(
        dims, doc_starts, w_query, w_key, w_value, w_out, attn_gain[None], mlp_gain[None], w_gate, w_up, w_down,
        hidden_in, cotangent, gain_q, gain_k)

    (_, mlp_grads, _, _, next_up, next_down, mlp_back, out_parts, d_middle, d_gain_two, d_low) = call_mlp(
        dims, two_full, grad_full, first_w, other_w, near_w, middle, r_two, cotangent, gain_rows)

    d_input, block_out, attn_back, gains_out, _, _, last_back = call_aft(
        dims, doc_starts, d_low, normed_one, out_parts, attn_w, pre, middle, d_middle, qkv, stats, mixed, table, mlp_grads, next_up, next_down, gain_q, gain_k,
        hidden_in, gain_rows, d_gain_two)

    all_back = jnp.concatenate([mlp_back, last_back], axis=0)

    def mlp_columns(first):
        part_of = all_back[:, :, first:first + unit, :]
        return jnp.transpose(part_of, (3, 1, 0, 2)).reshape(shard, inner * hidden_units).astype(F32)

    d_down = jnp.transpose(all_back[:, :, 2 * unit:, :], (1, 0, 2, 3)).reshape(inner * hidden_units, shard).astype(F32)
    own = lax.dynamic_slice(gains_out, (0, (t_index * inner + i_index) * shard), (2, shard))

    def columns(first, last):
        return jnp.moveaxis(attn_back[:, first:last, :], 2, 0).reshape(shard, -1).astype(F32)

    return (
        block_out, d_input, own[0], columns(0, nq), columns(nq, nq + hd), columns(nq + hd, kv),
        gains_out[2, :hd], gains_out[2, hd:2 * hd],
        attn_back[:, kv:kv + nq, :].reshape(inner * nq, shard).astype(F32), own[1],
        mlp_columns(0), mlp_columns(unit), d_down,
    )


def solution(mesh):
    dp, halves = mesh.shape["dp"], mesh.shape["mp"]
    inner = 4
    groups = dp // inner
    fine = Mesh(mesh.devices.reshape(groups, inner, halves), ("t", "i", "m"))
    rows = P(("t", "i"))
    block = P(("t", "i"), "m")
    turned = P("m", ("t", "i"))
    body = fast_body if groups == 4 and halves == 2 else plain_body
    return jax.shard_map(
        partial(body, groups=groups, inner=inner, halves=halves),
        mesh=fine,
        in_specs=(block, P(), rows, block, block, block, P(), P(), turned, rows, block, block, turned, block),
        out_specs=(block, block, rows, block, block, block, P(), P(), turned, rows, block, block, turned),
        check_vma=False,
    )
```

```python
from functools import partial
import math

import jax
import jax.numpy as jnp
from jax import lax
from jax.experimental import pallas as pl
from jax.experimental.pallas import tpu as pltpu
from jax.sharding import Mesh, PartitionSpec as P

BF = jnp.bfloat16
F32 = jnp.float32
EPS = 1e-05
TP = ("i", "m")
ALL = ("t", "i", "m")


def dot_f32(left, right, dims):
    return lax.dot_general(left, right, (dims, ((), ())), preferred_element_type=F32)


def nn(left, right):
    return dot_f32(left, right, ((1,), (0,)))


def nt(left, right):
    return dot_f32(left, right, ((1,), (1,)))


def tn(left, right):
    return dot_f32(left, right, ((0,), (0,)))


def rms_rows(v, gain):
    return v * lax.rsqrt(jnp.mean(v * v, axis=-1, keepdims=True) + EPS) * gain


def tables(cut_row, length, head_dim):
    position = jnp.arange(length, dtype=jnp.int32)
    doc = (position >= cut_row[0]).astype(jnp.int32) + (position >= cut_row[1]).astype(jnp.int32)
    starts = jnp.where(doc == 0, 0, jnp.where(doc == 1, cut_row[0], cut_row[1]))
    places = (position - starts).astype(F32)
    freqs = jnp.exp(-math.log(1000000.0) * 2.0 * jnp.arange(head_dim // 2, dtype=F32) / head_dim)
    angles = places[:, None] * freqs[None, :]
    angles = jnp.concatenate([angles, angles], axis=-1)
    allowed = (doc[:, None] == doc[None, :]) & (position[None, :] <= position[:, None])
    return jnp.cos(angles), jnp.sin(angles), allowed


def rotate(v, cosine, sine_table):
    halfway = v.shape[-1] // 2
    turned = jnp.concatenate([-v[..., halfway:], v[..., :halfway]], axis=-1)
    return v * cosine + turned * sine_table


def head_piece(pre, gain, cosine, sine_table):
    shaped = pre.reshape(pre.shape[0], -1, gain.shape[0])
    return rotate(rms_rows(shaped, gain), cosine, sine_table)


def attend(inputs, scale):
    queries, keys, values, allowed = inputs
    scores = jnp.einsum("qgd,td->gqt", queries, keys, preferred_element_type=F32) * scale
    scores = jnp.where(allowed[None], scores, -1e30)
    highest = jnp.max(scores, axis=-1, keepdims=True)
    weights_exp = jnp.exp(scores - highest)
    totals = jnp.sum(weights_exp, axis=-1, keepdims=True)
    probs = weights_exp / totals
    log_norm = highest[..., 0] + jnp.log(totals[..., 0])
    outputs = jnp.einsum("gqt,td->qgd", probs.astype(BF), values, preferred_element_type=F32)
    return outputs.astype(BF), log_norm


def attend_grad(inputs, scale):
    queries, keys, values, d_outputs, log_norm, allowed = inputs
    scores = jnp.einsum("qgd,td->gqt", queries, keys, preferred_element_type=F32) * scale
    scores = jnp.where(allowed[None], scores, -1e30)
    probs = jnp.exp(scores - log_norm[..., None])
    d_probs = jnp.einsum("qgd,td->gqt", d_outputs, values, preferred_element_type=F32)
    inner_sum = jnp.sum(probs * d_probs, axis=-1, keepdims=True)
    d_scores = (probs * (d_probs - inner_sum)).astype(BF)
    d_queries = jnp.einsum("gqt,td->qgd", d_scores, keys, preferred_element_type=F32) * scale
    d_keys = jnp.einsum("gqt,qgd->td", d_scores, queries, preferred_element_type=F32) * scale
    d_values = jnp.einsum("gqt,qgd->td", probs.astype(BF), d_outputs, preferred_element_type=F32)
    return d_queries, d_keys, d_values


def gather_pieces(piece, ranks):
    rows, cols = piece.shape
    parts = lax.all_gather(piece, TP, axis=0)
    parts = parts.reshape(ranks[0], ranks[1], rows, cols)
    return jnp.moveaxis(parts, 1, 2).reshape(ranks[0] * rows, ranks[1] * cols)


def scatter_pieces(partial_sum, ranks):
    rows, cols = partial_sum.shape
    parts = partial_sum.astype(BF).reshape(ranks[0], rows // ranks[0], ranks[1], cols // ranks[1])
    parts = jnp.moveaxis(parts, 2, 1).reshape(-1, rows // ranks[0], cols // ranks[1])
    mine = lax.psum_scatter(parts, TP, scatter_dimension=0, tiled=False)
    return mine.astype(F32)


def spread(local, inner):
    rows, cols = local.shape
    parts = jnp.moveaxis(local.reshape(rows, inner, cols // inner), 1, 0)
    parts = lax.all_to_all(parts, "i", 0, 0, tiled=False)
    return parts.reshape(inner * rows, cols // inner)


def collect(block, inner):
    rows, cols = block.shape
    parts = lax.all_to_all(block.reshape(inner, rows // inner, cols), "i", 0, 0, tiled=False)
    return jnp.moveaxis(parts, 0, 1).reshape(rows // inner, inner * cols)


def full_rows(local, inner):
    return lax.all_gather(spread(local, inner), "t", axis=0, tiled=True)


def grad_rows(part, inner):
    mine = lax.psum_scatter(part.astype(BF), "t", scatter_dimension=0, tiled=True)
    return collect(mine, inner).astype(F32)


def plain_body(
    hidden_in, doc_starts, attn_gain, w_query, w_key, w_value, query_gain, key_gain,
    w_out, mlp_gain, w_gate, w_up, w_down, cotangent, *, groups, inner, halves,
):
    length, width_part = hidden_in.shape
    ranks = (inner, halves)
    width = width_part * halves
    head_dim = query_gain.shape[0]
    scale = head_dim ** (-0.5)
    t_index, m_index = lax.axis_index("t"), lax.axis_index("m")
    cuts = lax.dynamic_slice_in_dim(doc_starts, t_index * inner, inner, 0)
    cosine, sine_table, allowed = jax.vmap(partial(tables, length=length, head_dim=head_dim))(cuts)
    cosine = cosine.reshape(inner * length, 1, head_dim)
    sine_table = sine_table.reshape(inner * length, 1, head_dim)
    q_gain, k_gain = query_gain.astype(F32), key_gain.astype(F32)
    gains = lax.all_gather(jnp.stack([attn_gain, mlp_gain], 1), ("t", "i"), axis=0, tiled=True)
    gain_one, gain_two = gains[:, 0].astype(F32), gains[:, 1].astype(F32)

    full_in = gather_pieces(hidden_in, ranks)
    sizes = [w.shape[1] // inner for w in (w_query, w_key, w_value)] + [w_out.shape[0] // inner]
    edges = [sum(sizes[:n]) for n in range(5)]

    def by_rank(w):
        return w.reshape(w.shape[0], inner, w.shape[1] // inner)

    attn_local = jnp.concatenate([by_rank(w_query), by_rank(w_key), by_rank(w_value), by_rank(w_out.T)], 2)
    attn_cols = full_rows(attn_local.reshape(attn_local.shape[0], -1), inner)
    query_cols, key_cols, value_cols, out_t = [attn_cols[:, edges[n]:edges[n + 1]] for n in range(4)]
    resid = full_in.astype(F32)
    r_one = lax.rsqrt(jnp.mean(resid * resid, axis=-1, keepdims=True) + EPS)
    normed_one = (resid * r_one * gain_one).astype(BF)
    gate_cols = full_rows(w_gate, inner)
    up_cols = full_rows(w_up, inner)
    down_t = full_rows(w_down.T, inner)
    grad_full = gather_pieces(cotangent, ranks)

    query_pre = nn(normed_one, query_cols)
    key_pre = nn(normed_one, key_cols)
    value_low = nn(normed_one, value_cols).astype(BF)
    query_rot = head_piece(query_pre, q_gain, cosine, sine_table).astype(BF)
    key_rot = head_piece(key_pre, k_gain, cosine, sine_table).astype(BF)
    group = query_rot.shape[1]
    query_stack = query_rot.reshape(inner, length, group, head_dim)
    key_stack = key_rot.reshape(inner, length, head_dim)
    value_stack = value_low.reshape(inner, length, head_dim)
    attended, log_norm = lax.map(partial(attend, scale=scale), (query_stack, key_stack, value_stack, allowed))
    mixed = attended.reshape(inner * length, group * head_dim)
    middle = hidden_in.astype(F32) + scatter_pieces(nt(mixed, out_t), ranks)
    my_gain_one = lax.dynamic_slice_in_dim(gain_one, m_index * width_part, width_part, 0)
    my_gain_two = lax.dynamic_slice_in_dim(gain_two, m_index * width_part, width_part, 0)
    r_two = lax.rsqrt(lax.psum(jnp.sum(middle * middle, axis=-1, keepdims=True), "m") / width + EPS)
    normed_two = gather_pieces((middle * r_two * my_gain_two).astype(BF), ranks)

    gate_pre, up_pre = nn(normed_two, gate_cols), nn(normed_two, up_cols)
    d_inner = nn(grad_full, down_t)
    sigmoid_gate = jax.nn.sigmoid(gate_pre)
    inner_act = (gate_pre * sigmoid_gate * up_pre).astype(BF)
    d_gate_pre = (d_inner * up_pre * sigmoid_gate * (1.0 + gate_pre * (1.0 - sigmoid_gate))).astype(BF)
    d_up_pre = (d_inner * gate_pre * sigmoid_gate).astype(BF)
    d_normed_two = scatter_pieces(nt(d_gate_pre, gate_cols) + nt(d_up_pre, up_cols), ranks)
    mlp_out = scatter_pieces(nt(inner_act, down_t), ranks)
    block_out = (middle + mlp_out).astype(BF)

    scaled = d_normed_two * my_gain_two
    dot_two = lax.psum(jnp.sum(scaled * middle, axis=-1, keepdims=True), "m") / width
    d_gain_two = jnp.sum(d_normed_two * middle * r_two, axis=0)
    d_middle = cotangent.astype(F32) + r_two * scaled - middle * (r_two * r_two * r_two) * dot_two
    d_middle_low = gather_pieces(d_middle.astype(BF), ranks)
    d_gate = grad_rows(tn(normed_two, d_gate_pre), inner)
    d_up = grad_rows(tn(normed_two, d_up_pre), inner)
    d_down = grad_rows(tn(grad_full, inner_act), inner).T

    d_mixed = nn(d_middle_low, out_t).astype(BF)
    d_out_part = tn(d_middle_low, mixed)
    d_mixed_stack = d_mixed.reshape(inner, length, group, head_dim)
    d_query_stack, d_key_stack, d_value_stack = lax.map(
        partial(attend_grad, scale=scale),
        (query_stack, key_stack, value_stack, d_mixed_stack, log_norm, allowed),
    )
    rotary_piece = partial(head_piece, cosine=cosine, sine_table=sine_table)
    _, query_pull = jax.vjp(rotary_piece, query_pre, q_gain)
    d_query_pre, d_qgain_part = query_pull(d_query_stack.reshape(inner * length, group, head_dim))
    _, key_pull = jax.vjp(rotary_piece, key_pre, k_gain)
    d_key_pre, d_kgain_part = key_pull(d_key_stack.reshape(inner * length, 1, head_dim))
    d_heads = jnp.concatenate(
        [d_query_pre, d_key_pre, d_value_stack.reshape(inner * length, head_dim)], 1
    ).astype(BF)
    heads_cols = attn_cols[:, : edges[3]]
    d_normed_one = scatter_pieces(nt(d_heads, heads_cols), ranks)
    d_attn = jnp.concatenate([tn(normed_one, d_heads), d_out_part], 1)
    d_attn = grad_rows(d_attn, inner).reshape(-1, inner, edges[4])
    d_query, d_key, d_value, d_out_t = [
        d_attn[:, :, edges[n]:edges[n + 1]].reshape(d_attn.shape[0], -1) for n in range(4)
    ]
    mine = hidden_in.astype(F32)
    i_index = lax.axis_index("i")
    r_own = lax.dynamic_slice_in_dim(r_one, i_index * length, length, 0)
    scaled = d_normed_one * my_gain_one
    dot_one = lax.psum(jnp.sum(scaled * mine, axis=-1, keepdims=True), "m") / width
    d_gain_one = jnp.sum(d_normed_one * mine * r_own, axis=0)
    d_input = d_middle + r_own * scaled - mine * (r_own * r_own * r_own) * dot_one

    both = jnp.stack([d_gain_one, d_gain_two], 0)
    wide = lax.dynamic_update_slice(jnp.zeros((2, width), F32), both, (0, m_index * width_part))
    small = jnp.concatenate([wide.reshape(-1), d_qgain_part, d_kgain_part])
    small = lax.psum(small, ALL)
    wide = small[: 2 * width].reshape(2, width)
    shard = attn_gain.shape[0]
    own = lax.dynamic_slice(wide, (0, (t_index * inner + i_index) * shard), (2, shard))
    return (
        block_out, d_input, own[0], d_query, d_key, d_value,
        small[2 * width : 2 * width + head_dim], small[2 * width + head_dim :],
        d_out_t.T, own[1], d_gate, d_up, d_down,
    )


MESH = pl.DeviceIdType.MESH
ANY = pl.BlockSpec(memory_space=pl.ANY)
VMEM = pl.BlockSpec(memory_space=pltpu.VMEM)
SMEM = pl.BlockSpec(memory_space=pltpu.SMEM)
DMA = pltpu.SemaphoreType.DMA
LIMIT = 62 * 1024 * 1024


def flip(index, mask):
    if mask == 1:
        return index + 1 - 2 * lax.rem(index, 2)
    if mask == 2:
        return lax.rem(index + 2, 4)
    return 3 - index


def meet(peers):
    barrier = pltpu.get_barrier_semaphore()
    for peer in peers:
        pl.semaphore_signal(barrier, inc=1, device_id=peer, device_id_type=MESH)
    pl.semaphore_wait(barrier, len(peers))


def remote(src, dst, sems, k, peer):
    return pltpu.make_async_remote_copy(
        src_ref=src, dst_ref=dst, send_sem=sems[0].at[k], recv_sem=sems[1].at[k],
        device_id=peer, device_id_type=MESH,
    )


def at(start, size):
    return pl.ds(pl.multiple_of(start, size), size)


def tp_peers(i, m):
    return {"i": flip(i, 1)}, {"m": 1 - m}, {"i": flip(i, 2)}


class TpGather:
    def __init__(self, piece, full, sems, base, i, m, lean=False):
        self.lean = lean
        rows, cols = piece.shape
        half = rows // 2
        core, across, along = tp_peers(i, m)

        def slot(a, b, part=None):
            if part is None:
                return full.at[at(a * rows, rows), at(b * cols, cols)]
            return full.at[at(a * rows + part * half, half), at(b * cols, cols)]

        def go(src, dst, k, peer):
            return remote(src, dst, sems, base + k, peer)

        mine, far = slot(i, m), flip(i, 2)
        self.local = pltpu.make_async_copy(piece, mine, sems[2].at[base // 8])
        self.copies = [
            go(piece, mine, 0, core),
            go(piece, mine, 1, across),
            go(piece, mine, 2, along),
            go(slot(i, 1 - m, 0), slot(i, 1 - m, 0), 3, along),
            go(slot(i, 1 - m), slot(i, 1 - m), 4, core),
            go(slot(far, m, None if lean else 1), slot(far, m, None if lean else 1), 5, across),
            go(slot(far, m), slot(far, m), 6, core),
            go(slot(far, 1 - m), slot(far, 1 - m), 7, core),
        ]

    def start(self):
        for k in (1, 2, 0):
            self.copies[k].start()
        self.local.start()

    def relay(self):
        self.copies[1].wait_recv()
        if not self.lean:
            self.copies[3].start()
        self.copies[4].start()
        self.copies[2].wait_recv()
        self.copies[5].start()
        self.copies[6].start()

    def relay_far(self):
        if not self.lean:
            self.copies[3].wait_recv()
        self.copies[5].wait_recv()
        self.copies[7].start()

    def finish(self):
        for k in (0, 4, 6, 7):
            self.copies[k].wait_recv()
        for k, copy in enumerate(self.copies):
            if k != 3 or not self.lean:
                copy.wait_send()
        self.local.wait()


def add_rows(target, first, second, step=64):
    rows = target.shape[0]

    @pl.loop(0, rows, step=step)
    def _(r):
        span = pl.ds(pl.multiple_of(r, step), step)
        total = first[span, :].astype(F32) + second[span, :].astype(F32)
        target[span, :] = total.astype(target.dtype)


def tp_reduce_scratch(rows, cols, halves):
    return [
        pltpu.VMEM((2, rows, cols * halves), BF),
        pltpu.VMEM((2, rows, cols * halves), BF),
        pltpu.VMEM((2, rows // 2, cols), BF),
        pltpu.VMEM((rows // 2, cols * halves), BF),
        pltpu.VMEM((2, rows // 2, cols), BF),
        DMA((7,)), DMA((7,)), DMA((2,)),
    ]


class TpReduce:
    def __init__(self, parts, out, scratch, i, m):
        own, mate, by_x, by_y, last, send, recv, load = scratch
        rows, cols = out.shape
        half = rows // 2
        core, across, along = tp_peers(i, m)
        sems = (send, recv)
        self.args = (own, mate, by_x, by_y, last, out, m, rows, cols, half)

        def seq(a):
            return parts.at[at(a * rows, rows), :]

        self.loads = [
            pltpu.make_async_copy(seq(flip(i, 2)), own.at[1], load.at[1]),
            pltpu.make_async_copy(seq(i), own.at[0], load.at[0]),
        ]
        theirs = at((1 - m) * cols, cols)
        ours = at(m * cols, cols)
        low, high = pl.ds(0, half), pl.ds(half, half)
        self.copies = [
            remote(seq(flip(i, 3)), mate.at[1], sems, 0, core),
            remote(seq(flip(i, 1)), mate.at[0], sems, 1, core),
            remote(own.at[1, low, theirs], by_x.at[1], sems, 2, across),
            remote(own.at[0, low, theirs], by_x.at[0], sems, 3, across),
            remote(own.at[1, high, :], by_y, sems, 4, along),
            remote(own.at[1, low, ours], last.at[0], sems, 5, along),
            remote(own.at[0, high, theirs], last.at[1], sems, 6, across),
        ]
        self.ours = ours

    def start(self):
        for k in (0, 1):
            self.copies[k].start()
            self.loads[k].start()

    def fold_pair(self):
        own, mate = self.args[:2]
        copies = self.copies
        for side, k in ((1, 0), (0, 1)):
            self.loads[k].wait()
            copies[k].wait_recv()
            add_rows(own.at[side], own.at[side], mate.at[side])
            if side == 1:
                copies[2].start()
                copies[4].start()
            else:
                copies[3].start()

    def fold_links(self):
        own, mate, by_x, by_y, last, out, m, rows, cols, half = self.args
        copies, ours = self.copies, self.ours
        low, high = pl.ds(0, half), pl.ds(half, half)
        copies[2].wait_recv()
        add_rows(own.at[1, low, ours], own.at[1, low, ours], by_x.at[1])
        copies[5].start()
        copies[4].wait_recv()
        add_rows(own.at[0, high, :], own.at[0, high, :], by_y)
        copies[6].start()
        copies[3].wait_recv()
        add_rows(own.at[0, low, ours], own.at[0, low, ours], by_x.at[0])
        copies[5].wait_recv()
        add_rows(out.at[low, :], own.at[0, low, ours], last.at[0])
        copies[6].wait_recv()
        add_rows(out.at[high, :], own.at[0, high, ours], last.at[1])
        for copy in copies:
            copy.wait_send()


def tp_fold_scratch(rows, cols, halves):
    return [
        pltpu.VMEM((2, rows, cols * halves), BF),
        pltpu.VMEM((2, rows // 2, cols), BF),
        pltpu.VMEM((rows // 2, cols * halves), BF),
        pltpu.VMEM((2, rows // 2, cols), BF),
        DMA((7,)), DMA((7,)),
    ]


class TpFold:
    def __init__(self, parts, out, scratch, i, m):
        mate, by_x, by_y, last, send, recv = scratch
        rows, cols = out.shape
        half = rows // 2
        core, across, along = tp_peers(i, m)
        sems = (send, recv)
        mate, by_x, last = [[v[k] if isinstance(v, list) else v.at[k] for k in range(2)] for v in (mate, by_x, last)]

        def seq(a):
            return parts.at[at(a * rows, rows), :]

        def piece(a, part, b):
            return parts.at[at(a * rows + part * half, half), at(b * cols, cols)]

        far = flip(i, 2)
        self.mine = [seq(i), seq(far)]
        self.copies = [
            remote(seq(flip(i, 3)), mate[1], sems, 0, core),
            remote(seq(flip(i, 1)), mate[0], sems, 1, core),
            remote(piece(far, 0, 1 - m), by_x[1], sems, 2, across),
            remote(piece(i, 0, 1 - m), by_x[0], sems, 3, across),
            remote(parts.at[at(far * rows + half, half), :], by_y, sems, 4, along),
            remote(piece(far, 0, m), last[0], sems, 5, along),
            remote(piece(i, 1, 1 - m), last[1], sems, 6, across),
        ]
        self.low_far, self.low, self.high = piece(far, 0, m), piece(i, 0, m), piece(i, 1, m)
        self.high_all = parts.at[at(i * rows + half, half), :]
        self.mate, self.by_x, self.by_y, self.last, self.out, self.half = mate, by_x, by_y, last, out, half

    def send(self, k):
        self.copies[k].start()

    def side(self, k):
        self.copies[1 - k].wait_recv()
        add_rows(self.mine[k], self.mine[k], self.mate[k])
        for n in ((2, 4) if k == 1 else (3,)):
            self.copies[n].start()

    def finish(self, meanwhile=None):
        copies, half = self.copies, self.half
        copies[2].wait_recv()
        add_rows(self.low_far, self.low_far, self.by_x[1])
        copies[5].start()
        copies[4].wait_recv()
        add_rows(self.high_all, self.high_all, self.by_y)
        copies[6].start()
        if meanwhile is not None:
            meanwhile()
        copies[3].wait_recv()
        add_rows(self.low, self.low, self.by_x[0])
        copies[5].wait_recv()
        add_rows(self.out.at[pl.ds(0, half), :], self.low, self.last[0])
        copies[6].wait_recv()
        add_rows(self.out.at[pl.ds(half, half), :], self.high, self.last[1])

    def wait_sends(self):
        for copy in self.copies:
            copy.wait_send()


def pick(step, i):
    return jnp.where(step == 0, flip(i, 3), jnp.where(step == 1, flip(i, 2), jnp.where(step == 2, flip(i, 1), i)))


class LineGather:
    def __init__(self, own, full, sems, base, groups, t, near=None):
        self.near = near
        self.own, self.full, self.sems, self.base, self.groups, self.t = own, full, sems, base, groups, t
        self.rows = full.shape[0] // groups

    def block(self, b):
        return self.full.at[at(b * self.rows, self.rows), :]

    def go(self, b, k, step, own=False):
        n = self.base + (0 if step > 0 else self.groups - 1) + k
        src = self.own if own else self.block(b)
        if self.near is not None and k == 1:
            src = self.near[0 if step > 0 else 1]
        return remote(src, self.block(b), self.sems, n, {"t": self.t + step})

    def send(self, k):
        t, last = self.t, self.groups - 1

        @pl.when((t < last) & (t - k >= 0))
        def _():
            self.go(t - k, k, 1, k == 0).start()

        @pl.when((t > 0) & (t + k <= last))
        def _():
            self.go(t + k, k, -1, k == 0).start()

    def arrive(self, k):
        t, last = self.t, self.groups - 1

        @pl.when(t - k - 1 >= 0)
        def _():
            self.go(t - k - 1, k, 1).wait_recv()

        @pl.when(t + k + 1 <= last)
        def _():
            self.go(t + k + 1, k, -1).wait_recv()

    def pass_on(self, k):
        if self.near is None or k > 1:
            self.arrive(k - 1)
        if k < self.groups - 1:
            self.send(k)

    def wait_sends(self):
        t, last = self.t, self.groups - 1
        for k in range(0 if self.near is None else 1, self.groups - 1):
            @pl.when((t < last) & (t - k >= 0))
            def _():
                self.go(t - k, k, 1, k == 0).wait_send()

            @pl.when((t > 0) & (t + k <= last))
            def _():
                self.go(t + k, k, -1, k == 0).wait_send()


class LineReduce:
    def __init__(self, grads, ups, downs, back, stage, spare, load, sems, base, move_sems, t, i, before, early=None):
        self.grads, self.ups, self.downs, self.back, self.stage, self.spare = grads, ups, downs, back, stage, spare
        self.load, self.sems, self.base, self.move_sems = load, sems, base, move_sems
        self.t, self.i, self.before, self.early = t, i, before, early

    def up(self, k, src):
        return remote(src, self.ups.at[k], self.sems, self.base + k, {"t": self.t + 1})

    def down(self, k, src):
        return remote(src, self.downs.at[k], self.sems, self.base + 3 + k, {"t": self.t - 1})

    def first(self, b):
        if b > 0:
            @pl.when(self.t == 0)
            def _():
                self.up(3 - b, self.grads.at[b]).start()
        if b < 3:
            @pl.when(self.t == 3)
            def _():
                self.down(b, self.grads.at[b]).start()

    def total(self, place, sources):
        loads = [pltpu.make_async_copy(sources[0], self.stage.at[place], self.load.at[0])]
        loads += [pltpu.make_async_copy(v, self.spare, self.load.at[1]) for v in sources[1:]]
        loads[0].start()
        loads[1].start()
        loads[0].wait()
        for n, copy in enumerate(loads[1:]):
            if n > 0:
                copy.start()
            copy.wait()
            add_rows(self.stage.at[place], self.stage.at[place], self.spare)

    def relay(self, place, way, k):
        make = self.up if way == "up" else self.down
        slots = self.ups if way == "up" else self.downs
        if self.early is not None and place == 0:
            slots = self.early[0 if way == "up" else 1]
        else:
            make(k, slots.at[k]).wait_recv()
        self.total(place, [slots.at[k], self.grads.at[3 - k if way == "up" else k]])
        make(k, self.stage.at[place]).start()

    def relayed(self, place, way, k):
        (self.up if way == "up" else self.down)(k, self.stage.at[place]).wait_send()

    PLAN = {1: ((0, "up", 0), (1, "up", 1), (2, "down", 0)), 2: ((0, "down", 0), (1, "up", 0), (2, "down", 1))}

    def hop(self, places):
        for t, plan in self.PLAN.items():
            @pl.when(self.t == t)
            def _():
                for place, way, k in plan:
                    if place in places:
                        if self.before is not None:
                            self.before.relayed(place, way, k)
                        self.relay(place, way, k)

    def moves(self):
        lanes = self.stage.shape[2] // 4
        found = []
        for j in (2, 3, 1):
            p = flip(self.i, j)
            view = self.stage.at[3, :, at(p * lanes, lanes)]
            found.append(remote(view, self.back.at[self.i], self.move_sems, self.base // 6 * 4 + j, {"i": p}))
        view = self.stage.at[3, :, at(self.i * lanes, lanes)]
        return found, pltpu.make_async_copy(view, self.back.at[self.i], self.load.at[2])

    def close(self):
        if self.before is not None:
            self.before.closed()
        for t in range(4):
            @pl.when(self.t == t)
            def _():
                sources = [self.grads.at[t]]
                if t > 0:
                    self.up(3 - t, self.ups.at[3 - t]).wait_recv()
                    sources.append(self.ups.at[3 - t])
                if t < 3:
                    self.down(t, self.downs.at[t]).wait_recv()
                    sources.append(self.downs.at[t])
                self.total(3, sources)

        found, keep = self.moves()
        for move in found:
            move.start()
        keep.start()

    def closed(self):
        found, keep = self.moves()
        for move in found:
            move.wait()
        keep.wait()

    def wait_firsts(self, ks=(0, 1, 2)):
        @pl.when(self.t == 0)
        def _():
            for k in ks:
                self.up(k, self.grads.at[3 - k]).wait_send()

        @pl.when(self.t == 3)
        def _():
            for k in ks:
                self.down(k, self.grads.at[k]).wait_send()

    def wait_early(self):
        @pl.when(self.t == 1)
        def _():
            self.up(0, self.ups.at[0]).wait_recv()

        @pl.when(self.t == 2)
        def _():
            self.down(0, self.downs.at[0]).wait_recv()

    def wait_relays(self):
        for t, plan in self.PLAN.items():
            @pl.when(self.t == t)
            def _():
                for place, way, k in plan:
                    self.relayed(place, way, k)


def tp_group(i, m):
    return list(tp_peers(i, m))


class Swap:
    def __init__(self, stat, other, mini, sems, m):
        self.stat, self.other, self.mini = stat, other, mini
        self.copy = remote(mini.at[0], mini.at[1], sems, 0, {"m": 1 - m})

    def start(self):
        self.mini[0] = jnp.transpose(self.stat[...])[0:8, :]
        self.copy.start()

    def wait(self):
        self.copy.wait()
        self.other[:, 0:8] = jnp.transpose(self.mini[1])


def row_loop(rows, step=64):
    def wrap(f):
        @pl.loop(0, rows, step=step)
        def _(r):
            f(pl.ds(pl.multiple_of(r, step), step))

    return wrap


def mlp_kernel(groups, two_full, grad_full, first_w, other_w, near_w, middle, stat, cot, gain_rows,
               rest_w, grads, ups, downs, next_up, next_down, back, out_parts, d_middle, d_gain, piece, *scratch):
    (x, g, w, act, act_t, fresh, stage, spare, sums, other, mini, load, z_send, z_recv,
     r_send, r_recv, m_send, m_recv, f_send, f_recv, s_send, s_recv, free) = scratch
    t, i, m = lax.axis_index("t"), lax.axis_index("i"), lax.axis_index("m")
    others = [{"i": flip(i, j)} for j in (1, 2, 3)]
    meet(others + [{"m": 1 - m}] + [{"t": flip(t, j)} for j in (1, 2, 3)])
    tokens, wide = x.shape
    rows, part = middle.shape
    unit = w.shape[2] // 3
    gain = gain_rows[1:2, at(m * part, part)]
    two, three = 2 * unit, 3 * unit
    block = wide // groups
    sems = (z_send, z_recv)
    lines = [
        LineGather(other_w.at[c], rest_w.at[c], sems, 6 * c, groups, t, [near_w.at[0], near_w.at[1]] if c == 0 else None)
        for c in range(2)
    ]
    lines[0].pass_on(1)
    lines[1].send(0)
    take_g = pltpu.make_async_copy(grad_full, g, load.at[3])
    take_x = pltpu.make_async_copy(two_full, x, load.at[8])
    take_w = [pltpu.make_async_copy(first_w.at[c], w.at[c], load.at[4 + c]) for c in range(2)]
    own = [
        pltpu.make_async_copy(other_w.at[c], w.at[2 + c, at(t * block, block), :], load.at[6 + c]) for c in range(2)
    ]

    def rest(c):
        spans = [at(flip(t, j) * block, block) for j in (1, 2, 3)]
        return [
            pltpu.make_async_copy(rest_w.at[c, span, :], w.at[2 + c, span, :], load.at[9 + 3 * c + j])
            for j, span in enumerate(spans)
        ]

    def fetch(c):
        for j, copy in enumerate(rest(c)):
            if c == 1:
                copy.start()
                continue
            b = flip(t, j + 1)
            span = at(b * block, block)
            for step, side in ((-1, 0), (1, 1)):
                @pl.when(b == t + step)
                def _():
                    pltpu.make_async_copy(near_w.at[side], w.at[2, span, :], load.at[9 + j]).start()

            @pl.when((b != t - 1) & (b != t + 1))
            def _():
                copy.start()

    first = [take_w[0], take_x, take_g, take_w[1]] + own
    for copy in first:
        copy.start()
    for copy in first:
        copy.wait()
    reds = []
    for c in range(2):
        reds.append(LineReduce(
            grads.at[c], ups.at[c], downs.at[c], back.at[c], stage, spare, load, (r_send, r_recv), 6 * c,
            (m_send, m_recv), t, i, reds[-1] if reds else None))
    ahead = LineReduce(grads.at[2], next_up, next_down, None, stage, spare, load, (r_send, r_recv), 12,
                       (m_send, m_recv), t, i, None)
    order = (3, 0, 2, 1)
    events = {
        (1, 0): lambda: lines[0].pass_on(2),
        (1, 4): lambda: lines[1].pass_on(1),
        (1, 7): lambda: (lines[0].pass_on(3), fetch(0), reds[0].hop((0,))),
        (2, 7): lambda: (lines[1].pass_on(2), reds[0].hop((1, 2)), lines[1].pass_on(3), fetch(1)),
        (3, 4): lambda: reds[1].hop((0,)),
    }

    def hook(c, slot):
        for (when_c, when_slot), run in events.items():
            if when_slot == slot:
                @pl.when(c == when_c)
                def _():
                    run()

    def stored(c, n):
        return pltpu.make_async_copy(fresh.at[n % 2], grads.at[c, order[n]], load.at[15 + n % 2])

    @pl.loop(0, 4)
    def _(c):
        for n in range(2):
            @pl.when(c == 2 + n)
            def _():
                for copy in rest(n):
                    copy.wait()

        for n in range(4):
            span = pl.ds(n * rows, rows)
            d_inner = nn(g[span, :], w[c, :, two:three])
            both = nn(x[span, :], w[c, :, 0:two])
            gate, up = both[:, :unit], both[:, unit:]
            sig = jax.nn.sigmoid(gate)
            silu = gate * sig
            d_gate = (d_inner * up * sig * (1.0 + gate * (1.0 - sig))).astype(BF)
            d_up = (d_inner * silu).astype(BF)
            inner = (silu * up).astype(BF)
            for k, v in enumerate((d_gate, d_up, inner)):
                act[c, span, k * unit:(k + 1) * unit] = v
                act_t[k * unit:(k + 1) * unit, span] = v.T
            hook(c, n)
        for n in range(4):
            cols = pl.ds(order[n] * block, block)
            fresh[n % 2, 0:two, :] = nn(act_t[0:two, :], x[:, cols]).astype(BF)
            fresh[n % 2, two:three, :] = nn(act_t[two:three, :], g[:, cols]).astype(BF)
            stored(c, n).start()
            for done in ((n - 1,) if n < 3 else (2, 3)):
                if done >= 0:
                    stored(c, done).wait()
                    for q in range(2):
                        @pl.when(c == q)
                        def _():
                            reds[q].first(order[done])

                    if done < 2:
                        @pl.when(c == 2)
                        def _():
                            ahead.first(order[done])
            hook(c, 4 + n)

    for peer in tp_group(i, m):
        pl.semaphore_signal(free, inc=1, device_id=peer, device_id_type=MESH)
    quarter, half = rows // 2, part
    base = 2 * rows
    lists = [
        [g.at[pl.ds(0, rows), :], g.at[pl.ds(rows, rows), :]],
        [g.at[pl.ds(base, quarter), pl.ds(k * half, half)] for k in range(2)],
        g.at[pl.ds(base + quarter, quarter), :],
        [g.at[pl.ds(base + 2 * quarter, quarter), pl.ds(k * half, half)] for k in range(2)],
    ]
    fold = TpFold(x, d_middle, lists + [f_send, f_recv], i, m)

    def product(span, cols, low, high):
        total = nt(act[0, span, low:high], w[0, cols, low:high])
        for c in range(1, 4):
            total += nt(act[c, span, low:high], w[c, cols, low:high])
        return total.astype(BF)

    def tiles(f):
        @pl.loop(0, wide, step=512)
        def _(col):
            f(pl.ds(pl.multiple_of(col, 512), 512))

    @pl.loop(0, 4)
    def _(step):
        span = at(pick(step, i) * rows, rows)

        @tiles
        def _(cols):
            x[span, cols] = product(span, cols, 0, two)

        @pl.when(step == 0)
        def _():
            pl.semaphore_wait(free, 3)
            fold.send(0)

        @pl.when(step == 1)
        def _():
            fold.side(1)
            reds[1].hop((1, 2))

        @pl.when(step == 2)
        def _():
            fold.send(1)

    fold.side(0)

    def project(first):
        @pl.loop(first, first + 2)
        def _(s):
            span = at(s * rows, rows)

            @tiles
            def _(cols):
                act_t[0:rows, cols] = product(span, cols, two, three)

            put = pltpu.make_async_copy(act_t.at[pl.ds(0, rows), :], out_parts.at[span, :], load.at[15])
            put.start()
            put.wait()

    reds[0].close()
    project(0)
    fold.finish(lambda: (project(2), reds[1].close()))
    d_gain[...] = jnp.zeros_like(d_gain)

    @row_loop(rows)
    def _(span):
        dn, v, r = d_middle[span, :], middle[span, :], stat[span, :]
        sums[span, :] = jnp.broadcast_to(jnp.sum(dn * gain * v, axis=-1, keepdims=True), r.shape)
        d_gain[0:1, :] += jnp.sum(dn * v * r[:, :1], axis=0, keepdims=True)

    swap = Swap(sums, other, mini, (s_send, s_recv), m)
    swap.start()
    swap.wait()

    @row_loop(rows)
    def _(span):
        r = stat[span, :]
        factor = (r * r * r * ((sums[span, :] + other[span, 0:1]) / wide))[:, :1]
        d = cot[span, :].astype(F32) + r[:, :1] * (d_middle[span, :] * gain) - middle[span, :] * factor
        d_middle[span, :] = d
        piece[span, :] = d.astype(BF)

    fold.wait_sends()
    for line in lines:
        line.wait_sends()
    ahead.wait_early()
    ahead.wait_firsts((0,))
    for red in reds:
        red.wait_firsts()
    reds[1].wait_relays()
    reds[1].closed()


def shape(dims, dtype):
    return jax.ShapeDtypeStruct(dims, dtype)


def comm_call(kernel, ins, outs, scratch, number):
    return pl.pallas_call(
        kernel,
        out_shape=[s for s, _ in outs],
        in_specs=ins,
        out_specs=[b for _, b in outs],
        scratch_shapes=scratch,
        compiler_params=pltpu.CompilerParams(
            collective_id=number, has_side_effects=True, vmem_limit_bytes=LIMIT
        ),
    )


def allow(cut, q0, qn, kn):
    q = q0 + lax.broadcasted_iota(jnp.int32, (qn, kn), 0)
    k = lax.broadcasted_iota(jnp.int32, (qn, kn), 1)
    doc_q = (q >= cut[0]).astype(jnp.int32) + (q >= cut[1]).astype(jnp.int32)
    doc_k = (k >= cut[0]).astype(jnp.int32) + (k >= cut[1]).astype(jnp.int32)
    return (doc_q == doc_k) & (k <= q)


def turn(v):
    half = v.shape[1] // 2
    return jnp.concatenate([-v[:, half:], v[:, :half]], axis=1)


def turn_back(v):
    half = v.shape[1] // 2
    return jnp.concatenate([v[:, half:], -v[:, :half]], axis=1)


def fore_kernel(groups, heads, hd, cuts, w_query, w_key, w_value, w_out, gain_a, gain_b, gate, up, w_down, hidden,
                cot, gain_q, gain_k, table, attn, first_w, other_w, near_w, normed_out, pre, qkv, stats, mixed, middle, stat, two_full, grad_full,
                gain_rows,
                *scratch):
    fold_scratch, (full, weights, pack, down, marks, piece, other, mini, load, c_send, c_recv, w_send, w_recv, w_local, z_send, z_recv,
                   g_send, g_recv, g_local, s_send, s_recv) = scratch[:6], scratch[6:]
    x = full
    t, i, m = lax.axis_index("t"), lax.axis_index("i"), lax.axis_index("m")
    rows, wide = hidden.shape[0], x.shape[1]
    nq, kv = heads * hd, (heads + 2) * hd
    shard = pack.shape[1]
    unit = first_w.shape[2] // 3
    others = [{"i": flip(i, j)} for j in (1, 2, 3)]
    away = [(a, b) for a in range(4) for b in range(4) if a + b > 0]
    places = {(a, b): {"t": flip(t, a) if a else t, "i": flip(i, b) if b else i} for a, b in away}
    meet([{"m": 1 - m}] + [places[ab] for ab in away])
    for p in range(4):
        pack[p, :, 0:nq] = w_query[:, p * nq:(p + 1) * nq]
        pack[p, :, nq:nq + hd] = w_key[:, p * hd:(p + 1) * hd]
        pack[p, :, nq + hd:kv] = w_value[:, p * hd:(p + 1) * hd]
        pack[p, :, kv:kv + nq] = w_out[p * nq:(p + 1) * nq, :].T
    mine = attn.at[at((t * 4 + i) * shard, shard), :]
    spread = [remote(pack.at[flip(i, j)], mine, (w_send, w_recv), j - 1, others[j - 1]) for j in (2, 3, 1)]
    own = pltpu.make_async_copy(pack.at[i], mine, w_local.at[0])
    for copy in spread:
        copy.start()
    own.start()
    gather_h = TpGather(hidden, full, (g_send, g_recv, g_local), 0, i, m, True)
    gather_g = TpGather(cot, grad_full, (g_send, g_recv, g_local), 8, i, m, True)
    gather_h.start()
    here = t * 4 + i
    marks[here] = jnp.concatenate([gain_a[...], gain_b[...], jnp.zeros((14, shard), BF)], axis=0)
    mark = [remote(marks.at[here], marks.at[here], (c_send, c_recv), 4 * a + b, places[(a, b)]) for a, b in away]
    for copy in mark:
        copy.start()
    for r in range(0, w_down.shape[0], 512):
        down[:, r:r + 512] = w_down[r:r + 512, :].T
    gq, gk = gain_q[...].astype(F32), gain_k[...].astype(F32)

    def chunk(c):
        if c < 2:
            place = first_w.at[c, at((t * 4 + i) * shard, shard), :]
        else:
            place = other_w.at[c - 2, at(i * shard, shard), :]
        found, kept = [], []
        for n, src in enumerate((gate, up, down)):
            dst = place.at[:, pl.ds(n * unit, unit)]

            def view(p):
                return src.at[:, at(p * 4 * unit + c * unit, unit)]

            for j in (2, 3, 1):
                found.append(remote(view(flip(i, j)), dst, (w_send, w_recv), 3 + 9 * c + 3 * n + j - 1, others[j - 1]))
            kept.append(pltpu.make_async_copy(view(i), dst, w_local.at[1 + 3 * c + n]))
        return found, kept

    chunks = [chunk(c) for c in range(4)]

    def begin(c):
        for copy in chunks[c][0] + chunks[c][1]:
            copy.start()

    def landed(c):
        for copy in chunks[c][0]:
            copy.wait_recv()
        for copy in chunks[c][1]:
            copy.wait()

    sems = (z_send, z_recv)
    block = 4 * shard
    line = LineGather(attn.at[at(t * block, block), :], attn, sems, 0, groups, t)
    lines = [
        LineGather(first_w.at[c, at(t * block, block), :], first_w.at[c], sems, 6 * c + 6, groups, t) for c in range(2)
    ]
    above = remote(other_w.at[0], near_w.at[0], sems, 18, {"t": t + 1})
    below = remote(other_w.at[0], near_w.at[1], sems, 19, {"t": t - 1})

    def near_start():
        @pl.when(t < groups - 1)
        def _():
            above.start()

        @pl.when(t > 0)
        def _():
            below.start()

    own.wait()
    for copy in spread:
        copy.wait_recv()
    line.send(0)
    begin(0)
    lane = lax.rem(lax.broadcasted_iota(jnp.int32, (1, hd), 1), hd // 2).astype(F32)
    freqs = jnp.exp(lane * (-math.log(1000000.0) * 2.0 / hd))

    @pl.loop(0, 4)
    def _(s):
        c1, c2 = cuts[t * 4 + s, 0], cuts[t * 4 + s, 1]
        position = lax.broadcasted_iota(jnp.int32, (rows, hd), 0)
        start = jnp.where(position >= c2, c2, jnp.where(position >= c1, c1, 0))
        angle = (position - start).astype(F32) * freqs
        table[at(s * rows, rows), 0:hd] = jnp.cos(angle)
        table[at(s * rows, rows), hd:2 * hd] = jnp.sin(angle)

    line.pass_on(1)
    gather_h.relay()
    begin(1)
    line.pass_on(2)
    gather_h.relay_far()
    gather_g.start()
    begin(2)
    begin(3)
    landed(0)
    lines[0].send(0)
    line.pass_on(3)
    landed(1)
    lines[1].send(0)
    fill = pltpu.make_async_copy(attn, weights, load.at[0])
    fill.start()
    gather_h.finish()
    fill.wait()
    for copy in mark:
        copy.wait()
    for n in range(4 * groups):
        gain_rows[:, n * shard:(n + 1) * shard] = marks[n].astype(F32)[0:8, :]
    gain_two = gain_rows[1:2, at(m * (wide // 2), wide // 2)]
    parts = full
    fold = TpFold(parts, middle, fold_scratch, i, m)

    @pl.loop(0, 4)
    def _(step):
        s = pick(step, i)
        start = s * rows
        def sub(r, size):
            return pl.ds(pl.multiple_of(start + r, size), size)

        cut = (cuts[t * 4 + s, 0], cuts[t * 4 + s, 1])

        @pl.loop(0, rows, step=64)
        def _(r):
            span = sub(r, 64)
            v = x[span, :].astype(F32)
            scale = lax.rsqrt(jnp.mean(v * v, axis=-1, keepdims=True) + EPS)
            stats[span, :] = jnp.broadcast_to(scale, (64, stats.shape[1]))
            x[span, :] = (v * scale * gain_rows[0:1, :]).astype(BF)

        everything = sub(0, rows)
        keep = pltpu.make_async_copy(x.at[everything, :], normed_out.at[everything, :], load.at[1])
        keep.start()
        heads_pre = nn(x[everything, :], weights[:, :kv])
        pre[everything, :] = heads_pre
        c, sn = table[everything, 0:hd], table[everything, hd:2 * hd]
        for h in range(heads + 1):
            lanes = slice(h * hd, (h + 1) * hd)
            n = rms_rows(heads_pre[:, lanes], gq if h < heads else gk)
            qkv[everything, lanes] = (n * c + turn(n) * sn).astype(BF)
        qkv[everything, nq + hd:kv] = heads_pre[:, nq + hd:kv].astype(BF)
        half = rows // 2
        for b in range(2):
            kn = (b + 1) * half
            span = sub(b * half, half)
            mask = allow(cut, b * half, half, kn)
            keys, values = qkv[pl.ds(start, kn), nq:nq + hd], qkv[pl.ds(start, kn), nq + hd:kv]
            for h in range(heads):
                q = qkv[span, h * hd:(h + 1) * hd]
                scores = jnp.where(mask, nt(q, keys) * (hd ** -0.5), -1e30)
                top = jnp.max(scores, axis=-1, keepdims=True)
                e = jnp.exp(scores - top)
                total = jnp.sum(e, axis=-1, keepdims=True)
                probs = (e * (1.0 / total)).astype(BF)
                stats[span, h:h + 1] = top + jnp.log(total)
                mixed[span, h * hd:(h + 1) * hd] = nn(probs, values).astype(BF)

        keep.wait()

        @pl.loop(0, wide, step=512)
        def _(col):
            cols = pl.ds(pl.multiple_of(col, 512), 512)
            parts[everything, cols] = nt(mixed[everything, :], weights[cols, kv:kv + nq]).astype(BF)

        @pl.when(step == 0)
        def _():
            fold.send(0)

        @pl.when(step == 1)
        def _():
            fold.side(1)
            lines[0].pass_on(1)

        @pl.when(step == 2)
        def _():
            fold.send(1)
            lines[1].pass_on(1)
            gather_g.relay()

    fold.side(0)
    lines[0].pass_on(2)
    gather_g.relay_far()
    fold.finish(lambda: (lines[1].pass_on(2), landed(2), near_start()))

    @row_loop(rows)
    def _(span):
        v = middle[span, :] + hidden[span, :].astype(F32)
        middle[span, :] = v
        stat[span, :] = jnp.broadcast_to(jnp.sum(v * v, axis=-1, keepdims=True), stat[span, :].shape)

    swap = Swap(stat, other, mini, (s_send, s_recv), m)
    swap.start()
    swap.wait()

    @row_loop(rows)
    def _(span):
        r = lax.rsqrt((stat[span, :] + other[span, 0:1]) / wide + EPS)
        stat[span, :] = r
        piece[span, :] = (middle[span, :] * r[:, :1] * gain_two).astype(BF)

    gather = TpGather(piece, two_full, (g_send, g_recv, g_local), 16, i, m)
    gather.start()
    gather_g.finish()
    fold.wait_sends()
    lines[0].pass_on(3)
    landed(3)
    for c in range(4):
        for copy in chunks[c][0]:
            copy.wait_send()
    for copy in spread:
        copy.wait_send()
    gather.relay()
    lines[1].pass_on(3)
    gather.relay_far()
    for one in [line] + lines:
        one.wait_sends()

    @pl.when(t > 0)
    def _():
        above.wait_recv()
        below.wait_send()

    @pl.when(t < groups - 1)
    def _():
        below.wait_recv()
        above.wait_send()

    gather.finish()


def aft_kernel(groups, heads, hd, cuts, piece, normed, out_parts, attn, pre_in, middle, d_middle, qkv_in, stats_in,
               mixed_in, table_in, mlp_grads, early_up, early_down, gain_q, gain_k, hidden, gain_rows, d_gain_two,
               d_input, block_out, back, gains, ups, downs, mlp_back, *scratch):
    fold_scratch, out_scratch = scratch[:6], scratch[6:14]
    (dm, nrm, pre, qkv, stats, mixed, table, weights, res, acc, grads, up_in, down_in, total, d_mix, d_pre, d_kv, qk_sum, sums, other, mini,
     g_in, load, a_send, a_recv, a_local, send, recv, z_send, z_recv, g_send, g_recv, s_send, s_recv,
     local, stage, spare, line_load, r_send, r_recv, m_send, m_recv) = scratch[14:]
    t, i, m = lax.axis_index("t"), lax.axis_index("i"), lax.axis_index("m")
    others = [{"i": flip(i, j)} for j in (1, 2, 3)]
    meet(others + [{"m": 1 - m}] + [{"t": flip(t, j)} for j in (1, 2, 3)])
    rows, wide = hidden.shape[0], dm.shape[1]
    nq, kv = heads * hd, (heads + 2) * hd
    scale = hd ** -0.5
    gain = gain_rows[0:1, at(m * (wide // 2), wide // 2)]
    qk_gain = (gain_q[...].astype(F32), gain_k[...].astype(F32))
    gather = TpGather(piece, dm, (a_send, a_recv, a_local), 0, i, m)
    gather.start()
    reds = []
    for c in range(2):
        reds.append(LineReduce(
            mlp_grads.at[2 + c], ups.at[c], downs.at[c], mlp_back.at[c], stage, spare, line_load, (r_send, r_recv),
            6 * c, (m_send, m_recv), t, i, reds[-1] if reds else None, (early_up, early_down) if c == 0 else None))
    for b in (2, 1):
        reds[0].first(b)
    for b in (3, 0, 2, 1):
        reds[1].first(b)
    reds[0].hop((0,))
    fill = pltpu.make_async_copy(attn, weights, load.at[2])
    fill.start()

    def fetch(step):
        span = at(pick(step, i) * rows, rows)
        return (pltpu.make_async_copy(normed.at[span, :], nrm, load.at[0]),
                *[pltpu.make_async_copy(src.at[span, :], dst, load.at[n]) for n, src, dst in (
                    (1, pre_in, pre), (4, qkv_in, qkv), (5, stats_in, stats),
                    (7, table_in, table))])

    two = TpReduce(out_parts, res, out_scratch, i, m)
    acc[...] = jnp.zeros_like(acc)
    qk_sum[...] = jnp.zeros_like(qk_sum)
    fold = TpFold(dm, d_input, fold_scratch, i, m)
    gather.relay()
    reds[0].hop((1, 2))
    gather.relay_far()
    two.start()
    reds[0].close()
    fill.wait()
    for copy in fetch(0)[1:]:
        copy.start()
    gather.finish()

    block = wide // groups
    spans = (slice(0, kv), slice(kv, kv + nq))

    def settle(which):
        for b in range(groups):
            grads[b, spans[which], :] = acc[spans[which], b * block:(b + 1) * block].astype(BF)

    def up(k, src, which):
        dst = up_in.at[k, spans[which], :]
        return remote(src, dst, (z_send, z_recv), 8 * which + k, {"t": t + 1})

    def down(k, src, which):
        dst = down_in.at[k, spans[which], :]
        return remote(src, dst, (z_send, z_recv), 8 * which + 4 + k, {"t": t - 1})

    def own_grads(b, which):
        return grads.at[b, spans[which], :]

    def begin(which):
        @pl.when(t == 0)
        def _():
            for k in range(groups - 1):
                up(k, own_grads(groups - 1 - k, which), which).start()

        @pl.when(t == groups - 1)
        def _():
            for k in range(groups - 1):
                down(k, own_grads(k, which), which).start()

    @pl.loop(0, 4)
    def _(s):
        span = at(s * rows, rows)
        take = pltpu.make_async_copy(mixed_in.at[span, :], mixed, load.at[6])
        take.start()
        take.wait()

        @pl.loop(0, wide, step=512)
        def _(col):
            cols = pl.ds(pl.multiple_of(col, 512), 512)
            acc[kv:kv + nq, cols] += tn(mixed[...], dm[span, cols])

    settle(1)
    begin(1)

    @pl.loop(0, 4)
    def _(step):
        s = pick(step, i)
        start = s * rows
        fetch(step)[0].start()

        def sub(r, size):
            return pl.ds(pl.multiple_of(start + r, size), size)

        cut = (cuts[t * 4 + s, 0], cuts[t * 4 + s, 1])
        everything = sub(0, rows)
        d_mix[...] = nn(dm[everything, :], weights[:, kv:kv + nq]).astype(BF)
        d_kv[...] = jnp.zeros_like(d_kv)
        half = rows // 2

        def undo(h, grad):
            lanes = slice(h * hd, (h + 1) * hd)
            row = 0 if h < heads else 1
            c, sn = table[:, 0:hd], table[:, hd:2 * hd]
            u = c * grad + turn_back(sn * grad)
            v = pre[:, lanes]
            r = lax.rsqrt(jnp.mean(v * v, axis=-1, keepdims=True) + EPS)
            qk_sum[0:1, row * hd:(row + 1) * hd] += jnp.sum(u * v * r, axis=0, keepdims=True)
            scaled = u * qk_gain[row]
            undone = r * scaled - v * (r * r * r) * jnp.mean(scaled * v, axis=-1, keepdims=True)
            d_pre[:, lanes] = undone.astype(BF)

        for copy in fetch(step)[1:]:
            copy.wait()
        for h in range(heads):
            lanes = slice(h * hd, (h + 1) * hd)
            found = []
            for b in range(2):
                kn = (b + 1) * half
                span = slice(b * half, kn)
                mask = allow(cut, b * half, half, kn)
                keys, values = qkv[0:kn, nq:nq + hd], qkv[0:kn, nq + hd:kv]
                q, go = qkv[span, lanes], d_mix[span, lanes]
                scores = jnp.where(mask, nt(q, keys) * scale, -1e30)
                probs = jnp.exp(scores - stats[span, h:h + 1])
                d_probs = nt(go, values)
                inner = jnp.sum(probs * d_probs, axis=-1, keepdims=True)
                d_scores = (probs * (d_probs - inner)).astype(BF)
                found.append(nn(d_scores, keys) * scale)
                d_kv[0:kn, 0:hd] += tn(d_scores, q) * scale
                d_kv[0:kn, hd:2 * hd] += tn(probs.astype(BF), go)
            undo(h, jnp.concatenate(found, axis=0))
        undo(heads, d_kv[:, 0:hd])
        d_pre[:, nq + hd:kv] = d_kv[:, hd:2 * hd].astype(BF)

        @pl.when(step < 3)
        def _():
            for copy in fetch(step + 1)[1:]:
                copy.start()

        fetch(step)[0].wait()

        @pl.loop(0, wide, step=512)
        def _(col):
            cols = pl.ds(pl.multiple_of(col, 512), 512)
            acc[0:kv, cols] += tn(d_pre[...], nrm[:, cols])
            dm[everything, cols] = nt(d_pre[...], weights[cols, 0:kv]).astype(BF)

        @pl.when(step == 0)
        def _():
            fold.send(0)
            two.fold_pair()
            reds[1].hop((0,))

        @pl.when(step == 1)
        def _():
            fold.side(1)
            reds[1].hop((1, 2))

        @pl.when(step == 2)
        def _():
            fold.send(1)

        @pl.when(step == 3)
        def _():
            fold.side(0)

    settle(0)
    begin(0)
    part = hidden.shape[1]
    kept = [acc.at[pl.ds(0, rows), pl.ds(n * part, part)] for n in range(2)]
    takes = [pltpu.make_async_copy(src, kept[n], load.at[2 + n]) for n, src in enumerate((middle, d_middle))]
    for take in takes:
        take.start()

    def hop(places, which):
        for at_t, plan in LineReduce.PLAN.items():
            @pl.when(t == at_t)
            def _():
                for place, way, n in plan:
                    if place in places:
                        make, slots = (up, up_in) if way == "up" else (down, down_in)
                        slot = slots.at[n, spans[which], :]
                        make(n, slot, which).wait_recv()
                        add_rows(slot, slot, own_grads(groups - 1 - n if way == "up" else n, which))
                        make(n, slot, which).start()

    hop((0,), 1)
    reds[1].close()
    for take in takes:
        take.wait()
    hop((1, 2), 1)
    fold.finish(lambda: hop((0,), 0))
    gains[...] = jnp.zeros_like(gains)
    own_half = at(m * (wide // 2), wide // 2)
    gains[1:2, own_half] = d_gain_two[0:1, :]
    gains[2:3, :] = jnp.concatenate([qk_sum[0:1, :]] * (wide // (2 * hd)), axis=1)

    @row_loop(rows)
    def _(span):
        dn, v = d_input[span, :], hidden[span, :].astype(F32)
        r = stats[span, heads:heads + 1]
        sums[span, :] = jnp.broadcast_to(jnp.sum(dn * gain * v, axis=-1, keepdims=True), sums[span, :].shape)
        gains[0:1, own_half] += jnp.sum(dn * v * r, axis=0, keepdims=True)

    swap = Swap(sums, other, mini, (s_send, s_recv), m)
    swap.start()
    ways = [{"i": flip(i, 1)}, {"m": 1 - m}, {"i": flip(i, 2)}, {"t": flip(t, 1)}, {"t": flip(t, 2)}]

    def trade(k):
        return remote(gains, g_in.at[k], (g_send, g_recv), k, ways[k])

    def give(n):
        trade(n).start()
        trade(n).wait()
        gains[...] += g_in[n]

    give(0)
    swap.wait()

    @row_loop(rows)
    def _(span):
        r = stats[span, heads:heads + 1]
        factor = r * r * r * ((sums[span, :] + other[span, 0:1]) / wide)[:, :1]
        d = kept[1][span, :] + r * (d_input[span, :] * gain)
        d_input[span, :] = d - hidden[span, :].astype(F32) * factor

    give(1)
    hop((1, 2), 0)
    give(2)
    give(3)
    give(4)
    two.fold_links()

    @row_loop(rows)
    def _(span):
        block_out[span, :] = (kept[0][span, :] + res[span, :]).astype(BF)

    for b in range(groups):
        @pl.when(t == b)
        def _():
            for which in (1, 0):
                final = total.at[spans[which], :]
                own = own_grads(b, which)
                if b > 0:
                    slot = up_in.at[groups - 1 - b, spans[which], :]
                    up(groups - 1 - b, slot, which).wait_recv()
                    add_rows(final, own, slot)
                    own = final
                if b < groups - 1:
                    slot = down_in.at[b, spans[which], :]
                    down(b, slot, which).wait_recv()
                    add_rows(final, own, slot)

    sub_cols = block // 4
    moves = []
    for j in (2, 3, 1):
        view = total.at[:, at(flip(i, j) * sub_cols, sub_cols)]
        moves.append(remote(view, back.at[i], (send, recv), j, others[j - 1]))
    keep = pltpu.make_async_copy(total.at[:, at(i * sub_cols, sub_cols)], back.at[i], local.at[0])
    for move in moves:
        move.start()
    keep.start()
    for which in range(2):
        for k in range(groups - 1):
            @pl.when(t < groups - 1 - k)
            def _():
                up(k, up_in.at[k, spans[which], :], which).wait_send()

            @pl.when(t > k)
            def _():
                down(k, down_in.at[k, spans[which], :], which).wait_send()

    fold.wait_sends()
    reds[0].wait_firsts((1, 2))
    reds[1].wait_firsts()
    reds[1].wait_relays()
    reds[1].closed()
    keep.wait()
    for move in moves:
        move.wait()


class Dims:
    def __init__(self, length, part, halves, inner, groups, hd, nq, shard, hidden_units):
        self.length, self.part, self.halves, self.inner, self.groups, self.hd = length, part, halves, inner, groups, hd
        self.nq, self.shard, self.heads, self.kv = nq, shard, nq // hd, nq + 2 * hd
        self.width, self.tokens = part * halves, length * inner
        self.unit, self.block, self.cols = hidden_units // 4, part * halves // groups, nq + 2 * hd + nq

    def values(self):
        return (self.length, self.part, self.halves, self.inner, self.groups, self.hd, self.nq, self.shard,
                self.heads, self.kv, self.width, self.tokens, self.unit, self.block, self.cols)


def call_fore(dims, *args):
    (length, part, halves, inner, groups, hd, nq, shard, heads, kv, width, tokens, unit, block, cols) = dims.values()
    fold_scratch = tp_fold_scratch(length, part, halves)
    return comm_call(
        partial(fore_kernel, groups, heads, hd), [SMEM] + [VMEM] * 13,
        [(shape((tokens, 2 * hd), F32), VMEM), (shape((width, cols), BF), ANY), (shape((2, width, 3 * unit), BF), ANY), (shape((2, block, 3 * unit), BF), ANY),
         (shape((2, block, 3 * unit), BF), ANY),
         (shape((tokens, width), BF), ANY), (shape((tokens, kv), F32), VMEM), (shape((tokens, kv), BF), VMEM),
         (shape((tokens, 128), F32), VMEM), (shape((tokens, nq), BF), VMEM), (shape((length, part), F32), VMEM),
         (shape((length, 128), F32), VMEM), (shape((tokens, width), BF), ANY), (shape((tokens, width), BF), ANY),
         (shape((8, width), F32), VMEM)],
        fold_scratch + [
            pltpu.VMEM((tokens, width), BF), pltpu.VMEM((width, cols), BF), pltpu.VMEM((inner, shard, cols), BF),
            pltpu.VMEM((shard, 4 * inner * unit), BF), pltpu.VMEM((inner * groups, 16, shard), BF),
            pltpu.VMEM((length, part), BF),
            pltpu.VMEM((length, 128), F32), pltpu.VMEM((2, 8, length), F32), DMA((2,)), DMA((16,)), DMA((16,)),
            DMA((39,)), DMA((39,)), DMA((13,)), DMA((20,)), DMA((20,)),
            DMA((24,)), DMA((24,)), DMA((3,)), DMA((1,)), DMA((1,))], 0,
    )(*args)


def call_mlp(dims, *args):
    (length, part, halves, inner, groups, hd, nq, shard, heads, kv, width, tokens, unit, block, cols) = dims.values()
    return comm_call(
        partial(mlp_kernel, groups), [ANY] * 5 + [VMEM] * 4,
        [(shape((2, width, 3 * unit), BF), ANY), (shape((4, groups, 3 * unit, block), BF), ANY),
         (shape((2, 3, 3 * unit, block), BF), ANY), (shape((2, 3, 3 * unit, block), BF), ANY),
         (shape((1, 3 * unit, block), BF), ANY), (shape((1, 3 * unit, block), BF), ANY),
         (shape((2, inner, 3 * unit, shard), BF), ANY), (shape((tokens, width), BF), ANY),
         (shape((length, part), F32), VMEM), (shape((8, part), F32), VMEM), (shape((length, part), BF), VMEM)],
        [pltpu.VMEM((tokens, width), BF), pltpu.VMEM((tokens, width), BF), pltpu.VMEM((4, width, 3 * unit), BF),
         pltpu.VMEM((4, tokens, 3 * unit), BF), pltpu.VMEM((3 * unit, tokens), BF),
         pltpu.VMEM((2, 3 * unit, block), BF), pltpu.VMEM((4, 3 * unit, block), BF), pltpu.VMEM((3 * unit, block), BF),
         pltpu.VMEM((length, 128), F32), pltpu.VMEM((length, 128), F32), pltpu.VMEM((2, 8, length), F32), DMA((17,)),
         DMA((12,)), DMA((12,)), DMA((18,)), DMA((18,)), DMA((8,)), DMA((8,)),
         DMA((7,)), DMA((7,)), DMA((1,)), DMA((1,)), pltpu.SemaphoreType.REGULAR], 1,
    )(*args)


def call_aft(dims, *args):
    (length, part, halves, inner, groups, hd, nq, shard, heads, kv, width, tokens, unit, block, cols) = dims.values()
    fold_scratch = tp_fold_scratch(length, part, halves)
    return comm_call(
        partial(aft_kernel, groups, heads, hd), [SMEM] + [ANY] * 14 + [VMEM] * 5,
        [(shape((length, part), F32), VMEM), (shape((length, part), BF), VMEM),
         (shape((inner, nq + kv, block // inner), BF), ANY), (shape((8, width), F32), VMEM),
         (shape((2, 3, 3 * unit, block), BF), ANY), (shape((2, 3, 3 * unit, block), BF), ANY),
         (shape((2, inner, 3 * unit, shard), BF), ANY)],
        fold_scratch + tp_reduce_scratch(length, part, halves) + [
            pltpu.VMEM((tokens, width), BF), pltpu.VMEM((length, width), BF), pltpu.VMEM((length, kv), F32),
            pltpu.VMEM((length, kv), BF), pltpu.VMEM((length, 128), F32), pltpu.VMEM((length, nq), BF),
            pltpu.VMEM((length, 128), F32),
            pltpu.VMEM((width, nq + kv), BF), pltpu.VMEM((length, part), F32), pltpu.VMEM((nq + kv, width), F32),
            pltpu.VMEM((groups, nq + kv, block), BF),
            pltpu.VMEM((groups - 1, nq + kv, block), BF), pltpu.VMEM((groups - 1, nq + kv, block), BF),
            pltpu.VMEM((nq + kv, block), BF), pltpu.VMEM((length, nq), BF), pltpu.VMEM((length, kv), BF),
            pltpu.VMEM((length, 2 * hd), F32), pltpu.VMEM((8, 2 * hd), F32),
            pltpu.VMEM((length, 128), F32), pltpu.VMEM((length, 128), F32), pltpu.VMEM((2, 8, length), F32), pltpu.VMEM((5, 8, width), F32),
            DMA((8,)), DMA((8,)), DMA((8,)), DMA((1,)),
            DMA((4,)), DMA((4,)), DMA((16,)), DMA((16,)), DMA((5,)), DMA((5,)),
            DMA((1,)), DMA((1,)), DMA((1,)),
            pltpu.VMEM((4, 3 * unit, block), BF), pltpu.VMEM((3 * unit, block), BF), DMA((3,)),
            DMA((12,)), DMA((12,)), DMA((8,)), DMA((8,))], 2,
    )(*args)


def fast_body(
    hidden_in, doc_starts, attn_gain, w_query, w_key, w_value, query_gain, key_gain,
    w_out, mlp_gain, w_gate, w_up, w_down, cotangent, *, groups, inner, halves,
):
    length, part = hidden_in.shape
    shard = w_query.shape[0]
    width, tokens = part * halves, length * inner
    hd = query_gain.shape[0]
    heads = w_query.shape[1] // inner // hd
    nq, kv = heads * hd, (heads + 2) * hd
    hidden_units = w_gate.shape[1] // inner
    t_index, i_index = lax.axis_index("t"), lax.axis_index("i")
    gain_q, gain_k = query_gain[None], key_gain[None]
    dims = Dims(length, part, halves, inner, groups, hd, nq, shard, hidden_units)
    unit = dims.unit
    (table, attn_w, first_w, other_w, near_w, normed_one, pre, qkv, stats, mixed, middle, r_two, two_full, grad_full,
     gain_rows) = call_fore(
        dims, doc_starts, w_query, w_key, w_value, w_out, attn_gain[None], mlp_gain[None], w_gate, w_up, w_down,
        hidden_in, cotangent, gain_q, gain_k)

    (_, mlp_grads, _, _, next_up, next_down, mlp_back, out_parts, d_middle, d_gain_two, d_low) = call_mlp(
        dims, two_full, grad_full, first_w, other_w, near_w, middle, r_two, cotangent, gain_rows)

    d_input, block_out, attn_back, gains_out, _, _, last_back = call_aft(
        dims, doc_starts, d_low, normed_one, out_parts, attn_w, pre, middle, d_middle, qkv, stats, mixed, table, mlp_grads, next_up, next_down, gain_q, gain_k,
        hidden_in, gain_rows, d_gain_two)

    all_back = jnp.concatenate([mlp_back, last_back], axis=0)

    def mlp_columns(first):
        part_of = all_back[:, :, first:first + unit, :]
        return jnp.transpose(part_of, (3, 1, 0, 2)).reshape(shard, inner * hidden_units).astype(F32)

    d_down = jnp.transpose(all_back[:, :, 2 * unit:, :], (1, 0, 2, 3)).reshape(inner * hidden_units, shard).astype(F32)
    own = lax.dynamic_slice(gains_out, (0, (t_index * inner + i_index) * shard), (2, shard))

    def columns(first, last):
        return jnp.moveaxis(attn_back[:, first:last, :], 2, 0).reshape(shard, -1).astype(F32)

    return (
        block_out, d_input, own[0], columns(0, nq), columns(nq, nq + hd), columns(nq + hd, kv),
        gains_out[2, :hd], gains_out[2, hd:2 * hd],
        attn_back[:, kv:kv + nq, :].reshape(inner * nq, shard).astype(F32), own[1],
        mlp_columns(0), mlp_columns(unit), d_down,
    )


def solution(mesh):
    dp, halves = mesh.shape["dp"], mesh.shape["mp"]
    inner = 4
    groups = dp // inner
    fine = Mesh(mesh.devices.reshape(groups, inner, halves), ("t", "i", "m"))
    rows = P(("t", "i"))
    block = P(("t", "i"), "m")
    turned = P("m", ("t", "i"))
    body = fast_body if groups == 4 and halves == 2 else plain_body
    return jax.shard_map(
        partial(body, groups=groups, inner=inner, halves=halves),
        mesh=fine,
        in_specs=(block, P(), rows, block, block, block, P(), P(), turned, rows, block, block, turned, block),
        out_specs=(block, block, rows, block, block, block, P(), P(), turned, rows, block, block, turned),
        check_vma=False,
    )
```
